128 devices in a mesh: ctx: 16 (over x, y), tp: 8 (over z, core).
Axes of the slice: x: 4, y: 4, z: 4, core: 2. Of those that a mesh axis runs over, the one named last changes fastest.
Arguments:
- queries: bfloat16 [8192, 8192], P('ctx', 'tp'), may hold values from -150 to 150
- keys: bfloat16 [8192, 512], P('ctx'), may hold values from -6 to 6
- values: bfloat16 [8192, 512], P('ctx'), may hold values from -6 to 6
- comp_keys: bfloat16 [512, 512], P('ctx'), may hold values from -6 to 6
- comp_values: bfloat16 [512, 512], P('ctx'), may hold values from -6 to 6
- gate_comp: float32 [8192, 64], P('ctx', 'tp'), may hold values from 0.1 to 1
- gate_sel: float32 [8192, 64], P('ctx', 'tp'), may hold values from 0.1 to 1
- grad_out: bfloat16 [8192, 8192], P('ctx', 'tp'), may hold values from -6 to 6
- selections: int32 [64, 4, 15], P('ctx'), may hold values from -1 to 63, as said below
Outputs:
- grad_queries: bfloat16 [8192, 8192], P('ctx', 'tp')
- grad_keys: bfloat16 [8192, 512], P('ctx', 'tp')
- grad_values: bfloat16 [8192, 512], P('ctx', 'tp')
- grad_comp_keys: bfloat16 [512, 512], P('ctx', 'tp')
- grad_comp_values: bfloat16 [512, 512], P('ctx', 'tp')
The draws below stay inside these ranges and needn't reach their ends.
Inputs may be any that keep to these rules, and one draw needn't show every extreme that they name: `selections`: entry -1 marks an unused slot. Every other entry of row b names a block that lies on a lower ctx index than block b, and the entries of a row differ. For each group, the rows of the 4 blocks of one ctx index name at most 2 distinct blocks of any one other ctx index, and this most is reached in every draw.
All inputs are finite; a program needn't handle non-finite values.
Results may differ from the reference program's by a relative error of at most 0.009.
Values may be sent and summed in bfloat16 or wider, within the bound.
A program may use at most 192 MiB of HBM per device.

```python
import math
import jax
import jax.numpy as jnp
from jax import lax

HD = 128
BLK = 128
STRIDE = 16
TOPK = 16
HEADS = 64
GROUPS = 4
SEL = 15
QB_DEV = 4
CAP = 2
TOKENS = 8192
NQB = 64
CTOK = 512
N_CTX = 16


def drawn_normal(key, salt_id, shape):
    return jnp.clip(jax.random.normal(jax.random.fold_in(key, salt_id), shape, jnp.float32), -6.0, 6.0)


def draw_key_base(key):
    base_rows = drawn_normal(key, 101, (TOKENS, GROUPS * HD))
    return base_rows


def draw_keys(key, part):
    return draw_key_base(key).astype(jnp.bfloat16)


def draw_queries(key, part):
    base_rows = drawn_normal(key, 202, (TOKENS, HEADS * HD))
    return base_rows.astype(jnp.bfloat16)


def draw_comp_keys(key, part):
    base_rows = drawn_normal(key, 303, (CTOK, GROUPS * HD))
    return base_rows.astype(jnp.bfloat16)


def draw_selections(key, part):

    def pick_group(group_key):

        def per_device(device):
            dev_key = jax.random.fold_in(group_key, device)
            owners = jnp.arange(N_CTX)

            def owner_pool(owner):
                return jax.random.permutation(jax.random.fold_in(dev_key, owner + 1), QB_DEV)[:CAP]
            local_ids = jax.vmap(owner_pool)(owners)
            pool_blocks = (owners[:, None] * QB_DEV + local_ids).reshape(-1)
            usable = jnp.repeat(owners, CAP) < device
            pool_total = N_CTX * CAP
            rank_keys = jax.random.permutation(jax.random.fold_in(dev_key, 0), pool_total)
            sort_score = rank_keys + jnp.where(usable, 0, pool_total)
            pool_order = jnp.argsort(sort_score)
            ordered = pool_blocks[pool_order]
            pool_size = device * CAP
            row_ids = jnp.arange(QB_DEV)[:, None]
            col_ids = jnp.arange(SEL)[None, :]
            rotated = (row_ids * SEL + col_ids) % jnp.maximum(pool_size, 1)
            pick_at = jnp.where(pool_size > SEL, rotated, col_ids + 0 * row_ids)
            return jnp.where(pick_at < pool_size, ordered[pick_at], -1).astype(jnp.int32)
        return jax.vmap(per_device)(jnp.arange(N_CTX)).reshape(NQB, SEL)
    picked = jax.vmap(lambda group_id: pick_group(jax.random.fold_in(key, group_id)))(jnp.arange(GROUPS))
    return jnp.transpose(picked, (1, 0, 2)).astype(jnp.int32)


def shard_levels(own_key, dims, shards, least, high):
    loudness = 1.0
    for position, blocks in shards:
        draws = jax.random.uniform(jax.random.fold_in(jax.random.fold_in(own_key, 6), position), (blocks,), jnp.float32, least / len(shards), high / len(shards))
        loudness = loudness * jnp.repeat(jnp.exp(draws), dims[position] // blocks).reshape((-1,) + (1,) * (len(dims) - 1 - position))
    return loudness


def gaussian(rng, shape, spread, limit, cuts=(), kind=jnp.bfloat16):
    level = shard_levels(rng, shape, cuts, -0.22, 0.18) if cuts else 1.0
    array = jax.random.normal(rng, shape, jnp.float32) * spread * level
    return jnp.minimum(jnp.maximum(array, -limit), limit).astype(kind)


def setup_inputs(seed: int = 0) -> dict:
    key_list = jax.random.split(jax.random.key(seed), 10)
    queries = draw_queries(jax.random.fold_in(key_list[9], 71), 0)
    keys = draw_keys(jax.random.fold_in(key_list[9], 71), 0)
    values = gaussian(key_list[2], (TOKENS, GROUPS * HD), 1.0, 6.0, ((0, 16),))
    comp_keys = draw_comp_keys(jax.random.fold_in(key_list[9], 71), 0)
    comp_values = gaussian(key_list[4], (CTOK, GROUPS * HD), 1.0, 6.0, ((0, 16),))
    gate_comp = jnp.clip(0.1 + 0.9 * jax.random.uniform(key_list[5], (TOKENS, HEADS), jnp.float32) ** shard_levels(key_list[5], (TOKENS, HEADS), ((0, 16), (1, 8)), -0.2, 0.2), 0.1, 1.0)
    gate_sel = jnp.clip(0.1 + 0.9 * jax.random.uniform(key_list[6], (TOKENS, HEADS), jnp.float32) ** shard_levels(key_list[6], (TOKENS, HEADS), ((0, 16), (1, 8)), -0.2, 0.2), 0.1, 1.0)
    grad_out = gaussian(key_list[7], (TOKENS, HEADS * HD), 1.0, 6.0, ((0, 16), (1, 8)))
    selections = draw_selections(jax.random.fold_in(key_list[9], 71), 0)
    return dict(queries=queries, keys=keys, values=values, comp_keys=comp_keys, comp_values=comp_values, gate_comp=gate_comp, gate_sel=gate_sel, grad_out=grad_out, selections=selections)


def rounded(values_in):
    return lax.optimization_barrier(values_in.astype(jnp.bfloat16)).astype(jnp.float32)

def attend_back(query_rows, grad_rows, key_tile, value_tile, allowed):
    scaling = 1.0 / math.sqrt(HD)
    scores = jnp.einsum('thd,kd->htk', query_rows, key_tile) * scaling
    scores = jnp.where(allowed[None], scores, -1e+30)
    row_max = lax.optimization_barrier(jnp.max(scores, axis=-1, keepdims=True))
    weights = jnp.exp(scores - row_max)
    probs_now = weights / lax.optimization_barrier(jnp.sum(weights, axis=-1, keepdims=True))
    dprobs = jnp.einsum('thd,kd->htk', grad_rows, value_tile)
    row_delta = lax.optimization_barrier(jnp.sum(probs_now * dprobs, axis=-1, keepdims=True))
    dscore = rounded(probs_now * (dprobs - row_delta))
    prob_b = rounded(probs_now)
    query_grad = scaling * jnp.einsum('htk,kd->thd', dscore, key_tile)
    key_grad = scaling * jnp.einsum('htk,thd->kd', dscore, query_rows)
    value_grad = jnp.einsum('htk,thd->kd', prob_b, grad_rows)
    return (query_grad, key_grad, value_grad)

def reference(queries, keys, values, comp_keys, comp_values, gate_comp, gate_sel, grad_out, selections):
    heads_group = HEADS // GROUPS
    comp_pos = jnp.arange(CTOK, dtype=jnp.int32) * STRIDE
    dq_cols, dk_cols, dv_cols, dkc_cols, dvc_cols = ([], [], [], [], [])
    for group_id in range(GROUPS):
        cols = slice(group_id * heads_group * HD, (group_id + 1) * heads_group * HD)
        kcols = slice(group_id * HD, (group_id + 1) * HD)
        query_all = queries[:, cols].astype(jnp.float32).reshape(TOKENS, heads_group, HD)
        grad_all = grad_out[:, cols].astype(jnp.float32).reshape(TOKENS, heads_group, HD)
        gate_c = gate_comp[:, group_id * heads_group:(group_id + 1) * heads_group]
        gate_s = gate_sel[:, group_id * heads_group:(group_id + 1) * heads_group]
        key_blocks = keys[:, kcols].astype(jnp.float32).reshape(NQB, BLK, HD)
        value_blocks = values[:, kcols].astype(jnp.float32).reshape(NQB, BLK, HD)
        ckeys = comp_keys[:, kcols].astype(jnp.float32)
        cvalues = comp_values[:, kcols].astype(jnp.float32)
        chosen_all = selections[:, group_id, :].astype(jnp.int32)

        def block_step(carried, block_id):
            dk_acc, dv_acc, dkc_acc, dvc_acc = carried
            row_start = block_id * BLK
            query_rows = lax.dynamic_slice_in_dim(query_all, row_start, BLK, 0)
            grad_rows = lax.dynamic_slice_in_dim(grad_all, row_start, BLK, 0)
            gate_crow = lax.dynamic_slice_in_dim(gate_c, row_start, BLK, 0)
            gate_srow = lax.dynamic_slice_in_dim(gate_s, row_start, BLK, 0)
            positions = row_start + jnp.arange(BLK, dtype=jnp.int32)
            go_cmp = rounded(gate_crow[:, :, None] * grad_rows)
            go_sel = rounded(gate_srow[:, :, None] * grad_rows)
            dq_comp, dkc_part, dvc_part = attend_back(query_rows, go_cmp, ckeys, cvalues, comp_pos[None, :] <= positions[:, None])
            chosen = lax.dynamic_index_in_dim(chosen_all, block_id, 0, keepdims=False)
            block_ids = jnp.concatenate([jnp.reshape(block_id, (1,)).astype(jnp.int32), chosen])
            live_ids = block_ids >= 0
            safe_ids = jnp.maximum(block_ids, 0)
            tile_keys = key_blocks[safe_ids].reshape(TOPK * BLK, HD)
            tile_values = value_blocks[safe_ids].reshape(TOPK * BLK, HD)
            key_pos = (safe_ids[:, None] * BLK + jnp.arange(BLK, dtype=jnp.int32)[None, :]).reshape(-1)
            key_live = jnp.repeat(live_ids, BLK)
            allowed = key_live[None, :] & (key_pos[None, :] <= positions[:, None])
            dq_sel, dk_part, dv_part = attend_back(query_rows, go_sel, tile_keys, tile_values, allowed)
            dk_acc = dk_acc.at[safe_ids].add(dk_part.reshape(TOPK, BLK, HD))
            dv_acc = dv_acc.at[safe_ids].add(dv_part.reshape(TOPK, BLK, HD))
            dq_block = (dq_comp + dq_sel).astype(jnp.bfloat16)
            return ((dk_acc, dv_acc, dkc_acc + dkc_part, dvc_acc + dvc_part), dq_block)
        start_state = (jnp.zeros((NQB, BLK, HD), jnp.float32), jnp.zeros((NQB, BLK, HD), jnp.float32), jnp.zeros((CTOK, HD), jnp.float32), jnp.zeros((CTOK, HD), jnp.float32))
        final_state, dq_blocks = lax.scan(block_step, start_state, jnp.arange(NQB, dtype=jnp.int32))
        dq_cols.append(dq_blocks.reshape(TOKENS, heads_group * HD))
        dk_cols.append(final_state[0].reshape(TOKENS, HD).astype(jnp.bfloat16))
        dv_cols.append(final_state[1].reshape(TOKENS, HD).astype(jnp.bfloat16))
        dkc_cols.append(final_state[2].astype(jnp.bfloat16))
        dvc_cols.append(final_state[3].astype(jnp.bfloat16))
    return (jnp.concatenate(dq_cols, axis=1), jnp.concatenate(dk_cols, axis=1), jnp.concatenate(dv_cols, axis=1), jnp.concatenate(dkc_cols, axis=1), jnp.concatenate(dvc_cols, axis=1))
```

```python
import functools
import math

import jax
import jax.numpy as jnp
from jax import lax
from jax.experimental import pallas as pl
from jax.experimental.pallas import tpu as pltpu
from jax.sharding import PartitionSpec as P

HD = 128
BLK = 128
STRIDE = 16
HEADS_DEV = 8
NEG = -1e30
SCALING = 1.0 / math.sqrt(HD)
LOG2E_SCALING = math.log2(math.e) / math.sqrt(HD)
NN = (((1,), (0,)), ((), ()))
NT = (((1,), (1,)), ((), ()))
TN = (((0,), (0,)), ((), ()))
f32 = jnp.float32
bf16 = jnp.bfloat16


def fold(x, op):
    return op(x.reshape(x.shape[0] // 8, 8, x.shape[1]), axis=0)


def branch(kref, vref, q, go, mask_first, live, s_ref, dp_ref, dq_ref, dk_ref, dv_ref, ck):
    nkeys, width = kref.shape[0], q.shape[0]
    chunks = nkeys // ck
    per = ck // BLK

    def scores(t, high, masked):
        k0 = t * ck if isinstance(t, int) else pl.multiple_of(t * ck, ck)
        s = lax.dot_general(kref[pl.ds(k0, ck), :], q, NT, preferred_element_type=f32)
        if masked:
            s = mask_first(t, s)
        s_ref[pl.ds(k0, ck), :] = s
        if live is None:
            return jnp.maximum(high, fold(s, jnp.max))
        for b in range(per):
            top = fold(s[b * BLK : (b + 1) * BLK], jnp.max) + live(t * per + b)
            high = jnp.maximum(high, top)
        return high

    high = jnp.full((8, width), NEG, f32)
    if live is None:
        high = lax.fori_loop(0, chunks, lambda t, m: scores(t, m, True), high)
    else:
        high = scores(0, high, True)
        high = lax.fori_loop(1, chunks, lambda t, m: scores(t, m, False), high)
    high = jnp.max(high, axis=0, keepdims=True)

    def weigh(t, carry):
        total, inner = carry
        k0 = pl.multiple_of(t * ck, ck)
        dp = lax.dot_general(vref[pl.ds(k0, ck), :], go, NT, preferred_element_type=f32)
        for b in range(per):
            top = high if live is None else high - live(t * per + b)
            rows = pl.ds(pl.multiple_of(k0 + b * BLK, BLK), BLK)
            w = jnp.exp2((s_ref[rows, :] - top) * LOG2E_SCALING)
            part = dp[b * BLK : (b + 1) * BLK]
            s_ref[rows, :] = w
            dp_ref[rows, :] = part
            total = total + fold(w, jnp.sum)
            inner = inner + fold(w * part, jnp.sum)
        return total, inner

    zero = jnp.zeros((8, width), f32)
    total, inner = lax.fori_loop(0, chunks, weigh, (zero, zero))
    inverse = 1.0 / jnp.sum(total, axis=0, keepdims=True)
    delta = jnp.sum(inner, axis=0, keepdims=True) * inverse

    def gradients(t, carry):
        k0 = pl.multiple_of(t * ck, ck)
        rows = pl.ds(k0, ck)
        probs = s_ref[rows, :] * inverse
        dscore = (probs * (dp_ref[rows, :] - delta)).astype(bf16)
        dk_ref[rows, :] += lax.dot_general(dscore, q, NN, preferred_element_type=f32)
        dv_ref[rows, :] += lax.dot_general(probs.astype(bf16), go, NN, preferred_element_type=f32)
        dq_ref[...] += lax.dot_general(kref[rows, :], dscore, TN, preferred_element_type=f32)
        return carry

    lax.fori_loop(0, chunks, gradients, 0)


def attend_kernel(
    ck, n, nsel, sel, q_ref, go_ref, gc_ref, gs_ref, kv_ref, ckv_ref, dq_out, dkv_out, dckv_out,
    acc, cacc, ksel, vsel, dks, dvs, s_ref, dp_ref, dqt, qt, gst, gct, slot,
):
    block = pl.program_id(0)
    me = lax.axis_index("ctx")
    group = lax.axis_index("tp") // 2
    own = 2 * n + block

    @pl.when(block == 0)
    def _():
        acc[...] = jnp.zeros_like(acc)
        cacc[...] = jnp.zeros_like(cacc)

        def clear(i, carry):
            slot[i] = 0
            return carry

        lax.fori_loop(0, 4 * n, clear, 0)
        for r in range(4):

            def mark(j, carry):
                name = sel[r, group, j]

                @pl.when(name >= 0)
                def _():
                    slot[name] = 1

                return carry

            lax.fori_loop(0, nsel, mark, 0)

        def place(i, carry):
            count = jnp.int32(0)
            for b in range(4):
                used = slot[i * 4 + b]
                slot[i * 4 + b] = i * 2 + jnp.minimum(count, 1)
                count = count + used
            return carry

        lax.fori_loop(0, n, place, 0)

    def where_is(j):
        if j == 0:
            return own
        name = sel[block, group, j - 1]
        return jnp.where(name >= 0, slot[jnp.maximum(name, 0)], own)

    for j in range(nsel + 1):
        at = where_is(j)
        ksel[j * BLK : (j + 1) * BLK, :] = kv_ref[0, at]
        vsel[j * BLK : (j + 1) * BLK, :] = kv_ref[1, at]
    gate_c = gc_ref[...].T
    gate_s = gs_ref[...].T
    for h in range(HEADS_DEV):
        rows = slice(h * BLK, (h + 1) * BLK)
        qt[rows, :] = q_ref[:, h * HD : (h + 1) * HD]
        wide = go_ref[:, h * HD : (h + 1) * HD].astype(f32)
        gct[rows, :] = (wide * gate_c[:, h : h + 1]).astype(bf16)
        gst[rows, :] = (wide * gate_s[:, h : h + 1]).astype(bf16)
    dks[...] = jnp.zeros_like(dks)
    dvs[...] = jnp.zeros_like(dvs)
    start = (me * 4 + block) * BLK

    def live(j):
        name = sel[block, group, jnp.maximum(j - 1, 0)]
        return jnp.where(jnp.logical_or(name >= 0, j == 0), 0.0, NEG).astype(f32)

    def before(t, s):
        key = lax.broadcasted_iota(jnp.int32, s.shape, 0) * STRIDE + t * (ck * STRIDE)
        row = lax.broadcasted_iota(jnp.int32, s.shape, 1) & (BLK - 1)
        return jnp.where(key - row <= start, s, NEG)

    def diagonal(t, s):
        key = lax.broadcasted_iota(jnp.int32, s.shape, 0)
        row = lax.broadcasted_iota(jnp.int32, s.shape, 1) & (BLK - 1)
        return jnp.where((key <= row) | (key >= BLK), s, NEG)

    dqt[...] = jnp.zeros_like(dqt)
    q = qt[...]
    branch(
        ckv_ref.at[0], ckv_ref.at[1], q, gct[...], before, None,
        s_ref, dp_ref, dqt, cacc.at[0], cacc.at[1], ck,
    )
    branch(ksel, vsel, q, gst[...], diagonal, live, s_ref, dp_ref, dqt, dks, dvs, ck)
    for h in range(HEADS_DEV):
        cols = slice(h * HD, (h + 1) * HD)
        dq_out[:, cols] = (dqt[:, cols].T * SCALING).astype(bf16)
    for j in range(nsel + 1):
        at = where_is(j)
        acc[0, at] += dks[j * BLK : (j + 1) * BLK, :]
        acc[1, at] += dvs[j * BLK : (j + 1) * BLK, :]

    @pl.when(block == pl.num_programs(0) - 1)
    def _():
        dkv_out[0] = (acc[0] * SCALING).astype(bf16)
        dkv_out[1] = acc[1].astype(bf16)
        dckv_out[0] = (cacc[0] * SCALING).astype(bf16)
        dckv_out[1] = cacc[1].astype(bf16)


def attend(selections, queries, grad_out, gates_c, gates_s, kv, ckv):
    n = lax.axis_size("ctx")
    blocks, _, nsel = selections.shape
    keys = (nsel + 1) * BLK
    ctok = ckv.shape[1]
    width = HEADS_DEV * BLK
    whole = lambda shape: pl.BlockSpec(shape, lambda i: (0,) * len(shape))
    rows = pl.BlockSpec((BLK, width), lambda i: (i, 0))
    gates = pl.BlockSpec((HEADS_DEV, BLK), lambda i: (0, i))
    return pl.pallas_call(
        functools.partial(attend_kernel, 512, n, nsel),
        grid=(blocks,),
        in_specs=[
            pl.BlockSpec(memory_space=pltpu.SMEM), rows, rows, gates, gates,
            whole(kv.shape), whole(ckv.shape),
        ],
        out_specs=[rows, whole(kv.shape), whole(ckv.shape)],
        out_shape=[
            jax.ShapeDtypeStruct(queries.shape, bf16),
            jax.ShapeDtypeStruct(kv.shape, bf16),
            jax.ShapeDtypeStruct(ckv.shape, bf16),
        ],
        scratch_shapes=[
            pltpu.VMEM(kv.shape, f32),
            pltpu.VMEM(ckv.shape, f32),
            pltpu.VMEM((keys, HD), bf16),
            pltpu.VMEM((keys, HD), bf16),
            pltpu.VMEM((keys, HD), f32),
            pltpu.VMEM((keys, HD), f32),
            pltpu.VMEM((keys, width), f32),
            pltpu.VMEM((keys, width), f32),
            pltpu.VMEM((HD, width), f32),
            pltpu.VMEM((width, HD), bf16),
            pltpu.VMEM((width, HD), bf16),
            pltpu.VMEM((width, HD), bf16),
            pltpu.SMEM((4 * n,), jnp.int32),
        ],
        compiler_params=pltpu.CompilerParams(
            vmem_limit_bytes=56 * 1024 * 1024, dimension_semantics=("arbitrary",)
        ),
        name="attend",
    )(selections, queries, grad_out, gates_c, gates_s, kv, ckv)


MESH = pl.DeviceIdType.MESH


def spots():
    me = lax.axis_index("ctx")
    tp = lax.axis_index("tp")
    return me, tp, lax.rem(tp, 2)


def enter(n, me, tp, core):
    barrier = pltpu.get_barrier_semaphore()
    for d in range(1, n):
        pl.semaphore_signal(
            barrier, inc=1, device_id=(lax.rem(me + d, n), tp), device_id_type=MESH
        )
    pl.semaphore_signal(barrier, inc=1, device_id=(me, tp + 1 - 2 * core), device_id_type=MESH)
    pl.semaphore_wait(barrier, n)


def remote(src, dst, send, recv, ctx, tp):
    return pltpu.make_async_remote_copy(
        src_ref=src, dst_ref=dst, send_sem=send, recv_sem=recv, device_id=(ctx, tp), device_id_type=MESH
    )


def gather_kernel(
    n, sel, keys, values, ckeys, cvalues, kv, ckv, need_out,
    own, owned, ownf, want, need_in, pack,
    in_sem, keep_sem, ns, nr, cs, cr, ks, kr, fs, fr,
):
    me, tp, core = spots()
    group = tp // 2
    partner = tp + 1 - 2 * core
    cols = pl.ds(pl.multiple_of(group * HD, HD), HD)
    loads = [
        pltpu.make_async_copy(ckeys.at[:, cols], owned.at[0], in_sem.at[0]),
        pltpu.make_async_copy(cvalues.at[:, cols], owned.at[1], in_sem.at[1]),
        pltpu.make_async_copy(keys.at[:, cols], own.at[0], in_sem.at[2]),
        pltpu.make_async_copy(values.at[:, cols], own.at[1], in_sem.at[3]),
    ]
    for load in loads:
        load.start()
    row = lax.broadcasted_iota(jnp.int32, (8 * n, HD), 0)
    quarter = lax.rem(row, 4)
    ident = 4 * (row // 8) + quarter
    used = jnp.zeros((8 * n, HD), f32)
    for r in range(4):
        for j in range(sel.shape[2]):
            used = jnp.where(ident == sel[r, group, j], 1.0, used)
    ahead = jnp.zeros_like(used)
    for k in range(1, 4):
        ahead = ahead + jnp.where(quarter >= k, pltpu.roll(used, k, 0), 0.0)
    place = lax.rem(row // 4, 2).astype(f32)
    want[...] = jnp.where(ahead == place, used, 0.0)
    for load in loads:
        load.wait()
    enter(n, me, tp, core)
    ctok = ckeys.shape[0]
    crows = pl.ds(pl.multiple_of(me * ctok, ctok), ctok)
    my_slots = pl.ds(pl.multiple_of(me * 2 * BLK, 2 * BLK), 2 * BLK)

    def slots(i):
        return pl.ds(pl.multiple_of(i * 2 * BLK, 2 * BLK), 2 * BLK)

    def send_need(i):
        rows = pl.ds(pl.multiple_of(i * 8, 8), 8)
        return remote(want.at[rows, :], need_in.at[me], ns.at[i], nr.at[me], i, tp)

    def send_comp(j):
        return remote(owned, ckv.at[:, crows, :], cs.at[j], cr.at[me], j, tp)

    def send_kv(j):
        return remote(pack.at[j], kv.at[core, my_slots, :], ks.at[j], kr.at[me], j, tp)

    def forward(i):
        return remote(
            kv.at[core, slots(i), :], kv.at[core, slots(i), :], fs.at[i], fr.at[i], me, partner
        )

    def need_from(j):
        return remote(want.at[pl.ds(0, 8), :], need_in.at[j], ns.at[j], nr.at[j], j, tp)

    def comp_from(j):
        rows = pl.ds(pl.multiple_of(j * ctok, ctok), ctok)
        return remote(owned, ckv.at[:, rows, :], cs.at[j], cr.at[j], j, tp)

    def kv_from(i):
        return remote(pack.at[i], kv.at[core, slots(i), :], ks.at[i], kr.at[i], i, tp)

    def forwarded(i):
        return remote(
            kv.at[core, slots(i), :], kv.at[1 - core, slots(i), :], fs.at[i], fr.at[i], me, partner
        )

    def down(fn):
        def step(k, carry):
            fn(me - 1 - k)
            return carry

        lax.fori_loop(0, me, step, 0)

    def up(fn):
        def step(j, carry):
            fn(j)
            return carry

        lax.fori_loop(me + 1, n, step, 0)

    down(lambda i: send_need(i).start())
    keep = [
        pltpu.make_async_copy(own, kv.at[:, pl.ds(2 * n * BLK, 4 * BLK), :], keep_sem.at[0]),
        pltpu.make_async_copy(owned, ckv.at[:, crows, :], keep_sem.at[1]),
    ]
    for copy in keep:
        copy.start()

    def others(fn):
        def step(d, carry):
            fn(lax.rem(me + d, n))
            return carry

        lax.fori_loop(1, n, step, 0)

    others(lambda j: send_comp(j).start())
    ownf[...] = own[core].astype(f32)

    def pack_and_send(j):
        need_from(j).wait_recv()
        mask = need_in[j]
        for s in range(2):
            total = mask[4 * s : 4 * s + 1] * ownf[:BLK, :]
            for b in range(1, 4):
                total = total + mask[4 * s + b : 4 * s + b + 1] * ownf[b * BLK : (b + 1) * BLK, :]
            pack[j, s * BLK : (s + 1) * BLK, :] = total.astype(bf16)
        need_out[j] = mask
        send_kv(j).start()

    up(pack_and_send)

    def pass_on(i):
        kv_from(i).wait_recv()
        forward(i).start()

    down(pass_on)
    down(lambda i: forwarded(i).wait_recv())
    others(lambda j: comp_from(j).wait_recv())
    down(lambda i: send_need(i).wait_send())
    up(lambda j: send_kv(j).wait_send())
    down(lambda i: forward(i).wait_send())
    others(lambda j: send_comp(j).wait_send())
    for copy in keep:
        copy.wait()


def reduce_kernel(
    n, dkv, dckv, need, dk_out, dv_out, dck_out, dcv_out,
    mine, mown, mcomp, xin, xown, xcomp, pack, recv, csend, crecv, acc, fin, cfin, fin_in, cfin_in,
    in_sem, xs, xr, ss, sr, cs, cr, es, er,
):
    me, tp, core = spots()
    partner = tp + 1 - 2 * core
    ctok = dckv.shape[1] // n
    base = 2 * n * BLK

    def slots(i):
        return pl.ds(pl.multiple_of(i * 2 * BLK, 2 * BLK), 2 * BLK)

    loads = [
        pltpu.make_async_copy(dckv.at[core], mcomp, in_sem.at[0]),
        pltpu.make_async_copy(dkv.at[core, pl.ds(0, base), :], mine, in_sem.at[1]),
        pltpu.make_async_copy(dkv.at[core, pl.ds(base, 4 * BLK), :], mown, in_sem.at[2]),
    ]
    for load in loads:
        load.start()
    enter(n, me, tp, core)

    def down(fn):
        def step(k, carry):
            fn(me - 1 - k)
            return carry

        lax.fori_loop(0, me, step, 0)

    def up(fn):
        def step(j, carry):
            fn(j)
            return carry

        lax.fori_loop(me + 1, n, step, 0)

    swap_comp = remote(dckv.at[1 - core], xcomp, xs.at[n], xr.at[n], me, partner)
    swap_own = remote(
        dkv.at[1 - core, pl.ds(base, 4 * BLK), :], xown, xs.at[n + 1], xr.at[n + 1], me, partner
    )

    def swap(i):
        return remote(dkv.at[1 - core, slots(i), :], xin.at[i], xs.at[i], xr.at[i], me, partner)

    def send(i):
        return remote(pack.at[i], recv.at[me], ss.at[i], sr.at[me], i, tp)

    def came(j):
        return remote(pack.at[j], recv.at[j], ss.at[j], sr.at[j], j, tp)

    def comp_rows(i):
        return pl.ds(pl.multiple_of(i * ctok, ctok), ctok)

    def send_comp(i):
        return remote(csend.at[comp_rows(i), :], crecv.at[me], cs.at[i], cr.at[me], i, tp)

    def comp_came(j):
        return remote(csend.at[comp_rows(j), :], crecv.at[j], cs.at[j], cr.at[j], j, tp)

    swap_comp.start()
    down(lambda i: swap(i).start())
    swap_own.start()
    for load in loads:
        load.wait()

    def add_and_send(i):
        swap(i).wait_recv()
        pack[i] = (mine[slots(i), :].astype(f32) + xin[i].astype(f32)).astype(bf16)
        send(i).start()

    down(add_and_send)
    swap_comp.wait_recv()
    csend[...] = (mcomp[...].astype(f32) + xcomp[...].astype(f32)).astype(bf16)
    down(lambda i: send_comp(i).start())
    swap_own.wait_recv()
    acc[...] = mown[...].astype(f32) + xown[...].astype(f32)
    rows = comp_rows(me)
    ctotal = mcomp[rows, :].astype(f32) + xcomp[rows, :].astype(f32)

    def take(j):
        came(j).wait_recv()
        mask = need[j]
        part = recv[j].astype(f32)
        for b in range(4):
            acc[b * BLK : (b + 1) * BLK, :] += (
                mask[b : b + 1] * part[:BLK] + mask[4 + b : 5 + b] * part[BLK:]
            )

    up(take)

    def ctake(j, total):
        comp_came(j).wait_recv()
        return total + crecv[j].astype(f32)

    ctotal = lax.fori_loop(me + 1, n, ctake, ctotal)
    cfin[...] = ctotal.astype(bf16)
    for b in range(4):
        fin[:, b * BLK : (b + 1) * BLK] = acc[b * BLK : (b + 1) * BLK, :].T.astype(bf16)
    half = HD // 2
    theirs = pl.ds(pl.multiple_of((1 - core) * half, half), half)
    ours = pl.ds(pl.multiple_of(core * half, half), half)
    ends = [
        remote(fin.at[theirs, :], fin_in, es.at[0], er.at[0], me, partner),
        remote(cfin, cfin_in, es.at[1], er.at[1], me, partner),
    ]
    for end in ends:
        end.start()
    kept = fin[ours, :]
    first = core == 0
    ckept = jnp.where(first, cfin[:, :half], cfin[:, half:])
    for end in ends:
        end.wait_recv()
    got = fin_in[...]
    cgot = jnp.where(first, cfin_in[:, :half], cfin_in[:, half:])
    dk_out[...] = jnp.where(first, kept, got)
    dv_out[...] = jnp.where(first, got, kept)
    dck_out[...] = jnp.where(first, ckept, cgot)
    dcv_out[...] = jnp.where(first, cgot, ckept)
    down(lambda i: swap(i).wait_send())
    swap_comp.wait_send()
    swap_own.wait_send()
    down(lambda i: send(i).wait_send())
    down(lambda i: send_comp(i).wait_send())
    for end in ends:
        end.wait_send()


def local(queries, keys, values, comp_keys, comp_values, gate_comp, gate_sel, grad_out, selections):
    n = lax.axis_size("ctx")
    ctok = comp_keys.shape[0]
    anywhere = pl.BlockSpec(memory_space=pl.ANY)
    scalars = pl.BlockSpec(memory_space=pltpu.SMEM)
    vmem = pl.BlockSpec(memory_space=pltpu.VMEM)
    dma = pltpu.SemaphoreType.DMA
    slot_rows = (2 * n + 4) * BLK
    kv, ckv, need = pl.pallas_call(
        functools.partial(gather_kernel, n),
        in_specs=[scalars] + [anywhere] * 4,
        out_specs=[anywhere, anywhere, vmem],
        out_shape=[
            jax.ShapeDtypeStruct((2, slot_rows, HD), bf16),
            jax.ShapeDtypeStruct((2, n * ctok, HD), bf16),
            jax.ShapeDtypeStruct((n, 8, HD), f32),
        ],
        scratch_shapes=[
            pltpu.VMEM((2, 4 * BLK, HD), bf16),
            pltpu.VMEM((2, ctok, HD), bf16),
            pltpu.VMEM((4 * BLK, HD), f32),
            pltpu.VMEM((8 * n, HD), f32),
            pltpu.VMEM((n, 8, HD), f32),
            pltpu.VMEM((n, 2 * BLK, HD), bf16),
            dma((4,)), dma((2,)),
            dma((n,)), dma((n,)), dma((n,)), dma((n,)),
            dma((n,)), dma((n,)), dma((n,)), dma((n,)),
        ],
        compiler_params=pltpu.CompilerParams(
            collective_id=0, has_side_effects=True, vmem_limit_bytes=16 * 1024 * 1024
        ),
        name="gather",
    )(selections, keys, values, comp_keys, comp_values)
    grad_queries, dkv, dckv = attend(
        selections, queries, grad_out, gate_comp.T, gate_sel.T,
        kv.reshape(2, 2 * n + 4, BLK, HD), ckv,
    )
    dk, dv, dck, dcv = pl.pallas_call(
        functools.partial(reduce_kernel, n),
        in_specs=[anywhere, anywhere, vmem],
        out_specs=[vmem] * 4,
        out_shape=[
            jax.ShapeDtypeStruct((HD // 2, 4 * BLK), bf16),
            jax.ShapeDtypeStruct((HD // 2, 4 * BLK), bf16),
            jax.ShapeDtypeStruct((ctok, HD // 2), bf16),
            jax.ShapeDtypeStruct((ctok, HD // 2), bf16),
        ],
        scratch_shapes=[
            pltpu.VMEM((2 * n * BLK, HD), bf16),
            pltpu.VMEM((4 * BLK, HD), bf16),
            pltpu.VMEM((n * ctok, HD), bf16),
            pltpu.VMEM((n, 2 * BLK, HD), bf16),
            pltpu.VMEM((4 * BLK, HD), bf16),
            pltpu.VMEM((n * ctok, HD), bf16),
            pltpu.VMEM((n, 2 * BLK, HD), bf16),
            pltpu.VMEM((n, 2 * BLK, HD), bf16),
            pltpu.VMEM((n * ctok, HD), bf16),
            pltpu.VMEM((n, ctok, HD), bf16),
            pltpu.VMEM((4 * BLK, HD), f32),
            pltpu.VMEM((HD, 4 * BLK), bf16),
            pltpu.VMEM((ctok, HD), bf16),
            pltpu.VMEM((HD // 2, 4 * BLK), bf16),
            pltpu.VMEM((ctok, HD), bf16),
            dma((3,)),
            dma((n + 2,)), dma((n + 2,)), dma((n,)), dma((n,)), dma((n,)), dma((n,)),
            dma((2,)), dma((2,)),
        ],
        compiler_params=pltpu.CompilerParams(
            collective_id=1, has_side_effects=True, vmem_limit_bytes=24 * 1024 * 1024
        ),
        name="reduce",
    )(dkv.reshape(2, slot_rows, HD), dckv, need)
    return grad_queries, dk.T, dv.T, dck, dcv


def solution(mesh):
    placed = (
        P("ctx", "tp"),
        P("ctx", None),
        P("ctx", None),
        P("ctx", None),
        P("ctx", None),
        P("ctx", "tp"),
        P("ctx", "tp"),
        P("ctx", "tp"),
        P("ctx", None, None),
    )
    return jax.shard_map(
        local,
        mesh=mesh,
        in_specs=placed,
        out_specs=(P("ctx", "tp"), P("ctx", "tp"), P("ctx", "tp"), P("ctx", "tp"), P("ctx", "tp")),
        check_vma=False,
    )
```

```python
import functools
import math

import jax
import jax.numpy as jnp
from jax import lax
from jax.experimental import pallas as pl
from jax.experimental.pallas import tpu as pltpu
from jax.sharding import PartitionSpec as P

HD = 128
BLK = 128
STRIDE = 16
HEADS_DEV = 8
NEG = -1e30
SCALING = 1.0 / math.sqrt(HD)
LOG2E_SCALING = math.log2(math.e) / math.sqrt(HD)
NN = (((1,), (0,)), ((), ()))
NT = (((1,), (1,)), ((), ()))
TN = (((0,), (0,)), ((), ()))
GRANT = 60 * 1024 * 1024
f32 = jnp.float32
bf16 = jnp.bfloat16


def fold(x, op):
    return op(x.reshape(x.shape[0] // 8, 8, x.shape[1]), axis=0)


def loop(low, high, fn, carry):
    if high - low == 1:
        return fn(low, carry)
    return lax.fori_loop(low, high, fn, carry)


def at_chunk(t, ck):
    return t * ck if isinstance(t, int) else pl.multiple_of(t * ck, ck)


def halves(dk, dv):
    half = HD // 2
    low = lax.broadcasted_iota(jnp.int32, dk.shape, 1) < half
    return (
        jnp.where(low, dk, pltpu.roll(dv, half, 1)),
        jnp.where(low, pltpu.roll(dk, half, 1), dv),
    )


def branch(kref, vref, q, go, mask_first, live, s_ref, dp_ref, dq_ref, dk_ref, dv_ref, ck):
    nkeys, width = kref.shape[0], q.shape[0]
    chunks = nkeys // ck
    per = ck // BLK

    def scores(t, high, masked):
        k0 = at_chunk(t, ck)
        s = lax.dot_general(kref[pl.ds(k0, ck), :], q, NT, preferred_element_type=f32)
        if masked:
            s = mask_first(t, s)
        s_ref[pl.ds(k0, ck), :] = s
        if live is None:
            return jnp.maximum(high, fold(s, jnp.max))
        for b in range(per):
            top = fold(s[b * BLK : (b + 1) * BLK], jnp.max) + live(t * per + b)
            high = jnp.maximum(high, top)
        return high

    high = jnp.full((8, width), NEG, f32)
    if live is None:
        high = loop(0, chunks, lambda t, m: scores(t, m, True), high)
    else:
        high = scores(0, high, True)
        high = loop(1, chunks, lambda t, m: scores(t, m, False), high)
    high = jnp.max(high, axis=0, keepdims=True)

    def weigh(t, carry):
        total, inner = carry
        k0 = at_chunk(t, ck)
        dp = lax.dot_general(vref[pl.ds(k0, ck), :], go, NT, preferred_element_type=f32)
        for b in range(per):
            top = high if live is None else high - live(t * per + b)
            rows = pl.ds(k0 + b * BLK if isinstance(k0, int) else pl.multiple_of(k0 + b * BLK, BLK), BLK)
            w = jnp.exp2((s_ref[rows, :] - top) * LOG2E_SCALING)
            part = dp[b * BLK : (b + 1) * BLK]
            s_ref[rows, :] = w
            dp_ref[rows, :] = part
            total = total + fold(w, jnp.sum)
            inner = inner + fold(w * part, jnp.sum)
        return total, inner

    zero = jnp.zeros((8, width), f32)
    total, inner = loop(0, chunks, weigh, (zero, zero))
    inverse = 1.0 / jnp.sum(total, axis=0, keepdims=True)
    delta = jnp.sum(inner, axis=0, keepdims=True) * inverse

    def gradients(t, carry):
        k0 = at_chunk(t, ck)
        rows = pl.ds(k0, ck)
        probs = s_ref[rows, :] * inverse
        dscore = (probs * (dp_ref[rows, :] - delta)).astype(bf16)
        dk_ref[rows, :] += lax.dot_general(dscore, q, NN, preferred_element_type=f32)
        dv_ref[rows, :] += lax.dot_general(probs.astype(bf16), go, NN, preferred_element_type=f32)
        dq_ref[...] += lax.dot_general(kref[rows, :], dscore, TN, preferred_element_type=f32)
        return carry

    loop(0, chunks, gradients, 0)


def attend_kernel(
    ck, n, nsel, sel, q_ref, go_ref, gs_ref, kv_ref, dqc_ref, dq_out, dkv_out,
    acc, ksel, vsel, dks, dvs, s_ref, dp_ref, dqt, qt, gst, slot,
):
    block = pl.program_id(0)
    group = lax.axis_index("tp") // 2
    own = 2 * n + block

    @pl.when(block == 0)
    def _():
        acc[...] = jnp.zeros_like(acc)

        def clear(i, carry):
            slot[i] = 0
            return carry

        lax.fori_loop(0, 4 * n, clear, 0)
        for r in range(4):

            def mark(j, carry):
                name = sel[r, group, j]

                @pl.when(name >= 0)
                def _():
                    slot[name] = 1

                return carry

            lax.fori_loop(0, nsel, mark, 0)

        def place(i, carry):
            count = jnp.int32(0)
            for b in range(4):
                used = slot[i * 4 + b]
                slot[i * 4 + b] = i * 2 + jnp.minimum(count, 1)
                count = count + used
            return carry

        lax.fori_loop(0, n, place, 0)

    def where_is(j):
        if j == 0:
            return own
        name = sel[block, group, j - 1]
        return jnp.where(name >= 0, slot[jnp.maximum(name, 0)], own)

    for j in range(nsel + 1):
        at = where_is(j)
        ksel[j * BLK : (j + 1) * BLK, :] = kv_ref[0, at]
        vsel[j * BLK : (j + 1) * BLK, :] = kv_ref[1, at]
    gate_s = gs_ref[...].T
    for h in range(HEADS_DEV):
        rows = slice(h * BLK, (h + 1) * BLK)
        qt[rows, :] = q_ref[:, h * HD : (h + 1) * HD]
        wide = go_ref[:, h * HD : (h + 1) * HD].astype(f32)
        gst[rows, :] = (wide * gate_s[:, h : h + 1]).astype(bf16)
    dks[...] = jnp.zeros_like(dks)
    dvs[...] = jnp.zeros_like(dvs)

    def live(j):
        name = sel[block, group, jnp.maximum(j - 1, 0)]
        return jnp.where(jnp.logical_or(name >= 0, j == 0), 0.0, NEG).astype(f32)

    def diagonal(t, s):
        key = lax.broadcasted_iota(jnp.int32, s.shape, 0)
        row = lax.broadcasted_iota(jnp.int32, s.shape, 1) & (BLK - 1)
        return jnp.where((key <= row) | (key >= BLK), s, NEG)

    dqt[...] = dqc_ref[0]
    branch(ksel, vsel, qt[...], gst[...], diagonal, live, s_ref, dp_ref, dqt, dks, dvs, ck)
    for h in range(HEADS_DEV):
        cols = slice(h * HD, (h + 1) * HD)
        dq_out[:, cols] = (dqt[:, cols].T * SCALING).astype(bf16)
    for j in range(nsel + 1):
        at = where_is(j)
        acc[0, at] += dks[j * BLK : (j + 1) * BLK, :]
        acc[1, at] += dvs[j * BLK : (j + 1) * BLK, :]

    @pl.when(block == pl.num_programs(0) - 1)
    def _():
        def finish(i, carry):
            first, second = halves(acc[0, i] * SCALING, acc[1, i])
            dkv_out[0, i] = first.astype(bf16)
            dkv_out[1, i] = second.astype(bf16)
            return carry

        lax.fori_loop(0, acc.shape[1], finish, 0)


def attend(selections, queries, grad_out, gates_s, kv, dqc):
    n = lax.axis_size("ctx")
    blocks, _, nsel = selections.shape
    keys = (nsel + 1) * BLK
    width = HEADS_DEV * BLK
    whole = lambda shape: pl.BlockSpec(shape, lambda i: (0,) * len(shape))
    rows = pl.BlockSpec((BLK, width), lambda i: (i, 0))
    gates = pl.BlockSpec((HEADS_DEV, BLK), lambda i: (0, i))
    return pl.pallas_call(
        functools.partial(attend_kernel, 512, n, nsel),
        grid=(blocks,),
        in_specs=[
            pl.BlockSpec(memory_space=pltpu.SMEM), rows, rows, gates,
            whole(kv.shape), pl.BlockSpec((1, HD, width), lambda i: (i, 0, 0)),
        ],
        out_specs=[rows, whole(kv.shape)],
        out_shape=[
            jax.ShapeDtypeStruct(queries.shape, bf16),
            jax.ShapeDtypeStruct(kv.shape, bf16),
        ],
        scratch_shapes=[
            pltpu.VMEM(kv.shape, f32),
            pltpu.VMEM((keys, HD), bf16),
            pltpu.VMEM((keys, HD), bf16),
            pltpu.VMEM((keys, HD), f32),
            pltpu.VMEM((keys, HD), f32),
            pltpu.VMEM((keys, width), f32),
            pltpu.VMEM((keys, width), f32),
            pltpu.VMEM((HD, width), f32),
            pltpu.VMEM((width, HD), bf16),
            pltpu.VMEM((width, HD), bf16),
            pltpu.SMEM((4 * n,), jnp.int32),
        ],
        compiler_params=pltpu.CompilerParams(
            vmem_limit_bytes=GRANT, dimension_semantics=("arbitrary",)
        ),
        name="attend",
    )(selections, queries, grad_out, gates_s, kv, dqc)


MESH = pl.DeviceIdType.MESH


def spots():
    me = lax.axis_index("ctx")
    tp = lax.axis_index("tp")
    return me, tp, lax.rem(tp, 2)


def enter(n, me, tp, core):
    barrier = pltpu.get_barrier_semaphore()
    for d in range(1, n):
        pl.semaphore_signal(
            barrier, inc=1, device_id=(lax.rem(me + d, n), tp), device_id_type=MESH
        )
    pl.semaphore_signal(barrier, inc=1, device_id=(me, tp + 1 - 2 * core), device_id_type=MESH)
    pl.semaphore_wait(barrier, n)


def remote(src, dst, send, recv, ctx, tp):
    return pltpu.make_async_remote_copy(
        src_ref=src, dst_ref=dst, send_sem=send, recv_sem=recv, device_id=(ctx, tp), device_id_type=MESH
    )


def gather_kernel(
    n, sel, keys, values, ckeys, cvalues, queries, grads, gc_ref, kv, need_out, dqc, dckv,
    own, owned, ownf, want, need_in, pack, ckv, q_all, go_all, qt, gct, s_ref, dp_ref, dqt, cacc,
    in_sem, keep_sem, dq_sem, ns, nr, cs, cr, ks, kr, fs, fr,
):
    me, tp, core = spots()
    group = tp // 2
    partner = tp + 1 - 2 * core
    cols = pl.ds(pl.multiple_of(group * HD, HD), HD)
    loads = [
        pltpu.make_async_copy(ckeys.at[:, cols], owned.at[0], in_sem.at[0]),
        pltpu.make_async_copy(cvalues.at[:, cols], owned.at[1], in_sem.at[1]),
        pltpu.make_async_copy(keys.at[:, cols], own.at[0], in_sem.at[2]),
        pltpu.make_async_copy(values.at[:, cols], own.at[1], in_sem.at[3]),
    ]
    late = [
        pltpu.make_async_copy(queries, q_all, in_sem.at[4]),
        pltpu.make_async_copy(grads, go_all, in_sem.at[5]),
    ]
    for load in loads + late:
        load.start()
    row = lax.broadcasted_iota(jnp.int32, (8 * n, HD), 0)
    quarter = lax.rem(row, 4)
    ident = 4 * (row // 8) + quarter
    used = jnp.zeros((8 * n, HD), f32)
    for r in range(4):
        for j in range(sel.shape[2]):
            used = jnp.where(ident == sel[r, group, j], 1.0, used)
    ahead = jnp.zeros_like(used)
    for k in range(1, 4):
        ahead = ahead + jnp.where(quarter >= k, pltpu.roll(used, k, 0), 0.0)
    place = lax.rem(row // 4, 2).astype(f32)
    want[...] = jnp.where(ahead == place, used, 0.0)
    for load in loads:
        load.wait()
    enter(n, me, tp, core)
    ctok = ckeys.shape[0]
    crows = pl.ds(pl.multiple_of(me * ctok, ctok), ctok)
    my_slots = pl.ds(pl.multiple_of(me * 2 * BLK, 2 * BLK), 2 * BLK)

    def slots(i):
        return pl.ds(pl.multiple_of(i * 2 * BLK, 2 * BLK), 2 * BLK)

    def send_need(i):
        rows = pl.ds(pl.multiple_of(i * 8, 8), 8)
        return remote(want.at[rows, :], need_in.at[me], ns.at[i], nr.at[me], i, tp)

    def send_comp(j):
        return remote(owned, ckv.at[:, crows, :], cs.at[j], cr.at[me], j, tp)

    def send_kv(j):
        return remote(pack.at[j], kv.at[core, my_slots, :], ks.at[j], kr.at[me], j, tp)

    def forward(i):
        return remote(
            kv.at[core, slots(i), :], kv.at[core, slots(i), :], fs.at[i], fr.at[i], me, partner
        )

    def need_from(j):
        return remote(want.at[pl.ds(0, 8), :], need_in.at[j], ns.at[j], nr.at[j], j, tp)

    def comp_from(j):
        rows = pl.ds(pl.multiple_of(j * ctok, ctok), ctok)
        return remote(owned, ckv.at[:, rows, :], cs.at[j], cr.at[j], j, tp)

    def kv_from(i):
        return remote(pack.at[i], kv.at[core, slots(i), :], ks.at[i], kr.at[i], i, tp)

    def forwarded(i):
        return remote(
            kv.at[core, slots(i), :], kv.at[1 - core, slots(i), :], fs.at[i], fr.at[i], me, partner
        )

    def down(fn):
        def step(k, carry):
            fn(me - 1 - k)
            return carry

        lax.fori_loop(0, me, step, 0)

    def up(fn):
        def step(j, carry):
            fn(j)
            return carry

        lax.fori_loop(me + 1, n, step, 0)

    down(lambda i: send_need(i).start())
    keep = [
        pltpu.make_async_copy(own, kv.at[:, pl.ds(2 * n * BLK, 4 * BLK), :], keep_sem.at[0]),
        pltpu.make_async_copy(owned, ckv.at[:, crows, :], keep_sem.at[1]),
    ]
    for copy in keep:
        copy.start()

    def others(fn):
        def step(d, carry):
            fn(lax.rem(me + d, n))
            return carry

        lax.fori_loop(1, n, step, 0)

    others(lambda j: send_comp(j).start())
    ownf[...] = own[core].astype(f32)

    def pack_and_send(j):
        need_from(j).wait_recv()
        mask = need_in[j]
        for s in range(2):
            total = mask[4 * s : 4 * s + 1] * ownf[:BLK, :]
            for b in range(1, 4):
                total = total + mask[4 * s + b : 4 * s + b + 1] * ownf[b * BLK : (b + 1) * BLK, :]
            pack[j, s * BLK : (s + 1) * BLK, :] = total.astype(bf16)
        need_out[j] = mask
        send_kv(j).start()

    up(pack_and_send)

    gate = gc_ref[...].T
    cacc[...] = jnp.zeros_like(cacc)
    for load in late:
        load.wait()
    others(lambda j: comp_from(j).wait_recv())
    keep[1].wait()
    ck = n * ctok

    def compressed(block, slot):
        tokens = pl.ds(block * BLK, BLK)
        start = (me * 4 + block) * BLK
        for h in range(HEADS_DEV):
            rows = slice(h * BLK, (h + 1) * BLK)
            cols = slice(h * HD, (h + 1) * HD)
            qt[rows, :] = q_all[tokens, cols]
            scale = gate[block * BLK : (block + 1) * BLK, h : h + 1]
            gct[rows, :] = (go_all[tokens, cols].astype(f32) * scale).astype(bf16)

        def before(t, s):
            key = lax.broadcasted_iota(jnp.int32, s.shape, 0) * STRIDE + t * (ck * STRIDE)
            row = lax.broadcasted_iota(jnp.int32, s.shape, 1) & (BLK - 1)
            return jnp.where(key - row <= start, s, NEG)

        dqt[slot] = jnp.zeros((HD, qt.shape[0]), f32)
        branch(
            ckv.at[0], ckv.at[1], qt[...], gct[...], before, None,
            s_ref, dp_ref, dqt.at[slot], cacc.at[0], cacc.at[1], ck,
        )

    def save(block):
        return pltpu.make_async_copy(dqt.at[block], dqc.at[block], dq_sem.at[block])

    def pass_on(i):
        kv_from(i).wait_recv()
        forward(i).start()

    for block in range(3):
        compressed(block, block)
        save(block).start()
    down(pass_on)
    compressed(3, 3)
    save(3).start()
    first, second = halves(cacc[0] * SCALING, cacc[1])
    dckv[0] = first.astype(bf16)
    dckv[1] = second.astype(bf16)
    down(lambda i: forwarded(i).wait_recv())
    down(lambda i: send_need(i).wait_send())
    up(lambda j: send_kv(j).wait_send())
    down(lambda i: forward(i).wait_send())
    others(lambda j: send_comp(j).wait_send())
    keep[0].wait()
    for block in range(4):
        save(block).wait()


def reduce_kernel(
    n, dkv, dckv, need, total_out, ctotal_out,
    mine, mown, mcomp, xin, xown, xcomp, pack, recv, acc,
    in_sem, xs, xr, ss, sr,
):
    me, tp, core = spots()
    partner = tp + 1 - 2 * core
    ctok = dckv.shape[1] // n
    base = 2 * n * BLK
    pair = 2 * BLK

    def slots(i):
        return pl.ds(pl.multiple_of(i * pair, pair), pair)

    def comp_rows(i):
        return pl.ds(pl.multiple_of(i * ctok, ctok), ctok)

    loads = [
        pltpu.make_async_copy(dckv.at[core], mcomp, in_sem.at[0]),
        pltpu.make_async_copy(dkv.at[core, pl.ds(0, base), :], mine, in_sem.at[1]),
        pltpu.make_async_copy(dkv.at[core, pl.ds(base, 4 * BLK), :], mown, in_sem.at[2]),
    ]
    for load in loads:
        load.start()
    enter(n, me, tp, core)

    def below(fn):
        def step(i, carry):
            fn(i)
            return carry

        lax.fori_loop(0, me, step, 0)

    swap_comp = remote(dckv.at[1 - core], xcomp, xs.at[n], xr.at[n], me, partner)
    swap_own = remote(
        dkv.at[1 - core, pl.ds(base, 4 * BLK), :], xown, xs.at[n + 1], xr.at[n + 1], me, partner
    )

    def swap(i):
        return remote(dkv.at[1 - core, slots(i), :], xin.at[i], xs.at[i], xr.at[i], me, partner)

    def send(i):
        return remote(pack.at[i], recv.at[me], ss.at[i], sr.at[me], i, tp)

    def came(j):
        return remote(pack.at[j], recv.at[j], ss.at[j], sr.at[j], j, tp)

    swap_comp.start()
    below(lambda i: swap(i).start())
    swap_own.start()
    for load in loads:
        load.wait()
    swap_comp.wait_recv()

    def add_and_send(i):
        swap(i).wait_recv()
        pack[i, :pair, :] = (mine[slots(i), :].astype(f32) + xin[i].astype(f32)).astype(bf16)
        rows = comp_rows(i)
        pack[i, pair:, :] = (mcomp[rows, :].astype(f32) + xcomp[rows, :].astype(f32)).astype(bf16)
        send(i).start()

    below(add_and_send)
    swap_own.wait_recv()
    acc[...] = mown[...].astype(f32) + xown[...].astype(f32)
    rows = comp_rows(me)

    def take(k, ctotal):
        j = n - 1 - k
        came(j).wait_recv()
        mask = need[j]
        part = recv[j].astype(f32)
        for b in range(4):
            acc[b * BLK : (b + 1) * BLK, :] += (
                mask[b : b + 1] * part[:BLK] + mask[4 + b : 5 + b] * part[BLK:pair]
            )
        return ctotal + part[pair:]

    ctotal_out[...] = lax.fori_loop(
        0, n - 1 - me, take, mcomp[rows, :].astype(f32) + xcomp[rows, :].astype(f32)
    )
    for b in range(4):
        total_out[:, b * BLK : (b + 1) * BLK] = acc[b * BLK : (b + 1) * BLK, :].T.astype(bf16)
    below(lambda i: swap(i).wait_send())
    swap_comp.wait_send()
    swap_own.wait_send()
    below(lambda i: send(i).wait_send())


def part_kernel(total, ctotal, dk_out, dv_out, dck_out, dcv_out):
    half = HD // 2
    dk_out[...] = total[:half, :]
    dv_out[...] = total[half:, :]
    both = ctotal[...]
    dck_out[...] = both[:, :half].astype(bf16)
    dcv_out[...] = both[:, half:].astype(bf16)


def local(queries, keys, values, comp_keys, comp_values, gate_comp, gate_sel, grad_out, selections):
    n = lax.axis_size("ctx")
    ctok = comp_keys.shape[0]
    anywhere = pl.BlockSpec(memory_space=pl.ANY)
    scalars = pl.BlockSpec(memory_space=pltpu.SMEM)
    vmem = pl.BlockSpec(memory_space=pltpu.VMEM)
    dma = pltpu.SemaphoreType.DMA
    slot_rows = (2 * n + 4) * BLK
    width = HEADS_DEV * BLK
    kv, need, dqc, dckv = pl.pallas_call(
        functools.partial(gather_kernel, n),
        in_specs=[scalars] + [anywhere] * 6 + [vmem],
        out_specs=[anywhere, vmem, anywhere, vmem],
        out_shape=[
            jax.ShapeDtypeStruct((2, slot_rows, HD), bf16),
            jax.ShapeDtypeStruct((n, 8, HD), f32),
            jax.ShapeDtypeStruct((4, HD, width), f32),
            jax.ShapeDtypeStruct((2, n * ctok, HD), bf16),
        ],
        scratch_shapes=[
            pltpu.VMEM((2, 4 * BLK, HD), bf16),
            pltpu.VMEM((2, ctok, HD), bf16),
            pltpu.VMEM((4 * BLK, HD), f32),
            pltpu.VMEM((8 * n, HD), f32),
            pltpu.VMEM((n, 8, HD), f32),
            pltpu.VMEM((n, 2 * BLK, HD), bf16),
            pltpu.VMEM((2, n * ctok, HD), bf16),
            pltpu.VMEM(queries.shape, bf16),
            pltpu.VMEM(queries.shape, bf16),
            pltpu.VMEM((width, HD), bf16),
            pltpu.VMEM((width, HD), bf16),
            pltpu.VMEM((n * ctok, width), f32),
            pltpu.VMEM((n * ctok, width), f32),
            pltpu.VMEM((4, HD, width), f32),
            pltpu.VMEM((2, n * ctok, HD), f32),
            dma((6,)), dma((2,)), dma((4,)),
            dma((n,)), dma((n,)), dma((n,)), dma((n,)),
            dma((n,)), dma((n,)), dma((n,)), dma((n,)),
        ],
        compiler_params=pltpu.CompilerParams(
            collective_id=0, has_side_effects=True, vmem_limit_bytes=GRANT
        ),
        name="gather",
    )(
        selections, keys, values, comp_keys, comp_values, queries, grad_out,
        gate_comp.T,
    )
    grad_queries, dkv = attend(
        selections, queries, grad_out, gate_sel.T, kv.reshape(2, 2 * n + 4, BLK, HD), dqc
    )
    total, ctotal = pl.pallas_call(
        functools.partial(reduce_kernel, n),
        in_specs=[anywhere, anywhere, vmem],
        out_specs=[vmem] * 2,
        out_shape=[
            jax.ShapeDtypeStruct((HD, 4 * BLK), bf16),
            jax.ShapeDtypeStruct((ctok, HD), f32),
        ],
        scratch_shapes=[
            pltpu.VMEM((2 * n * BLK, HD), bf16),
            pltpu.VMEM((4 * BLK, HD), bf16),
            pltpu.VMEM((n * ctok, HD), bf16),
            pltpu.VMEM((n, 2 * BLK, HD), bf16),
            pltpu.VMEM((4 * BLK, HD), bf16),
            pltpu.VMEM((n * ctok, HD), bf16),
            pltpu.VMEM((n, 2 * BLK + ctok, HD), bf16),
            pltpu.VMEM((n, 2 * BLK + ctok, HD), bf16),
            pltpu.VMEM((4 * BLK, HD), f32),
            dma((3,)),
            dma((n + 2,)), dma((n + 2,)), dma((n,)), dma((n,)),
        ],
        compiler_params=pltpu.CompilerParams(
            collective_id=1, has_side_effects=True, vmem_limit_bytes=GRANT
        ),
        name="reduce",
    )(dkv.reshape(2, slot_rows, HD), dckv, need)
    half = jax.ShapeDtypeStruct((HD // 2, 4 * BLK), bf16)
    chalf = jax.ShapeDtypeStruct((ctok, HD // 2), bf16)
    dk, dv, dck, dcv = pl.pallas_call(
        part_kernel,
        in_specs=[vmem] * 2,
        out_specs=[vmem] * 4,
        out_shape=[half, half, chalf, chalf],
        name="part",
    )(total, ctotal)
    return grad_queries, dk.T, dv.T, dck, dcv


def solution(mesh):
    placed = (
        P("ctx", "tp"),
        P("ctx", None),
        P("ctx", None),
        P("ctx", None),
        P("ctx", None),
        P("ctx", "tp"),
        P("ctx", "tp"),
        P("ctx", "tp"),
        P("ctx", None, None),
    )
    return jax.shard_map(
        local,
        mesh=mesh,
        in_specs=placed,
        out_specs=(P("ctx", "tp"), P("ctx", "tp"), P("ctx", "tp"), P("ctx", "tp"), P("ctx", "tp")),
        check_vma=False,
    )
```

```python
import functools
import math

import jax
import jax.numpy as jnp
from jax import lax
from jax.experimental import pallas as pl
from jax.experimental.pallas import tpu as pltpu
from jax.sharding import PartitionSpec as P

HD = 128
BLK = 128
STRIDE = 16
HEADS_DEV = 8
NEG = -1e30
SCALING = 1.0 / math.sqrt(HD)
LOG2E_SCALING = math.log2(math.e) / math.sqrt(HD)
NN = (((1,), (0,)), ((), ()))
ROWS = 256
COLS = 512
GRANT = 60 * 1024 * 1024
f32 = jnp.float32
bf16 = jnp.bfloat16


def tiles(x, op):
    total = x[:, :HD]
    for t in range(1, x.shape[1] // HD):
        total = op(total, x[:, t * HD : (t + 1) * HD])
    return total


def column_chunks(width):
    return [slice(k0, k0 + COLS) for k0 in range(0, width, COLS)]


def weights(q, go, kt, vt, masked, s_ref, dp_ref):
    chunks = column_chunks(kt.shape[1])
    high = None
    for t, cols in enumerate(chunks):
        s = masked(t, lax.dot_general(q, kt[:, cols], NN, preferred_element_type=f32))
        s_ref[:, cols] = s
        top = tiles(s, jnp.maximum)
        high = top if high is None else jnp.maximum(high, top)
    high = jnp.max(high, axis=1, keepdims=True)
    total = inner = 0.0
    for cols in chunks:
        dp = lax.dot_general(go, vt[:, cols], NN, preferred_element_type=f32)
        w = jnp.exp2((s_ref[:, cols] - high) * LOG2E_SCALING)
        s_ref[:, cols] = w
        dp_ref[:, cols] = dp
        total = total + tiles(w, jnp.add)
        inner = inner + tiles(w * dp, jnp.add)
    inverse = 1.0 / jnp.sum(total, axis=1, keepdims=True)
    return inverse, jnp.sum(inner, axis=1, keepdims=True) * inverse


def branch(q, go, qt, got, kt, vt, keys, masked, s_ref, dp_ref, dk_ref, dv_ref):
    inverse, delta = weights(q, go, kt, vt, masked, s_ref, dp_ref)
    dq = 0.0
    for cols in column_chunks(kt.shape[1]):
        probs = s_ref[:, cols] * inverse
        dscore = (probs * (dp_ref[:, cols] - delta)).astype(bf16)
        dq = dq + lax.dot_general(dscore, keys[cols, :], NN, preferred_element_type=f32)
        dk_ref[:, cols] += lax.dot_general(qt, dscore, NN, preferred_element_type=f32)
        dv_ref[:, cols] += lax.dot_general(got, probs.astype(bf16), NN, preferred_element_type=f32)
    return dq


def attend_kernel(
    n, nsel, sel, q_ref, go_ref, gs_ref, kv_ref, dv_out, ds_out, where, source,
    acc, kt, vt, bias, s_ref, dp_ref, qs, gs, gt, slot,
):
    block = pl.program_id(0)
    group = lax.axis_index("tp") // 2
    own = 2 * n + block

    @pl.when(block == 0)
    def _():
        acc[...] = jnp.zeros_like(acc)

        def clear(i, carry):
            slot[i] = 0
            return carry

        lax.fori_loop(0, 4 * n, clear, 0)

        def nowhere(i, carry):
            for r in range(4):
                source[r, i] = nsel + 1
            return carry

        lax.fori_loop(0, 2 * n, nowhere, 0)
        for r in range(4):

            def mark(j, carry):
                name = sel[r, group, j]

                @pl.when(name >= 0)
                def _():
                    slot[name] = 1

                return carry

            lax.fori_loop(0, nsel, mark, 0)

        def place(i, carry):
            count = jnp.int32(0)
            for b in range(4):
                used = slot[i * 4 + b]
                slot[i * 4 + b] = i * 2 + jnp.minimum(count, 1)
                count = count + used
            return carry

        lax.fori_loop(0, n, place, 0)
        for r in range(4):
            where[r, 0] = 2 * n + r

            def point(j, carry):
                name = sel[r, group, j]
                at = jnp.where(name >= 0, slot[jnp.maximum(name, 0)], 2 * n + r)
                where[r, j + 1] = at

                @pl.when(name >= 0)
                def _():
                    source[r, at] = j + 1

                return carry

            lax.fori_loop(0, nsel, point, 0)

    for j in range(nsel + 1):
        at = where[block, j]
        cols = slice(j * BLK, (j + 1) * BLK)
        kt[:, cols] = kv_ref[0, at].T
        vt[:, cols] = kv_ref[1, at].T
        counts = jnp.float32(0.0)
        if j > 0:
            counts = jnp.where(sel[block, group, j - 1] >= 0, 0.0, NEG).astype(f32)
        bias[:, cols] = jnp.full((8, BLK), counts, f32)
    gate = gs_ref[...].T
    for h in range(HEADS_DEV):
        cols = slice(h * HD, (h + 1) * HD)
        rows = slice(h * BLK, (h + 1) * BLK)
        qs[rows, :] = q_ref[:, cols]
        gated = (go_ref[:, cols].astype(f32) * gate[:, h : h + 1]).astype(bf16)
        gs[rows, :] = gated
        gt[:, rows] = gated.T

    def masked(t, s):
        if t > 0:
            return s + bias[:1, t * COLS : (t + 1) * COLS]
        row = lax.broadcasted_iota(jnp.int32, (s.shape[0], BLK), 0) & (BLK - 1)
        key = lax.broadcasted_iota(jnp.int32, (s.shape[0], BLK), 1)
        own_part = jnp.where(key <= row, s[:, :BLK], NEG)
        return jnp.concatenate([own_part, s[:, BLK:] + bias[:1, BLK:COLS]], axis=1)

    inverse, delta = weights(qs[...], gs[...], kt, vt, masked, s_ref, dp_ref)
    for t, cols in enumerate(column_chunks(kt.shape[1])):
        probs = s_ref[:, cols] * inverse
        ds_out[0, :, cols] = (probs * (dp_ref[:, cols] - delta)).astype(bf16)
        dv = lax.dot_general(gt[...], probs.astype(bf16), NN, preferred_element_type=f32)
        for b in range(COLS // BLK):
            at = where[block, t * (COLS // BLK) + b]
            acc[at] += dv[:, b * BLK : (b + 1) * BLK]

    @pl.when(block == pl.num_programs(0) - 1)
    def _():
        half = HD // 2

        def finish(i, carry):
            for side in range(2):
                dv_out[side, i] = acc[i, side * half : (side + 1) * half, :].astype(bf16)
            return carry

        lax.fori_loop(0, acc.shape[0], finish, 0)


def attend(selections, queries, grad_out, gates_s, kv):
    n = lax.axis_size("ctx")
    blocks, _, nsel = selections.shape
    keys = (nsel + 1) * BLK
    width = HEADS_DEV * BLK
    whole = lambda shape: pl.BlockSpec(shape, lambda i: (0,) * len(shape))
    scalars = pl.BlockSpec(memory_space=pltpu.SMEM)
    rows = pl.BlockSpec((BLK, width), lambda i: (i, 0))
    half = (2, kv.shape[1], HD // 2, BLK)
    return pl.pallas_call(
        functools.partial(attend_kernel, n, nsel),
        grid=(blocks,),
        in_specs=[
            scalars, rows, rows, pl.BlockSpec((HEADS_DEV, BLK), lambda i: (0, i)), whole(kv.shape),
        ],
        out_specs=[
            whole(half), pl.BlockSpec((1, width, keys), lambda i: (i, 0, 0)), scalars, scalars,
        ],
        out_shape=[
            jax.ShapeDtypeStruct(half, bf16),
            jax.ShapeDtypeStruct((blocks, width, keys), bf16),
            jax.ShapeDtypeStruct((blocks, nsel + 1), jnp.int32),
            jax.ShapeDtypeStruct((blocks, 2 * n), jnp.int32),
        ],
        scratch_shapes=[
            pltpu.VMEM((kv.shape[1], HD, BLK), f32),
            pltpu.VMEM((HD, keys), bf16),
            pltpu.VMEM((HD, keys), bf16),
            pltpu.VMEM((8, keys), f32),
            pltpu.VMEM((width, keys), f32),
            pltpu.VMEM((width, keys), f32),
            pltpu.VMEM((width, HD), bf16),
            pltpu.VMEM((width, HD), bf16),
            pltpu.VMEM((HD, width), bf16),
            pltpu.SMEM((4 * n,), jnp.int32),
        ],
        compiler_params=pltpu.CompilerParams(
            vmem_limit_bytes=GRANT, dimension_semantics=("arbitrary",)
        ),
        name="attend",
    )(selections, queries, grad_out, gates_s, kv)


MESH = pl.DeviceIdType.MESH


def spots():
    me = lax.axis_index("ctx")
    tp = lax.axis_index("tp")
    return me, tp, lax.rem(tp, 2)


def enter(n, me, tp, core):
    barrier = pltpu.get_barrier_semaphore()
    for d in range(1, n):
        pl.semaphore_signal(
            barrier, inc=1, device_id=(lax.rem(me + d, n), tp), device_id_type=MESH
        )
    pl.semaphore_signal(barrier, inc=1, device_id=(me, tp + 1 - 2 * core), device_id_type=MESH)
    pl.semaphore_wait(barrier, n)


def remote(src, dst, send, recv, ctx, tp):
    return pltpu.make_async_remote_copy(
        src_ref=src, dst_ref=dst, send_sem=send, recv_sem=recv, device_id=(ctx, tp), device_id_type=MESH
    )


def gather_kernel(
    n, sel, keys, values, ckeys, cvalues, queries, grads, gc_ref, kv, need_out, dqc, dckv,
    own, owned, ownf, want, need_in, pack, ckv, q_all, go_all, ckt, cvt, s_ref, dp_ref, dqc_all, cacc,
    in_sem, keep_sem, dq_sem, ns, nr, cs, cr, ks, kr, fs, fr,
):
    me, tp, core = spots()
    group = tp // 2
    partner = tp + 1 - 2 * core
    cols = pl.ds(pl.multiple_of(group * HD, HD), HD)
    loads = [
        pltpu.make_async_copy(ckeys.at[:, cols], owned.at[0], in_sem.at[0]),
        pltpu.make_async_copy(cvalues.at[:, cols], owned.at[1], in_sem.at[1]),
        pltpu.make_async_copy(keys.at[:, cols], own.at[0], in_sem.at[2]),
        pltpu.make_async_copy(values.at[:, cols], own.at[1], in_sem.at[3]),
    ]
    late = [
        pltpu.make_async_copy(queries, q_all, in_sem.at[4]),
        pltpu.make_async_copy(grads, go_all, in_sem.at[5]),
    ]
    for load in loads + late:
        load.start()
    row = lax.broadcasted_iota(jnp.int32, (8 * n, HD), 0)
    quarter = lax.rem(row, 4)
    ident = 4 * (row // 8) + quarter
    used = jnp.zeros((8 * n, HD), f32)
    for r in range(4):
        for j in range(sel.shape[2]):
            used = jnp.where(ident == sel[r, group, j], 1.0, used)
    ahead = jnp.zeros_like(used)
    for k in range(1, 4):
        ahead = ahead + jnp.where(quarter >= k, pltpu.roll(used, k, 0), 0.0)
    place = lax.rem(row // 4, 2).astype(f32)
    want[...] = jnp.where(ahead == place, used, 0.0)
    for load in loads:
        load.wait()
    enter(n, me, tp, core)
    ctok = ckeys.shape[0]
    crows = pl.ds(pl.multiple_of(me * ctok, ctok), ctok)
    my_slots = pl.ds(pl.multiple_of(me * 2 * BLK, 2 * BLK), 2 * BLK)

    def slots(i):
        return pl.ds(pl.multiple_of(i * 2 * BLK, 2 * BLK), 2 * BLK)

    def send_need(i):
        rows = pl.ds(pl.multiple_of(i * 8, 8), 8)
        return remote(want.at[rows, :], need_in.at[me], ns.at[i], nr.at[me], i, tp)

    def send_comp(j):
        return remote(owned, ckv.at[:, crows, :], cs.at[j], cr.at[me], j, tp)

    def send_kv(j):
        return remote(pack.at[j], kv.at[core, my_slots, :], ks.at[j], kr.at[me], j, tp)

    def forward(i):
        return remote(
            kv.at[core, slots(i), :], kv.at[core, slots(i), :], fs.at[i], fr.at[i], me, partner
        )

    def need_from(j):
        return remote(want.at[pl.ds(0, 8), :], need_in.at[j], ns.at[j], nr.at[j], j, tp)

    def comp_from(j):
        rows = pl.ds(pl.multiple_of(j * ctok, ctok), ctok)
        return remote(owned, ckv.at[:, rows, :], cs.at[j], cr.at[j], j, tp)

    def kv_from(i):
        return remote(pack.at[i], kv.at[core, slots(i), :], ks.at[i], kr.at[i], i, tp)

    def forwarded(i):
        return remote(
            kv.at[core, slots(i), :], kv.at[1 - core, slots(i), :], fs.at[i], fr.at[i], me, partner
        )

    def down(fn):
        def step(k, carry):
            fn(me - 1 - k)
            return carry

        lax.fori_loop(0, me, step, 0)

    def up(fn):
        def step(j, carry):
            fn(j)
            return carry

        lax.fori_loop(me + 1, n, step, 0)

    down(lambda i: send_need(i).start())
    keep = [
        pltpu.make_async_copy(own, kv.at[:, pl.ds(2 * n * BLK, 4 * BLK), :], keep_sem.at[0]),
        pltpu.make_async_copy(owned, ckv.at[:, crows, :], keep_sem.at[1]),
    ]
    for copy in keep:
        copy.start()

    def others(fn):
        def step(d, carry):
            fn(lax.rem(me + d, n))
            return carry

        lax.fori_loop(1, n, step, 0)

    others(lambda j: send_comp(j).start())
    ownf[...] = own[core].astype(f32)

    def pack_and_send(j):
        need_from(j).wait_recv()
        mask = need_in[j]
        for s in range(2):
            total = mask[4 * s : 4 * s + 1] * ownf[:BLK, :]
            for b in range(1, 4):
                total = total + mask[4 * s + b : 4 * s + b + 1] * ownf[b * BLK : (b + 1) * BLK, :]
            pack[j, s * BLK : (s + 1) * BLK, :] = total.astype(bf16)
        need_out[j] = mask
        send_kv(j).start()

    up(pack_and_send)

    cacc[...] = jnp.zeros_like(cacc)
    for load in late:
        load.wait()
    others(lambda j: comp_from(j).wait_recv())
    keep[1].wait()
    ckt[...] = ckv[0].T
    cvt[...] = ckv[1].T
    gate = gc_ref[...].T

    def compressed(block):
        tokens = slice(block * BLK, (block + 1) * BLK)
        start = (me * 4 + block) * BLK

        def before(t, s):
            row = lax.broadcasted_iota(jnp.int32, s.shape, 0) & (BLK - 1)
            key = lax.broadcasted_iota(jnp.int32, s.shape, 1) * STRIDE + t * (COLS * STRIDE)
            return jnp.where(key - row <= start, s, NEG)

        for r in range(HEADS_DEV * BLK // ROWS):
            parts = range(r * ROWS // BLK, (r + 1) * ROWS // BLK)
            q = jnp.concatenate([q_all[tokens, h * HD : (h + 1) * HD] for h in parts], axis=0)
            go = jnp.concatenate(
                [
                    (go_all[tokens, h * HD : (h + 1) * HD].astype(f32) * gate[tokens, h : h + 1]).astype(bf16)
                    for h in parts
                ],
                axis=0,
            )
            dqc_all[block, r * ROWS : (r + 1) * ROWS, :] = branch(
                q, go, q.T, go.T, ckt, cvt, ckv.at[0], before,
                s_ref, dp_ref, cacc.at[0], cacc.at[1],
            )

    def save(block):
        return pltpu.make_async_copy(dqc_all.at[block], dqc.at[block], dq_sem.at[block])

    def pass_on(i):
        kv_from(i).wait_recv()
        forward(i).start()

    for block in range(3):
        compressed(block)
        save(block).start()
    down(pass_on)
    compressed(3)
    save(3).start()
    half = HD // 2
    for side in range(2):
        rows = slice(side * half, (side + 1) * half)
        joined = jnp.concatenate([cacc[0, rows, :] * SCALING, cacc[1, rows, :]], axis=0)
        dckv[side] = joined.T.astype(bf16)
    down(lambda i: forwarded(i).wait_recv())
    down(lambda i: send_need(i).wait_send())
    up(lambda j: send_kv(j).wait_send())
    down(lambda i: forward(i).wait_send())
    others(lambda j: send_comp(j).wait_send())
    keep[0].wait()
    for block in range(4):
        save(block).wait()


def reduce_kernel(
    n, dv, ds, dckv, need, queries, kv, dqc, where, source, total_out, ctotal_out, dq_out,
    ds_all, dks, mine, mcomp, xin, xown, xcomp, pack, recv, kmine, kgive, kin, kown_give, kown_in,
    kpack, krecv, acc, q_all, qt, kbuf, ksel, dqc_all,
    in_sem, ds_sem, xs, xr, ss, sr, ks, kr, ts, tr,
):
    me, tp, core = spots()
    partner = tp + 1 - 2 * core
    ctok = dckv.shape[1] // n
    half = HD // 2
    blocks, nkeys = ds.shape[0], ds.shape[2]
    per = nkeys // BLK
    own = pl.ds(2 * n, 4)

    def slots(i):
        return pl.ds(i * 2, 2)

    def comp_rows(i):
        return pl.ds(pl.multiple_of(i * ctok, ctok), ctok)

    loads = [
        pltpu.make_async_copy(queries, q_all, in_sem.at[0]),
        pltpu.make_async_copy(dckv.at[core], mcomp, in_sem.at[1]),
        pltpu.make_async_copy(dv.at[core], mine, in_sem.at[2]),
        pltpu.make_async_copy(kv.at[0], kbuf, in_sem.at[3]),
        pltpu.make_async_copy(dqc, dqc_all, in_sem.at[4]),
    ]
    ds_loads = [
        pltpu.make_async_copy(ds.at[b], ds_all.at[b], ds_sem.at[b]) for b in range(blocks)
    ]
    loads[0].start()
    ds_loads[0].start()
    for load in loads[1:] + ds_loads[1:]:
        load.start()
    enter(n, me, tp, core)

    def below(fn):
        def step(i, carry):
            fn(i)
            return carry

        lax.fori_loop(0, me, step, 0)

    swap_comp = remote(dckv.at[1 - core], xcomp, xs.at[n], xr.at[n], me, partner)
    swap_own = remote(dv.at[1 - core, own], xown, xs.at[n + 1], xr.at[n + 1], me, partner)
    swap_kown = remote(kown_give, kown_in, ts.at[n], tr.at[n], me, partner)

    def swap(i):
        return remote(dv.at[1 - core, slots(i)], xin.at[i], xs.at[i], xr.at[i], me, partner)

    def send(i):
        return remote(pack.at[i], recv.at[me], ss.at[i], sr.at[me], i, tp)

    def came(j):
        return remote(pack.at[j], recv.at[j], ss.at[j], sr.at[j], j, tp)

    def kswap(i):
        return remote(kgive.at[i], kin.at[i], ts.at[i], tr.at[i], me, partner)

    def ksend(i):
        return remote(kpack.at[i], krecv.at[me], ks.at[i], kr.at[me], i, tp)

    def kcame(j):
        return remote(kpack.at[j], krecv.at[j], ks.at[j], kr.at[j], j, tp)

    swap_comp.start()
    below(lambda i: swap(i).start())
    swap_own.start()
    for load in loads:
        load.wait()

    def add_and_send(i):
        swap(i).wait_recv()
        for s in range(2):
            pack[i, s * half : (s + 1) * half, :] = (
                mine[2 * i + s].astype(f32) + xin[i, s].astype(f32)
            ).astype(bf16)
        rows = comp_rows(i)
        pack[i, HD:, :] = (mcomp[rows, :].astype(f32) + xcomp[rows, :].astype(f32)).astype(bf16)
        send(i).start()

    for b in range(blocks):
        for h in range(HEADS_DEV):
            cols = slice(h * HD, (h + 1) * HD)
            qt[:, cols] = q_all[b * BLK : (b + 1) * BLK, cols].T
        ds_loads[b].wait()
        for t, cols in enumerate(column_chunks(nkeys)):
            dk = SCALING * lax.dot_general(qt[...], ds_all[b, :, cols], NN, preferred_element_type=f32)
            for c in range(COLS // BLK):
                dks[b * (per + 1) + t * (COLS // BLK) + c] = dk[:, c * BLK : (c + 1) * BLK]
        dks[b * (per + 1) + per] = jnp.zeros((HD, BLK), f32)
        if b == 0:
            swap_comp.wait_recv()
            below(add_and_send)
    first = core == 0

    def ours(x):
        return jnp.where(first, x[:half], x[half:])

    def theirs(x):
        return jnp.where(first, x[half:], x[:half])

    def slot_sum(i):
        for s in range(2):
            total = dks[source[0, 2 * i + s]]
            for b in range(1, blocks):
                total = total + dks[b * (per + 1) + source[b, 2 * i + s]]
            kmine[i, s * half : (s + 1) * half, :] = ours(total)
            kgive[i, s * half : (s + 1) * half, :] = theirs(total).astype(bf16)
        kswap(i).start()

    below(slot_sum)
    for b in range(blocks):
        kown_give[b] = theirs(dks[b * (per + 1)]).astype(bf16)
    swap_kown.start()

    def kadd_and_send(i):
        kswap(i).wait_recv()
        kpack[i] = (kmine[i] + kin[i].astype(f32)).astype(bf16)
        ksend(i).start()

    below(kadd_and_send)
    for b in range(blocks):
        for j in range(per):
            ksel[j * BLK : (j + 1) * BLK, :] = kbuf[where[b, j]]
        dq = dqc_all[b]
        for cols in column_chunks(nkeys):
            dq = dq + lax.dot_general(
                ds_all[b, :, cols], ksel[cols, :], NN, preferred_element_type=f32
            )
        for h in range(HEADS_DEV):
            dq_out[b * BLK : (b + 1) * BLK, h * HD : (h + 1) * HD] = (
                dq[h * BLK : (h + 1) * BLK] * SCALING
            ).astype(bf16)
    swap_own.wait_recv()
    swap_kown.wait_recv()
    for b in range(blocks):
        acc[b, half:, :] = mine[2 * n + b].astype(f32) + xown[b].astype(f32)
        acc[b, :half, :] = ours(dks[b * (per + 1)]) + kown_in[b].astype(f32)
    rows = comp_rows(me)

    def take(k, ctotal):
        j = n - 1 - k
        came(j).wait_recv()
        mask = need[j]
        part = recv[j].astype(f32)
        for b in range(4):
            acc[b, half:, :] += mask[b : b + 1] * part[:half] + mask[4 + b : 5 + b] * part[half:HD]
        return ctotal + part[HD:]

    ctotal_out[...] = lax.fori_loop(
        0, n - 1 - me, take, mcomp[rows, :].astype(f32) + xcomp[rows, :].astype(f32)
    )

    def ktake(k, carry):
        j = n - 1 - k
        kcame(j).wait_recv()
        mask = need[j]
        part = krecv[j].astype(f32)
        for b in range(4):
            acc[b, :half, :] += mask[b : b + 1] * part[:half] + mask[4 + b : 5 + b] * part[half:]
        return carry

    lax.fori_loop(0, n - 1 - me, ktake, 0)
    for b in range(4):
        total_out[:, b * BLK : (b + 1) * BLK] = acc[b].astype(bf16)
    below(lambda i: swap(i).wait_send())
    swap_comp.wait_send()
    swap_own.wait_send()
    swap_kown.wait_send()
    below(lambda i: send(i).wait_send())
    below(lambda i: kswap(i).wait_send())
    below(lambda i: ksend(i).wait_send())


def part_kernel(total, ctotal, dk_out, dv_out, dck_out, dcv_out):
    half = HD // 2
    dk_out[...] = total[:half, :]
    dv_out[...] = total[half:, :]
    both = ctotal[...]
    dck_out[...] = both[:, :half].astype(bf16)
    dcv_out[...] = both[:, half:].astype(bf16)


def local(queries, keys, values, comp_keys, comp_values, gate_comp, gate_sel, grad_out, selections):
    n = lax.axis_size("ctx")
    ctok = comp_keys.shape[0]
    anywhere = pl.BlockSpec(memory_space=pl.ANY)
    scalars = pl.BlockSpec(memory_space=pltpu.SMEM)
    vmem = pl.BlockSpec(memory_space=pltpu.VMEM)
    dma = pltpu.SemaphoreType.DMA
    slot_rows = (2 * n + 4) * BLK
    width = HEADS_DEV * BLK
    kv, need, dqc, dckv = pl.pallas_call(
        functools.partial(gather_kernel, n),
        in_specs=[scalars] + [anywhere] * 6 + [vmem],
        out_specs=[anywhere, vmem, anywhere, vmem],
        out_shape=[
            jax.ShapeDtypeStruct((2, slot_rows, HD), bf16),
            jax.ShapeDtypeStruct((n, 8, HD), f32),
            jax.ShapeDtypeStruct((4, width, HD), f32),
            jax.ShapeDtypeStruct((2, n * ctok, HD), bf16),
        ],
        scratch_shapes=[
            pltpu.VMEM((2, 4 * BLK, HD), bf16),
            pltpu.VMEM((2, ctok, HD), bf16),
            pltpu.VMEM((4 * BLK, HD), f32),
            pltpu.VMEM((8 * n, HD), f32),
            pltpu.VMEM((n, 8, HD), f32),
            pltpu.VMEM((n, 2 * BLK, HD), bf16),
            pltpu.VMEM((2, n * ctok, HD), bf16),
            pltpu.VMEM(queries.shape, bf16),
            pltpu.VMEM(queries.shape, bf16),
            pltpu.VMEM((HD, n * ctok), bf16),
            pltpu.VMEM((HD, n * ctok), bf16),
            pltpu.VMEM((ROWS, n * ctok), f32),
            pltpu.VMEM((ROWS, n * ctok), f32),
            pltpu.VMEM((4, width, HD), f32),
            pltpu.VMEM((2, HD, n * ctok), f32),
            dma((6,)), dma((2,)), dma((4,)),
            dma((n,)), dma((n,)), dma((n,)), dma((n,)),
            dma((n,)), dma((n,)), dma((n,)), dma((n,)),
        ],
        compiler_params=pltpu.CompilerParams(
            collective_id=0, has_side_effects=True, vmem_limit_bytes=GRANT
        ),
        name="gather",
    )(
        selections, keys, values, comp_keys, comp_values, queries, grad_out,
        gate_comp.T,
    )
    kv = kv.reshape(2, 2 * n + 4, BLK, HD)
    dv_half, ds, where, source = attend(selections, queries, grad_out, gate_sel.T, kv)
    blocks, _, nkeys = ds.shape
    half = HD // 2
    total, ctotal, grad_queries = pl.pallas_call(
        functools.partial(reduce_kernel, n),
        in_specs=[anywhere, anywhere, anywhere, vmem, anywhere, anywhere, anywhere, scalars, scalars],
        out_specs=[vmem] * 3,
        out_shape=[
            jax.ShapeDtypeStruct((HD, 4 * BLK), bf16),
            jax.ShapeDtypeStruct((ctok, HD), f32),
            jax.ShapeDtypeStruct(queries.shape, bf16),
        ],
        scratch_shapes=[
            pltpu.VMEM(ds.shape, bf16),
            pltpu.VMEM((blocks * (nkeys // BLK + 1), HD, BLK), f32),
            pltpu.VMEM((2 * n + 4, half, BLK), bf16),
            pltpu.VMEM((n * ctok, HD), bf16),
            pltpu.VMEM((n, 2, half, BLK), bf16),
            pltpu.VMEM((4, half, BLK), bf16),
            pltpu.VMEM((n * ctok, HD), bf16),
            pltpu.VMEM((n, HD + ctok, BLK), bf16),
            pltpu.VMEM((n, HD + ctok, BLK), bf16),
            pltpu.VMEM((n, HD, BLK), f32),
            pltpu.VMEM((n, HD, BLK), bf16),
            pltpu.VMEM((n, HD, BLK), bf16),
            pltpu.VMEM((4, half, BLK), bf16),
            pltpu.VMEM((4, half, BLK), bf16),
            pltpu.VMEM((n, HD, BLK), bf16),
            pltpu.VMEM((n, HD, BLK), bf16),
            pltpu.VMEM((4, HD, BLK), f32),
            pltpu.VMEM(queries.shape, bf16),
            pltpu.VMEM((HD, width), bf16),
            pltpu.VMEM((2 * n + 4, BLK, HD), bf16),
            pltpu.VMEM((nkeys, HD), bf16),
            pltpu.VMEM(dqc.shape, f32),
            dma((5,)), dma((blocks,)),
            dma((n + 2,)), dma((n + 2,)), dma((n,)), dma((n,)),
            dma((n,)), dma((n,)), dma((n + 1,)), dma((n + 1,)),
        ],
        compiler_params=pltpu.CompilerParams(
            collective_id=1, has_side_effects=True, vmem_limit_bytes=GRANT
        ),
        name="reduce",
    )(dv_half, ds, dckv, need, queries, kv, dqc, where, source)
    half = jax.ShapeDtypeStruct((HD // 2, 4 * BLK), bf16)
    chalf = jax.ShapeDtypeStruct((ctok, HD // 2), bf16)
    dk, dv, dck, dcv = pl.pallas_call(
        part_kernel,
        in_specs=[vmem] * 2,
        out_specs=[vmem] * 4,
        out_shape=[half, half, chalf, chalf],
        name="part",
    )(total, ctotal)
    return grad_queries, dk.T, dv.T, dck, dcv


def solution(mesh):
    placed = (
        P("ctx", "tp"),
        P("ctx", None),
        P("ctx", None),
        P("ctx", None),
        P("ctx", None),
        P("ctx", "tp"),
        P("ctx", "tp"),
        P("ctx", "tp"),
        P("ctx", None, None),
    )
    return jax.shard_map(
        local,
        mesh=mesh,
        in_specs=placed,
        out_specs=(P("ctx", "tp"), P("ctx", "tp"), P("ctx", "tp"), P("ctx", "tp"), P("ctx", "tp")),
        check_vma=False,
    )
```

```python
import functools
import math

import jax
import jax.numpy as jnp
from jax import lax
from jax.experimental import pallas as pl
from jax.experimental.pallas import tpu as pltpu
from jax.sharding import PartitionSpec as P

HD = 128
BLK = 128
STRIDE = 16
HEADS_DEV = 8
NEG = -1e30
SCALING = 1.0 / math.sqrt(HD)
LOG2E_SCALING = math.log2(math.e) / math.sqrt(HD)
NN = (((1,), (0,)), ((), ()))
ROWS = 512
COLS = 512
GRANT = 60 * 1024 * 1024
f32 = jnp.float32
bf16 = jnp.bfloat16


def tiles(x, op):
    total = x[:, :HD]
    for t in range(1, x.shape[1] // HD):
        total = op(total, x[:, t * HD : (t + 1) * HD])
    return total


def column_chunks(width):
    return [slice(k0, k0 + COLS) for k0 in range(0, width, COLS)]


class Rows:
    def __init__(self, q, go, kt, vt, masked, s_ref, dp_ref):
        self.q, self.go, self.kt, self.vt, self.masked = q, go, kt, vt, masked
        self.s_ref, self.dp_ref = s_ref, dp_ref
        self.chunks = column_chunks(kt.shape[1])
        self.high = self.total = self.inner = None

    def scores(self, t):
        cols = self.chunks[t]
        s = lax.dot_general(self.q, self.kt[:, cols], NN, preferred_element_type=f32)
        s = self.masked(t, s * LOG2E_SCALING)
        self.s_ref[:, cols] = s
        top = tiles(s, jnp.maximum)
        self.high = top if t == 0 else jnp.maximum(self.high, top)
        if t == len(self.chunks) - 1:
            self.high = jnp.max(self.high, axis=1, keepdims=True)

    def weigh(self, t):
        cols = self.chunks[t]
        dp = lax.dot_general(self.go, self.vt[:, cols], NN, preferred_element_type=f32)
        w = jnp.exp2(self.s_ref[:, cols] - self.high)
        self.s_ref[:, cols] = w
        self.dp_ref[:, cols] = dp
        total, inner = tiles(w, jnp.add), tiles(w * dp, jnp.add)
        self.total = total if t == 0 else self.total + total
        self.inner = inner if t == 0 else self.inner + inner
        if t == len(self.chunks) - 1:
            self.inverse = 1.0 / jnp.sum(self.total, axis=1, keepdims=True)
            self.delta = jnp.sum(self.inner, axis=1, keepdims=True) * self.inverse

    def probs(self, t):
        cols = self.chunks[t]
        p = self.s_ref[:, cols] * self.inverse
        return p.astype(bf16), (p * (self.dp_ref[:, cols] - self.delta)).astype(bf16)


def run_stages(parts, last):
    for k in range(len(parts) + 2):
        for t in range(len(parts[0].chunks)):
            if k < len(parts):
                parts[k].scores(t)
            if 0 <= k - 1 < len(parts):
                parts[k - 1].weigh(t)
            if 0 <= k - 2:
                last(k - 2, t)


def attend_kernel(
    n, nsel, sel, q_ref, go_ref, gs_ref, kv_ref, dq_out, dkv_out,
    acc, ksel, kt, vt, bias, s_ref, dp_ref, qs, gs, qt, gt, masks,
):
    block = pl.program_id(0)
    group = lax.axis_index("tp") // 2

    @pl.when(block == 0)
    def _():
        acc[...] = jnp.zeros_like(acc)
        words = [jnp.int32(0)] * (4 * n // 32)
        for r in range(4):
            for j in range(nsel):
                name = sel[r, group, j]
                bit = jnp.left_shift(jnp.int32(1), name & 31)
                for w in range(len(words)):
                    words[w] = words[w] | jnp.where((name >> 5) == w, bit, 0)
        for w, word in enumerate(words):
            masks[w] = word

    places = [2 * n + block]
    alive = [None]
    for j in range(nsel):
        name = sel[block, group, j]
        live = name >= 0
        safe = jnp.maximum(name, 0)
        before = jnp.right_shift(masks[safe >> 5], safe & 28) & (
            jnp.left_shift(jnp.int32(1), safe & 3) - 1
        )
        second = jnp.where(before != 0, 1, 0)
        places.append(jnp.where(live, 2 * (safe >> 2) + second, 2 * n + block))
        alive.append(live)
    for j, at in enumerate(places):
        cols = slice(j * BLK, (j + 1) * BLK)
        k = kv_ref[0, at]
        ksel[cols, :] = k
        kt[:, cols] = k.T
        vt[:, cols] = kv_ref[1, at].T
        counts = jnp.float32(0.0)
        if j > 0:
            counts = jnp.where(alive[j], 0.0, NEG).astype(f32)
        bias[:, cols] = jnp.full((8, BLK), counts, f32)
    gate = gs_ref[...].T
    for h in range(HEADS_DEV):
        cols = slice(h * HD, (h + 1) * HD)
        rows = slice(h * BLK, (h + 1) * BLK)
        q = q_ref[:, cols]
        qs[rows, :] = q
        qt[:, rows] = q.T
        gated = (go_ref[:, cols].astype(f32) * gate[:, h : h + 1]).astype(bf16)
        gs[rows, :] = gated
        gt[:, rows] = gated.T

    def masked(t, s):
        if t > 0:
            return s + bias[:1, t * COLS : (t + 1) * COLS]
        row = lax.broadcasted_iota(jnp.int32, (s.shape[0], BLK), 0) & (BLK - 1)
        key = lax.broadcasted_iota(jnp.int32, (s.shape[0], BLK), 1)
        own_part = jnp.where(key <= row, s[:, :BLK], NEG)
        return jnp.concatenate([own_part, s[:, BLK:] + bias[:1, BLK:COLS]], axis=1)

    spans = [slice(r, r + ROWS) for r in range(0, HEADS_DEV * BLK, ROWS)]
    parts = [
        Rows(qs[rows, :], gs[rows, :], kt, vt, masked, s_ref.at[rows], dp_ref.at[rows])
        for rows in spans
    ]

    def gradients(r, t):
        rows, cols = spans[r], parts[r].chunks[t]
        probs, dscore = parts[r].probs(t)
        dq = lax.dot_general(dscore, ksel[cols, :], NN, preferred_element_type=f32)
        dq_out[0, rows, :] = dq if t == 0 else dq + dq_out[0, rows, :]
        dk = lax.dot_general(qt[:, rows], dscore, NN, preferred_element_type=f32)
        dv = lax.dot_general(gt[:, rows], probs, NN, preferred_element_type=f32)
        for b in range(COLS // BLK):
            at = places[t * (COLS // BLK) + b]
            acc[0, at] += dk[:, b * BLK : (b + 1) * BLK]
            acc[1, at] += dv[:, b * BLK : (b + 1) * BLK]

    run_stages(parts, gradients)

    @pl.when(block == pl.num_programs(0) - 1)
    def _():
        half = HD // 2

        def finish(i, carry):
            for side in range(2):
                rows = slice(side * half, (side + 1) * half)
                dkv_out[side, i, :half, :] = (acc[0, i, rows, :] * SCALING).astype(bf16)
                dkv_out[side, i, half:, :] = acc[1, i, rows, :].astype(bf16)
            return carry

        lax.fori_loop(0, acc.shape[1], finish, 0)


def attend(selections, queries, grad_out, gates_s, kv):
    n = lax.axis_size("ctx")
    blocks, _, nsel = selections.shape
    keys = (nsel + 1) * BLK
    width = HEADS_DEV * BLK
    whole = lambda shape: pl.BlockSpec(shape, lambda i: (0,) * len(shape))
    rows = pl.BlockSpec((BLK, width), lambda i: (i, 0))
    return pl.pallas_call(
        functools.partial(attend_kernel, n, nsel),
        grid=(blocks,),
        in_specs=[
            pl.BlockSpec(memory_space=pltpu.SMEM), rows, rows,
            pl.BlockSpec((HEADS_DEV, BLK), lambda i: (0, i)), whole(kv.shape),
        ],
        out_specs=[pl.BlockSpec((1, width, HD), lambda i: (i, 0, 0)), whole(kv.shape)],
        out_shape=[
            jax.ShapeDtypeStruct((blocks, width, HD), f32),
            jax.ShapeDtypeStruct(kv.shape, bf16),
        ],
        scratch_shapes=[
            pltpu.VMEM(kv.shape, f32),
            pltpu.VMEM((keys, HD), bf16),
            pltpu.VMEM((HD, keys), bf16),
            pltpu.VMEM((HD, keys), bf16),
            pltpu.VMEM((8, keys), f32),
            pltpu.VMEM((width, keys), f32),
            pltpu.VMEM((width, keys), f32),
            pltpu.VMEM((width, HD), bf16),
            pltpu.VMEM((width, HD), bf16),
            pltpu.VMEM((HD, width), bf16),
            pltpu.VMEM((HD, width), bf16),
            pltpu.SMEM((4 * n // 32,), jnp.int32),
        ],
        compiler_params=pltpu.CompilerParams(
            vmem_limit_bytes=GRANT, dimension_semantics=("arbitrary",)
        ),
        name="attend",
    )(selections, queries, grad_out, gates_s, kv)


MESH = pl.DeviceIdType.MESH


def spots():
    me = lax.axis_index("ctx")
    tp = lax.axis_index("tp")
    return me, tp, lax.rem(tp, 2)


def greet(n, me, tp, core):
    barrier = pltpu.get_barrier_semaphore()
    for d in range(1, n):
        pl.semaphore_signal(
            barrier, inc=1, device_id=(lax.rem(me + d, n), tp), device_id_type=MESH
        )
    pl.semaphore_signal(barrier, inc=1, device_id=(me, tp + 1 - 2 * core), device_id_type=MESH)


def all_here(n):
    pl.semaphore_wait(pltpu.get_barrier_semaphore(), n)


def remote(src, dst, send, recv, ctx, tp):
    return pltpu.make_async_remote_copy(
        src_ref=src, dst_ref=dst, send_sem=send, recv_sem=recv, device_id=(ctx, tp), device_id_type=MESH
    )


def gather_kernel(
    n, sel, keys, values, ckeys, cvalues, kv, ckv, need_out,
    own, owned, ownf, want, need_in, pack,
    in_sem, keep_sem, ns, nr, cs, cr, ks, kr, fs, fr,
):
    me, tp, core = spots()
    group = tp // 2
    partner = tp + 1 - 2 * core
    cols = pl.ds(pl.multiple_of(group * HD, HD), HD)
    loads = [
        pltpu.make_async_copy(ckeys.at[:, cols], owned.at[0], in_sem.at[0]),
        pltpu.make_async_copy(cvalues.at[:, cols], owned.at[1], in_sem.at[1]),
        pltpu.make_async_copy(keys.at[:, cols], own.at[0], in_sem.at[2]),
        pltpu.make_async_copy(values.at[:, cols], own.at[1], in_sem.at[3]),
    ]
    greet(n, me, tp, core)
    for load in loads:
        load.start()
    row = lax.broadcasted_iota(jnp.int32, (8 * n, HD), 0)
    quarter = lax.rem(row, 4)
    ident = 4 * (row // 8) + quarter
    used = jnp.zeros((8 * n, HD), f32)
    for r in range(4):
        for j in range(sel.shape[2]):
            used = jnp.where(ident == sel[r, group, j], 1.0, used)
    ahead = jnp.zeros_like(used)
    for k in range(1, 4):
        ahead = ahead + jnp.where(quarter >= k, pltpu.roll(used, k, 0), 0.0)
    place = lax.rem(row // 4, 2).astype(f32)
    want[...] = jnp.where(ahead == place, used, 0.0)
    ctok = ckeys.shape[0]
    crows = pl.ds(pl.multiple_of(me * ctok, ctok), ctok)
    my_slots = pl.ds(pl.multiple_of(me * 2 * BLK, 2 * BLK), 2 * BLK)

    def slots(i):
        return pl.ds(pl.multiple_of(i * 2 * BLK, 2 * BLK), 2 * BLK)

    def send_need(i):
        rows = pl.ds(pl.multiple_of(i * 8, 8), 8)
        return remote(want.at[rows, :], need_in.at[me], ns.at[i], nr.at[me], i, tp)

    def send_comp(j):
        return remote(owned, ckv.at[:, crows, :], cs.at[j], cr.at[me], j, tp)

    def send_kv(j):
        return remote(pack.at[j], kv.at[core, my_slots, :], ks.at[j], kr.at[me], j, tp)

    def forward(i):
        return remote(
            kv.at[core, slots(i), :], kv.at[core, slots(i), :], fs.at[i], fr.at[i], me, partner
        )

    def need_from(j):
        return remote(want.at[pl.ds(0, 8), :], need_in.at[j], ns.at[j], nr.at[j], j, tp)

    def comp_from(j):
        rows = pl.ds(pl.multiple_of(j * ctok, ctok), ctok)
        return remote(owned, ckv.at[:, rows, :], cs.at[j], cr.at[j], j, tp)

    def kv_from(i):
        return remote(pack.at[i], kv.at[core, slots(i), :], ks.at[i], kr.at[i], i, tp)

    def forwarded(i):
        return remote(
            kv.at[core, slots(i), :], kv.at[1 - core, slots(i), :], fs.at[i], fr.at[i], me, partner
        )

    def down(fn):
        def step(k, carry):
            fn(me - 1 - k)
            return carry

        lax.fori_loop(0, me, step, 0)

    def up(fn):
        def step(j, carry):
            fn(j)
            return carry

        lax.fori_loop(me + 1, n, step, 0)

    all_here(n)
    down(lambda i: send_need(i).start())
    for load in loads:
        load.wait()
    keep = [
        pltpu.make_async_copy(own, kv.at[:, pl.ds(2 * n * BLK, 4 * BLK), :], keep_sem.at[0]),
        pltpu.make_async_copy(owned, ckv.at[:, crows, :], keep_sem.at[1]),
    ]
    for copy in keep:
        copy.start()

    def others(fn):
        def step(d, carry):
            fn(lax.rem(me + d, n))
            return carry

        lax.fori_loop(1, n, step, 0)

    ownf[...] = own[core].astype(f32)

    def pack_and_send(j):
        need_from(j).wait_recv()
        mask = need_in[j]
        for s in range(2):
            total = mask[4 * s : 4 * s + 1] * ownf[:BLK, :]
            for b in range(1, 4):
                total = total + mask[4 * s + b : 4 * s + b + 1] * ownf[b * BLK : (b + 1) * BLK, :]
            pack[j, s * BLK : (s + 1) * BLK, :] = total.astype(bf16)
        need_out[j] = mask
        send_kv(j).start()

    up(pack_and_send)
    others(lambda j: send_comp(j).start())

    def pass_on(i):
        kv_from(i).wait_recv()
        forward(i).start()

    down(pass_on)
    down(lambda i: forwarded(i).wait_recv())
    others(lambda j: comp_from(j).wait_recv())
    down(lambda i: send_need(i).wait_send())
    up(lambda j: send_kv(j).wait_send())
    down(lambda i: forward(i).wait_send())
    others(lambda j: send_comp(j).wait_send())
    for copy in keep:
        copy.wait()


def reduce_kernel(
    n, dkv, need, ckv, queries, grads, gc_ref, dq_sel, total_out, ctotal_out, dq_out,
    mine, mown, xin, xown, pack, recv, acc, ckv_in, ckt, cvt, q_all, go_all, s_ref, dp_ref, bias,
    dq_all, cacc, dckv, xcomp, cpack, crecv,
    in_sem, xs, xr, ss, sr, cs, cr,
):
    me, tp, core = spots()
    greet(n, me, tp, core)
    partner = tp + 1 - 2 * core
    ctok = ckv.shape[1] // n
    base = 2 * n * BLK
    pair = 2 * BLK
    half = HD // 2

    def slots(i):
        return pl.ds(pl.multiple_of(i * pair, pair), pair)

    def comp_rows(i):
        return pl.ds(pl.multiple_of(i * ctok, ctok), ctok)

    loads = [
        pltpu.make_async_copy(dkv.at[core, pl.ds(0, base), :], mine, in_sem.at[0]),
        pltpu.make_async_copy(dkv.at[core, pl.ds(base, 4 * BLK), :], mown, in_sem.at[1]),
    ]
    late = [
        pltpu.make_async_copy(ckv, ckv_in, in_sem.at[2]),
        pltpu.make_async_copy(queries, q_all, in_sem.at[3]),
        pltpu.make_async_copy(grads, go_all, in_sem.at[4]),
        pltpu.make_async_copy(dq_sel, dq_all, in_sem.at[5]),
    ]
    for load in loads:
        load.start()
    all_here(n)

    def below(fn):
        def step(i, carry):
            fn(i)
            return carry

        lax.fori_loop(0, me, step, 0)

    swap_comp = remote(dckv.at[1 - core], xcomp, xs.at[n], xr.at[n], me, partner)
    swap_own = remote(
        dkv.at[1 - core, pl.ds(base, 4 * BLK), :], xown, xs.at[n + 1], xr.at[n + 1], me, partner
    )

    def swap(i):
        return remote(dkv.at[1 - core, slots(i), :], xin.at[i], xs.at[i], xr.at[i], me, partner)

    def send(i):
        return remote(pack.at[i], recv.at[me], ss.at[i], sr.at[me], i, tp)

    def came(j):
        return remote(pack.at[j], recv.at[j], ss.at[j], sr.at[j], j, tp)

    def send_comp(i):
        return remote(cpack.at[comp_rows(i), :], crecv.at[me], cs.at[i], cr.at[me], i, tp)

    def comp_came(j):
        return remote(cpack.at[comp_rows(j), :], crecv.at[j], cs.at[j], cr.at[j], j, tp)

    below(lambda i: swap(i).start())
    swap_own.start()
    for load in late:
        load.start()
    for load in loads:
        load.wait()

    def add_and_send(i):
        swap(i).wait_recv()
        pack[i] = (mine[slots(i), :].astype(f32) + xin[i].astype(f32)).astype(bf16)
        send(i).start()

    below(add_and_send)
    gate = gc_ref[...].T
    cacc[...] = jnp.zeros_like(cacc)
    for load in late:
        load.wait()
    ckt[...] = ckv_in[0].T
    cvt[...] = ckv_in[1].T

    def compressed(block):
        tokens = slice(block * BLK, (block + 1) * BLK)
        start = (me * 4 + block) * BLK

        row = lax.broadcasted_iota(jnp.int32, (BLK, ckt.shape[1]), 0)
        key = lax.broadcasted_iota(jnp.int32, (BLK, ckt.shape[1]), 1) * STRIDE
        bias[...] = jnp.where(key - row <= start, 0.0, NEG)

        def before(t, s):
            part = bias[:, t * COLS : (t + 1) * COLS]
            return s + jnp.concatenate([part] * (ROWS // BLK), axis=0)

        spans = [slice(r, r + ROWS) for r in range(0, HEADS_DEV * BLK, ROWS)]
        parts, sides = [], []
        for rows in spans:
            heads = range(rows.start // BLK, rows.stop // BLK)
            q = jnp.concatenate([q_all[tokens, h * HD : (h + 1) * HD] for h in heads], axis=0)
            go = jnp.concatenate(
                [
                    (go_all[tokens, h * HD : (h + 1) * HD].astype(f32) * gate[tokens, h : h + 1]).astype(bf16)
                    for h in heads
                ],
                axis=0,
            )
            parts.append(Rows(q, go, ckt, cvt, before, s_ref.at[rows], dp_ref.at[rows]))
            sides.append((q.T, go.T))

        def gradients(r, t):
            probs, dscore = parts[r].probs(t)
            cols = parts[r].chunks[t]
            dq_all[block, spans[r], :] += lax.dot_general(
                dscore, ckv_in[0, cols, :], NN, preferred_element_type=f32
            )
            cacc[0, :, cols] += lax.dot_general(sides[r][0], dscore, NN, preferred_element_type=f32)
            cacc[1, :, cols] += lax.dot_general(sides[r][1], probs, NN, preferred_element_type=f32)

        run_stages(parts, gradients)

        for h in range(HEADS_DEV):
            dq_out[tokens, h * HD : (h + 1) * HD] = (
                dq_all[block, h * BLK : (h + 1) * BLK, :] * SCALING
            ).astype(bf16)

    for block in range(4):
        compressed(block)
    for side in range(2):
        rows = slice(side * half, (side + 1) * half)
        joined = jnp.concatenate([cacc[0, rows, :] * SCALING, cacc[1, rows, :]], axis=0)
        dckv[side] = joined.T.astype(bf16)
    swap_comp.start()
    swap_own.wait_recv()
    acc[...] = mown[...].astype(f32) + xown[...].astype(f32)
    swap_comp.wait_recv()
    cpack[...] = (dckv[core].astype(f32) + xcomp[...].astype(f32)).astype(bf16)
    below(lambda i: send_comp(i).start())

    def take(k, carry):
        j = n - 1 - k
        came(j).wait_recv()
        mask = need[j]
        part = recv[j].astype(f32)
        for b in range(4):
            acc[b * BLK : (b + 1) * BLK, :] += (
                mask[b : b + 1] * part[:BLK] + mask[4 + b : 5 + b] * part[BLK:]
            )
        return carry

    lax.fori_loop(0, n - 1 - me, take, 0)
    for b in range(4):
        total_out[:, b * BLK : (b + 1) * BLK] = acc[b * BLK : (b + 1) * BLK, :].astype(bf16)

    def ctake(k, ctotal):
        j = n - 1 - k
        comp_came(j).wait_recv()
        return ctotal + crecv[j].astype(f32)

    ctotal_out[...] = lax.fori_loop(0, n - 1 - me, ctake, cpack[comp_rows(me), :].astype(f32))
    below(lambda i: swap(i).wait_send())
    swap_comp.wait_send()
    swap_own.wait_send()
    below(lambda i: send(i).wait_send())
    below(lambda i: send_comp(i).wait_send())


def part_kernel(total, ctotal, dq, dq_out, dk_out, dv_out, dck_out, dcv_out):
    half = HD // 2
    dq_out[...] = dq[...]
    dk_out[...] = total[:half, :]
    dv_out[...] = total[half:, :]
    both = ctotal[...]
    dck_out[...] = both[:, :half].astype(bf16)
    dcv_out[...] = both[:, half:].astype(bf16)


def local(queries, keys, values, comp_keys, comp_values, gate_comp, gate_sel, grad_out, selections):
    n = lax.axis_size("ctx")
    ctok = comp_keys.shape[0]
    anywhere = pl.BlockSpec(memory_space=pl.ANY)
    scalars = pl.BlockSpec(memory_space=pltpu.SMEM)
    vmem = pl.BlockSpec(memory_space=pltpu.VMEM)
    dma = pltpu.SemaphoreType.DMA
    slot_rows = (2 * n + 4) * BLK
    width = HEADS_DEV * BLK
    kv, ckv, need = pl.pallas_call(
        functools.partial(gather_kernel, n),
        in_specs=[scalars] + [anywhere] * 4,
        out_specs=[anywhere, anywhere, vmem],
        out_shape=[
            jax.ShapeDtypeStruct((2, slot_rows, HD), bf16),
            jax.ShapeDtypeStruct((2, n * ctok, HD), bf16),
            jax.ShapeDtypeStruct((n, 8, HD), f32),
        ],
        scratch_shapes=[
            pltpu.VMEM((2, 4 * BLK, HD), bf16),
            pltpu.VMEM((2, ctok, HD), bf16),
            pltpu.VMEM((4 * BLK, HD), f32),
            pltpu.VMEM((8 * n, HD), f32),
            pltpu.VMEM((n, 8, HD), f32),
            pltpu.VMEM((n, 2 * BLK, HD), bf16),
            dma((4,)), dma((2,)),
            dma((n,)), dma((n,)), dma((n,)), dma((n,)),
            dma((n,)), dma((n,)), dma((n,)), dma((n,)),
        ],
        compiler_params=pltpu.CompilerParams(
            collective_id=0, has_side_effects=True, vmem_limit_bytes=GRANT
        ),
        name="gather",
    )(selections, keys, values, comp_keys, comp_values)
    dq_sel, dkv = attend(
        selections, queries, grad_out, gate_sel.T, kv.reshape(2, 2 * n + 4, BLK, HD)
    )
    total, ctotal, dq = pl.pallas_call(
        functools.partial(reduce_kernel, n),
        in_specs=[anywhere, vmem, anywhere, anywhere, anywhere, vmem, anywhere],
        out_specs=[vmem] * 3,
        out_shape=[
            jax.ShapeDtypeStruct((HD, 4 * BLK), bf16),
            jax.ShapeDtypeStruct((ctok, HD), f32),
            jax.ShapeDtypeStruct(queries.shape, bf16),
        ],
        scratch_shapes=[
            pltpu.VMEM((2 * n * BLK, HD), bf16),
            pltpu.VMEM((4 * BLK, HD), bf16),
            pltpu.VMEM((n, 2 * BLK, HD), bf16),
            pltpu.VMEM((4 * BLK, HD), bf16),
            pltpu.VMEM((n, 2 * BLK, HD), bf16),
            pltpu.VMEM((n, 2 * BLK, HD), bf16),
            pltpu.VMEM((4 * BLK, HD), f32),
            pltpu.VMEM((2, n * ctok, HD), bf16),
            pltpu.VMEM((HD, n * ctok), bf16),
            pltpu.VMEM((HD, n * ctok), bf16),
            pltpu.VMEM(queries.shape, bf16),
            pltpu.VMEM(queries.shape, bf16),
            pltpu.VMEM((width, n * ctok), f32),
            pltpu.VMEM((width, n * ctok), f32),
            pltpu.VMEM((BLK, n * ctok), f32),
            pltpu.VMEM((4, width, HD), f32),
            pltpu.VMEM((2, HD, n * ctok), f32),
            pltpu.VMEM((2, n * ctok, HD), bf16),
            pltpu.VMEM((n * ctok, HD), bf16),
            pltpu.VMEM((n * ctok, HD), bf16),
            pltpu.VMEM((n, ctok, HD), bf16),
            dma((6,)),
            dma((n + 2,)), dma((n + 2,)), dma((n,)), dma((n,)), dma((n,)), dma((n,)),
        ],
        compiler_params=pltpu.CompilerParams(
            collective_id=1, has_side_effects=True, vmem_limit_bytes=GRANT
        ),
        name="reduce",
    )(dkv.reshape(2, slot_rows, HD), need, ckv, queries, grad_out, gate_comp.T, dq_sel)
    half = jax.ShapeDtypeStruct((HD // 2, 4 * BLK), bf16)
    chalf = jax.ShapeDtypeStruct((ctok, HD // 2), bf16)
    grad_queries, dk, dv, dck, dcv = pl.pallas_call(
        part_kernel,
        in_specs=[vmem] * 3,
        out_specs=[vmem] * 5,
        out_shape=[jax.ShapeDtypeStruct(queries.shape, bf16), half, half, chalf, chalf],
        name="part",
    )(total, ctotal, dq)
    return grad_queries, dk.T, dv.T, dck, dcv


def solution(mesh):
    placed = (
        P("ctx", "tp"),
        P("ctx", None),
        P("ctx", None),
        P("ctx", None),
        P("ctx", None),
        P("ctx", "tp"),
        P("ctx", "tp"),
        P("ctx", "tp"),
        P("ctx", None, None),
    )
    return jax.shard_map(
        local,
        mesh=mesh,
        in_specs=placed,
        out_specs=(P("ctx", "tp"), P("ctx", "tp"), P("ctx", "tp"), P("ctx", "tp"), P("ctx", "tp")),
        check_vma=False,
    )
```

```python
import functools
import math

import jax
import jax.numpy as jnp
from jax import lax
from jax.experimental import pallas as pl
from jax.experimental.pallas import tpu as pltpu
from jax.sharding import PartitionSpec as P

HD = 128
BLK = 128
STRIDE = 16
HEADS_DEV = 8
NEG = -1e30
SCALING = 1.0 / math.sqrt(HD)
LOG2E_SCALING = math.log2(math.e) / math.sqrt(HD)
NN = (((1,), (0,)), ((), ()))
ROWS = 512
COLS = 512
GRANT = 60 * 1024 * 1024
f32 = jnp.float32
bf16 = jnp.bfloat16


def tiles(x, op):
    total = x[:, :HD]
    for t in range(1, x.shape[1] // HD):
        total = op(total, x[:, t * HD : (t + 1) * HD])
    return total


def column_chunks(width):
    return [slice(k0, k0 + COLS) for k0 in range(0, width, COLS)]


class Rows:
    def __init__(self, q, go, kt, vt, masked, s_ref, dp_ref):
        self.q, self.go, self.kt, self.vt, self.masked = q, go, kt, vt, masked
        self.s_ref, self.dp_ref = s_ref, dp_ref
        self.chunks = column_chunks(kt.shape[1])
        self.high = self.total = self.inner = None

    def scores(self, t):
        cols = self.chunks[t]
        s = lax.dot_general(self.q, self.kt[:, cols], NN, preferred_element_type=f32)
        s = self.masked(t, s * LOG2E_SCALING)
        self.s_ref[:, cols] = s
        top = tiles(s, jnp.maximum)
        self.high = top if t == 0 else jnp.maximum(self.high, top)
        if t == len(self.chunks) - 1:
            self.high = jnp.max(self.high, axis=1, keepdims=True)

    def weigh(self, t):
        cols = self.chunks[t]
        dp = lax.dot_general(self.go, self.vt[:, cols], NN, preferred_element_type=f32)
        w = jnp.exp2(self.s_ref[:, cols] - self.high)
        self.s_ref[:, cols] = w
        self.dp_ref[:, cols] = dp
        total, inner = tiles(w, jnp.add), tiles(w * dp, jnp.add)
        self.total = total if t == 0 else self.total + total
        self.inner = inner if t == 0 else self.inner + inner
        if t == len(self.chunks) - 1:
            self.inverse = 1.0 / jnp.sum(self.total, axis=1, keepdims=True)
            self.delta = jnp.sum(self.inner, axis=1, keepdims=True) * self.inverse

    def probs(self, t):
        cols = self.chunks[t]
        p = self.s_ref[:, cols] * self.inverse
        return p.astype(bf16), (p * (self.dp_ref[:, cols] - self.delta)).astype(bf16)


def run_stages(parts, last):
    for k in range(len(parts) + 2):
        for t in range(len(parts[0].chunks)):
            if k < len(parts):
                parts[k].scores(t)
            if 0 <= k - 1 < len(parts):
                parts[k - 1].weigh(t)
            if 0 <= k - 2:
                last(k - 2, t)


def attend_kernel(
    n, nsel, sel, q_ref, go_ref, gs_ref, kv_ref, dq_out, dkv_out,
    acc, ksel, kt, vt, bias, s_ref, dp_ref, qs, gs, qt, gt, masks,
):
    block = pl.program_id(0)
    group = lax.axis_index("tp") // 2

    @pl.when(block == 0)
    def _():
        acc[...] = jnp.zeros_like(acc)
        words = [jnp.int32(0)] * (4 * n // 32)
        for r in range(4):
            for j in range(nsel):
                name = sel[r, group, j]
                bit = jnp.left_shift(jnp.int32(1), name & 31)
                for w in range(len(words)):
                    words[w] = words[w] | jnp.where((name >> 5) == w, bit, 0)
        for w, word in enumerate(words):
            masks[w] = word

    places = [2 * n + block]
    alive = [None]
    for j in range(nsel):
        name = sel[block, group, j]
        live = name >= 0
        safe = jnp.maximum(name, 0)
        before = jnp.right_shift(masks[safe >> 5], safe & 28) & (
            jnp.left_shift(jnp.int32(1), safe & 3) - 1
        )
        second = jnp.where(before != 0, 1, 0)
        places.append(jnp.where(live, 2 * (safe >> 2) + second, 2 * n + block))
        alive.append(live)
    for j, at in enumerate(places):
        cols = slice(j * BLK, (j + 1) * BLK)
        k = kv_ref[0, at]
        ksel[cols, :] = k
        kt[:, cols] = k.T
        vt[:, cols] = kv_ref[1, at].T
        counts = jnp.float32(0.0)
        if j > 0:
            counts = jnp.where(alive[j], 0.0, NEG).astype(f32)
        bias[:, cols] = jnp.full((8, BLK), counts, f32)
    gate = gs_ref[...].T
    for h in range(HEADS_DEV):
        cols = slice(h * HD, (h + 1) * HD)
        rows = slice(h * BLK, (h + 1) * BLK)
        q = q_ref[:, cols]
        qs[rows, :] = q
        qt[:, rows] = q.T
        gated = (go_ref[:, cols].astype(f32) * gate[:, h : h + 1]).astype(bf16)
        gs[rows, :] = gated
        gt[:, rows] = gated.T

    def masked(t, s):
        if t > 0:
            return s + bias[:1, t * COLS : (t + 1) * COLS]
        row = lax.broadcasted_iota(jnp.int32, (s.shape[0], BLK), 0) & (BLK - 1)
        key = lax.broadcasted_iota(jnp.int32, (s.shape[0], BLK), 1)
        own_part = jnp.where(key <= row, s[:, :BLK], NEG)
        return jnp.concatenate([own_part, s[:, BLK:] + bias[:1, BLK:COLS]], axis=1)

    spans = [slice(r, r + ROWS) for r in range(0, HEADS_DEV * BLK, ROWS)]
    parts = [
        Rows(qs[rows, :], gs[rows, :], kt, vt, masked, s_ref.at[rows], dp_ref.at[rows])
        for rows in spans
    ]

    def gradients(r, t):
        rows, cols = spans[r], parts[r].chunks[t]
        probs, dscore = parts[r].probs(t)
        dq = lax.dot_general(dscore, ksel[cols, :], NN, preferred_element_type=f32)
        dq_out[0, rows, :] = dq if t == 0 else dq + dq_out[0, rows, :]
        dk = lax.dot_general(qt[:, rows], dscore, NN, preferred_element_type=f32)
        dv = lax.dot_general(gt[:, rows], probs, NN, preferred_element_type=f32)
        for b in range(COLS // BLK):
            at = places[t * (COLS // BLK) + b]
            acc[0, at] += dk[:, b * BLK : (b + 1) * BLK]
            acc[1, at] += dv[:, b * BLK : (b + 1) * BLK]

    run_stages(parts, gradients)

    @pl.when(block == pl.num_programs(0) - 1)
    def _():
        half = HD // 2

        def finish(i, carry):
            for side in range(2):
                rows = slice(side * half, (side + 1) * half)
                dkv_out[side, i, :half, :] = (acc[0, i, rows, :] * SCALING).astype(bf16)
                dkv_out[side, i, half:, :] = acc[1, i, rows, :].astype(bf16)
            return carry

        lax.fori_loop(0, acc.shape[1], finish, 0)


def attend(selections, queries, grad_out, gates_s, kv):
    n = lax.axis_size("ctx")
    blocks, _, nsel = selections.shape
    keys = (nsel + 1) * BLK
    width = HEADS_DEV * BLK
    whole = lambda shape: pl.BlockSpec(shape, lambda i: (0,) * len(shape))
    rows = pl.BlockSpec((BLK, width), lambda i: (i, 0))
    return pl.pallas_call(
        functools.partial(attend_kernel, n, nsel),
        grid=(blocks,),
        in_specs=[
            pl.BlockSpec(memory_space=pltpu.SMEM), rows, rows,
            pl.BlockSpec((HEADS_DEV, BLK), lambda i: (0, i)), whole(kv.shape),
        ],
        out_specs=[pl.BlockSpec((1, width, HD), lambda i: (i, 0, 0)), whole(kv.shape)],
        out_shape=[
            jax.ShapeDtypeStruct((blocks, width, HD), f32),
            jax.ShapeDtypeStruct(kv.shape, bf16),
        ],
        scratch_shapes=[
            pltpu.VMEM(kv.shape, f32),
            pltpu.VMEM((keys, HD), bf16),
            pltpu.VMEM((HD, keys), bf16),
            pltpu.VMEM((HD, keys), bf16),
            pltpu.VMEM((8, keys), f32),
            pltpu.VMEM((width, keys), f32),
            pltpu.VMEM((width, keys), f32),
            pltpu.VMEM((width, HD), bf16),
            pltpu.VMEM((width, HD), bf16),
            pltpu.VMEM((HD, width), bf16),
            pltpu.VMEM((HD, width), bf16),
            pltpu.SMEM((4 * n // 32,), jnp.int32),
        ],
        compiler_params=pltpu.CompilerParams(
            vmem_limit_bytes=GRANT, dimension_semantics=("arbitrary",)
        ),
        name="attend",
    )(selections, queries, grad_out, gates_s, kv)


MESH = pl.DeviceIdType.MESH


def spots():
    me = lax.axis_index("ctx")
    tp = lax.axis_index("tp")
    return me, tp, lax.rem(tp, 2)


def greet(n, me, tp, core):
    barrier = pltpu.get_barrier_semaphore()
    for d in range(1, n):
        pl.semaphore_signal(
            barrier, inc=1, device_id=(lax.rem(me + d, n), tp), device_id_type=MESH
        )
    pl.semaphore_signal(barrier, inc=1, device_id=(me, tp + 1 - 2 * core), device_id_type=MESH)


def all_here(n):
    pl.semaphore_wait(pltpu.get_barrier_semaphore(), n)


def remote(src, dst, send, recv, ctx, tp):
    return pltpu.make_async_remote_copy(
        src_ref=src, dst_ref=dst, send_sem=send, recv_sem=recv, device_id=(ctx, tp), device_id_type=MESH
    )


class Relays:
    def __init__(self, me, tp, core, turn, sign, buf, arrive, leave):
        self.me, self.tp, self.core, self.turn, self.sign = me, tp, core, turn, sign
        self.buf, self.arrive, self.leave = buf, arrive, leave
        self.x, self.y = me // 4, lax.rem(me, 4)

    def send(self, src, dst, send_sem, recv_sem, ctx, start):
        x, y = ctx // 4, lax.rem(ctx, 4)
        across = (self.x == self.turn[0]) & (x == self.turn[1])
        along = jnp.logical_not(across) & (lax.rem(y + 4 - self.y, 4) == 2) & (self.core == 1)
        direct = remote(src, dst, send_sem, recv_sem, ctx, self.tp)
        if not start:
            direct.wait_send()
            return
        by = jnp.where(across, 4 * self.turn[2] + self.y, 4 * x + lax.rem(self.y + 3, 4))
        slot = jnp.where(across, y, 4 + self.x)

        @pl.when(across | along)
        def _():
            remote(src, self.buf.at[slot], send_sem, self.arrive.at[slot], by, self.tp).start()

        @pl.when(jnp.logical_not(across | along))
        def _():
            direct.start()

    def each(self, fn):
        @pl.when(self.x == self.turn[2])
        def _():
            for y in range(4):
                fn(y, 4 * self.turn[0] + self.y, 4 * self.turn[1] + y)

        source_y, target_y = lax.rem(self.y + 1, 4), lax.rem(self.y + 3, 4)
        for x in range(4):
            source, target = 4 * x + source_y, 4 * self.x + target_y
            turned = (self.x == self.turn[1]) if x == self.turn[0] else False

            @pl.when((self.core == 1) & (self.sign * (target - source) > 0) & jnp.logical_not(turned))
            def _():
                fn(4 + x, source, target)

    def pass_on(self, place, recv_sem):
        def step(slot, source, target):
            copy = remote(
                self.buf.at[slot], self.buf.at[slot], self.leave.at[slot], self.arrive.at[slot],
                target, self.tp,
            )
            copy.wait_recv()
            remote(
                self.buf.at[slot], place(source), self.leave.at[slot], recv_sem.at[source],
                target, self.tp,
            ).start()

        self.each(step)

    def finish(self, place, recv_sem):
        def step(slot, source, target):
            remote(
                self.buf.at[slot], place(source), self.leave.at[slot], recv_sem.at[source],
                target, self.tp,
            ).wait_send()

        self.each(step)


def gather_kernel(
    n, sel, keys, values, ckeys, cvalues, kv, ckv, need_out,
    own, owned, ownf, want, need_in, pack, passing,
    in_sem, keep_sem, ns, nr, cs, cr, ks, kr, fs, fr, arrive, leave,
):
    me, tp, core = spots()
    group = tp // 2
    partner = tp + 1 - 2 * core
    cols = pl.ds(pl.multiple_of(group * HD, HD), HD)
    loads = [
        pltpu.make_async_copy(ckeys.at[:, cols], owned.at[0], in_sem.at[0]),
        pltpu.make_async_copy(cvalues.at[:, cols], owned.at[1], in_sem.at[1]),
        pltpu.make_async_copy(keys.at[:, cols], own.at[0], in_sem.at[2]),
        pltpu.make_async_copy(values.at[:, cols], own.at[1], in_sem.at[3]),
    ]
    greet(n, me, tp, core)
    for load in loads:
        load.start()
    row = lax.broadcasted_iota(jnp.int32, (8 * n, HD), 0)
    quarter = lax.rem(row, 4)
    ident = 4 * (row // 8) + quarter
    used = jnp.zeros((8 * n, HD), f32)
    for r in range(4):
        for j in range(sel.shape[2]):
            used = jnp.where(ident == sel[r, group, j], 1.0, used)
    ahead = jnp.zeros_like(used)
    for k in range(1, 4):
        ahead = ahead + jnp.where(quarter >= k, pltpu.roll(used, k, 0), 0.0)
    place = lax.rem(row // 4, 2).astype(f32)
    want[...] = jnp.where(ahead == place, used, 0.0)
    ctok = ckeys.shape[0]
    crows = pl.ds(pl.multiple_of(me * ctok, ctok), ctok)

    def slots(i):
        return pl.ds(pl.multiple_of(i * 2 * BLK, 2 * BLK), 2 * BLK)

    def send_need(i):
        rows = pl.ds(pl.multiple_of(i * 8, 8), 8)
        return remote(want.at[rows, :], need_in.at[me], ns.at[i], nr.at[me], i, tp)

    def send_comp(j):
        return remote(owned, ckv.at[:, crows, :], cs.at[j], cr.at[me], j, tp)

    relays = Relays(me, tp, core, (0, 2, 3), 1, passing, arrive, leave)

    def place(i):
        return kv.at[core, slots(i), :]

    def send_kv(j, start):
        relays.send(pack.at[j], place(me), ks.at[j], kr.at[me], j, start)

    def forward(i):
        return remote(
            kv.at[core, slots(i), :], kv.at[core, slots(i), :], fs.at[i], fr.at[i], me, partner
        )

    def need_from(j):
        return remote(want.at[pl.ds(0, 8), :], need_in.at[j], ns.at[j], nr.at[j], j, tp)

    def comp_from(j):
        rows = pl.ds(pl.multiple_of(j * ctok, ctok), ctok)
        return remote(owned, ckv.at[:, rows, :], cs.at[j], cr.at[j], j, tp)

    def kv_from(i):
        return remote(pack.at[i], kv.at[core, slots(i), :], ks.at[i], kr.at[i], i, tp)

    def forwarded(i):
        return remote(
            kv.at[core, slots(i), :], kv.at[1 - core, slots(i), :], fs.at[i], fr.at[i], me, partner
        )

    def down(fn):
        def step(k, carry):
            fn(me - 1 - k)
            return carry

        lax.fori_loop(0, me, step, 0)

    def up(fn):
        def step(j, carry):
            fn(j)
            return carry

        lax.fori_loop(me + 1, n, step, 0)

    all_here(n)
    down(lambda i: send_need(i).start())
    for load in loads:
        load.wait()
    keep = [
        pltpu.make_async_copy(own, kv.at[:, pl.ds(2 * n * BLK, 4 * BLK), :], keep_sem.at[0]),
        pltpu.make_async_copy(owned, ckv.at[:, crows, :], keep_sem.at[1]),
    ]
    for copy in keep:
        copy.start()

    ownf[...] = own[core].astype(f32)

    def pack_and_send(j):
        need_from(j).wait_recv()
        mask = need_in[j]
        for s in range(2):
            total = mask[4 * s : 4 * s + 1] * ownf[:BLK, :]
            for b in range(1, 4):
                total = total + mask[4 * s + b : 4 * s + b + 1] * ownf[b * BLK : (b + 1) * BLK, :]
            pack[j, s * BLK : (s + 1) * BLK, :] = total.astype(bf16)
        need_out[j] = mask
        send_kv(j, True)

    up(pack_and_send)
    relays.pass_on(place, kr)
    up(lambda j: send_comp(j).start())

    def pass_on(i):
        kv_from(i).wait_recv()
        forward(i).start()

    down(pass_on)
    down(lambda i: forwarded(i).wait_recv())
    down(lambda j: comp_from(j).wait_recv())
    down(lambda i: send_need(i).wait_send())
    up(lambda j: send_kv(j, False))
    relays.finish(place, kr)
    down(lambda i: forward(i).wait_send())
    up(lambda j: send_comp(j).wait_send())
    for copy in keep:
        copy.wait()


def reduce_kernel(
    n, dkv, need, ckv, queries, grads, gc_ref, dq_sel, total_out, ctotal_out, dq_out,
    mine, mown, xin, xown, pack, recv, acc, ckv_in, ckt, cvt, q_all, go_all, s_ref, dp_ref, bias,
    dq_all, cacc, dckv, xcomp, cpack, crecv, passing,
    in_sem, xs, xr, ss, sr, cs, cr, arrive, leave,
):
    me, tp, core = spots()
    greet(n, me, tp, core)
    partner = tp + 1 - 2 * core
    ctok = ckv.shape[1] // n
    base = 2 * n * BLK
    pair = 2 * BLK
    half = HD // 2

    def slots(i):
        return pl.ds(pl.multiple_of(i * pair, pair), pair)

    def comp_rows(i):
        return pl.ds(pl.multiple_of(i * ctok, ctok), ctok)

    loads = [
        pltpu.make_async_copy(dkv.at[core, pl.ds(0, base), :], mine, in_sem.at[0]),
        pltpu.make_async_copy(dkv.at[core, pl.ds(base, 4 * BLK), :], mown, in_sem.at[1]),
    ]
    late = [
        pltpu.make_async_copy(ckv, ckv_in, in_sem.at[2]),
        pltpu.make_async_copy(queries, q_all, in_sem.at[3]),
        pltpu.make_async_copy(grads, go_all, in_sem.at[4]),
        pltpu.make_async_copy(dq_sel, dq_all, in_sem.at[5]),
    ]
    for load in loads:
        load.start()
    all_here(n)

    def below(fn):
        def step(i, carry):
            fn(i)
            return carry

        lax.fori_loop(0, me, step, 0)

    swap_comp = remote(dckv.at[1 - core], xcomp, xs.at[n], xr.at[n], me, partner)
    swap_own = remote(
        dkv.at[1 - core, pl.ds(base, 4 * BLK), :], xown, xs.at[n + 1], xr.at[n + 1], me, partner
    )

    def swap(i):
        return remote(dkv.at[1 - core, slots(i), :], xin.at[i], xs.at[i], xr.at[i], me, partner)

    relays = Relays(me, tp, core, (3, 1, 2), -1, passing, arrive, leave)

    def place(j):
        return recv.at[j]

    def send(i, start):
        relays.send(pack.at[i], place(me), ss.at[i], sr.at[me], i, start)

    def came(j):
        return remote(pack.at[j], recv.at[j], ss.at[j], sr.at[j], j, tp)

    def send_comp(i):
        return remote(cpack.at[comp_rows(i), :], crecv.at[me], cs.at[i], cr.at[me], i, tp)

    def comp_came(j):
        return remote(cpack.at[comp_rows(j), :], crecv.at[j], cs.at[j], cr.at[j], j, tp)

    below(lambda i: swap(i).start())
    swap_own.start()
    for load in late:
        load.start()
    for load in loads:
        load.wait()

    def add_and_send(i):
        swap(i).wait_recv()
        pack[i] = (mine[slots(i), :].astype(f32) + xin[i].astype(f32)).astype(bf16)
        send(i, True)

    below(add_and_send)
    gate = gc_ref[...].T
    cacc[...] = jnp.zeros_like(cacc)
    for load in late:
        load.wait()
    came_rows = lax.broadcasted_iota(jnp.int32, (n * ctok, HD), 0) < (me + 1) * ctok
    for side in range(2):
        ckv_in[side] = jnp.where(came_rows, ckv_in[side].astype(f32), 0.0).astype(bf16)
    ckt[...] = ckv_in[0].T
    cvt[...] = ckv_in[1].T

    def compressed(block):
        tokens = slice(block * BLK, (block + 1) * BLK)
        start = (me * 4 + block) * BLK

        row = lax.broadcasted_iota(jnp.int32, (BLK, ckt.shape[1]), 0)
        key = lax.broadcasted_iota(jnp.int32, (BLK, ckt.shape[1]), 1) * STRIDE
        bias[...] = jnp.where(key - row <= start, 0.0, NEG)

        def before(t, s):
            part = bias[:, t * COLS : (t + 1) * COLS]
            return s + jnp.concatenate([part] * (ROWS // BLK), axis=0)

        spans = [slice(r, r + ROWS) for r in range(0, HEADS_DEV * BLK, ROWS)]
        parts, sides = [], []
        for rows in spans:
            heads = range(rows.start // BLK, rows.stop // BLK)
            q = jnp.concatenate([q_all[tokens, h * HD : (h + 1) * HD] for h in heads], axis=0)
            go = jnp.concatenate(
                [
                    (go_all[tokens, h * HD : (h + 1) * HD].astype(f32) * gate[tokens, h : h + 1]).astype(bf16)
                    for h in heads
                ],
                axis=0,
            )
            parts.append(Rows(q, go, ckt, cvt, before, s_ref.at[rows], dp_ref.at[rows]))
            sides.append((q.T, go.T))

        def gradients(r, t):
            probs, dscore = parts[r].probs(t)
            cols = parts[r].chunks[t]
            dq_all[block, spans[r], :] += lax.dot_general(
                dscore, ckv_in[0, cols, :], NN, preferred_element_type=f32
            )
            cacc[0, :, cols] += lax.dot_general(sides[r][0], dscore, NN, preferred_element_type=f32)
            cacc[1, :, cols] += lax.dot_general(sides[r][1], probs, NN, preferred_element_type=f32)

        run_stages(parts, gradients)

        for h in range(HEADS_DEV):
            dq_out[tokens, h * HD : (h + 1) * HD] = (
                dq_all[block, h * BLK : (h + 1) * BLK, :] * SCALING
            ).astype(bf16)

    compressed(0)
    relays.pass_on(place, sr)
    for block in range(1, 4):
        compressed(block)
    for side in range(2):
        rows = slice(side * half, (side + 1) * half)
        joined = jnp.concatenate([cacc[0, rows, :] * SCALING, cacc[1, rows, :]], axis=0)
        dckv[side] = joined.T.astype(bf16)
    swap_comp.start()
    swap_own.wait_recv()
    acc[...] = mown[...].astype(f32) + xown[...].astype(f32)
    swap_comp.wait_recv()
    cpack[...] = (dckv[core].astype(f32) + xcomp[...].astype(f32)).astype(bf16)
    below(lambda i: send_comp(i).start())

    def take(k, carry):
        j = n - 1 - k
        came(j).wait_recv()
        mask = need[j]
        part = recv[j].astype(f32)
        for b in range(4):
            acc[b * BLK : (b + 1) * BLK, :] += (
                mask[b : b + 1] * part[:BLK] + mask[4 + b : 5 + b] * part[BLK:]
            )
        return carry

    lax.fori_loop(0, n - 1 - me, take, 0)
    for b in range(4):
        total_out[:, b * BLK : (b + 1) * BLK] = acc[b * BLK : (b + 1) * BLK, :].astype(bf16)

    def ctake(k, ctotal):
        j = n - 1 - k
        comp_came(j).wait_recv()
        return ctotal + crecv[j].astype(f32)

    ctotal_out[...] = lax.fori_loop(0, n - 1 - me, ctake, cpack[comp_rows(me), :].astype(f32))
    below(lambda i: swap(i).wait_send())
    swap_comp.wait_send()
    swap_own.wait_send()
    below(lambda i: send(i, False))
    relays.finish(place, sr)
    below(lambda i: send_comp(i).wait_send())


def part_kernel(total, ctotal, dq, dq_out, dk_out, dv_out, dck_out, dcv_out):
    half = HD // 2
    dq_out[...] = dq[...]
    dk_out[...] = total[:half, :]
    dv_out[...] = total[half:, :]
    both = ctotal[...]
    dck_out[...] = both[:, :half].astype(bf16)
    dcv_out[...] = both[:, half:].astype(bf16)


def local(queries, keys, values, comp_keys, comp_values, gate_comp, gate_sel, grad_out, selections):
    n = lax.axis_size("ctx")
    ctok = comp_keys.shape[0]
    anywhere = pl.BlockSpec(memory_space=pl.ANY)
    scalars = pl.BlockSpec(memory_space=pltpu.SMEM)
    vmem = pl.BlockSpec(memory_space=pltpu.VMEM)
    dma = pltpu.SemaphoreType.DMA
    slot_rows = (2 * n + 4) * BLK
    width = HEADS_DEV * BLK
    kv, ckv, need = pl.pallas_call(
        functools.partial(gather_kernel, n),
        in_specs=[scalars] + [anywhere] * 4,
        out_specs=[anywhere, anywhere, vmem],
        out_shape=[
            jax.ShapeDtypeStruct((2, slot_rows, HD), bf16),
            jax.ShapeDtypeStruct((2, n * ctok, HD), bf16),
            jax.ShapeDtypeStruct((n, 8, HD), f32),
        ],
        scratch_shapes=[
            pltpu.VMEM((2, 4 * BLK, HD), bf16),
            pltpu.VMEM((2, ctok, HD), bf16),
            pltpu.VMEM((4 * BLK, HD), f32),
            pltpu.VMEM((8 * n, HD), f32),
            pltpu.VMEM((n, 8, HD), f32),
            pltpu.VMEM((n, 2 * BLK, HD), bf16),
            pltpu.VMEM((8, 2 * BLK, HD), bf16),
            dma((4,)), dma((2,)),
            dma((n,)), dma((n,)), dma((n,)), dma((n,)),
            dma((n,)), dma((n,)), dma((n,)), dma((n,)), dma((8,)), dma((8,)),
        ],
        compiler_params=pltpu.CompilerParams(
            collective_id=0, has_side_effects=True, vmem_limit_bytes=GRANT
        ),
        name="gather",
    )(selections, keys, values, comp_keys, comp_values)
    dq_sel, dkv = attend(
        selections, queries, grad_out, gate_sel.T, kv.reshape(2, 2 * n + 4, BLK, HD)
    )
    total, ctotal, dq = pl.pallas_call(
        functools.partial(reduce_kernel, n),
        in_specs=[anywhere, vmem, anywhere, anywhere, anywhere, vmem, anywhere],
        out_specs=[vmem] * 3,
        out_shape=[
            jax.ShapeDtypeStruct((HD, 4 * BLK), bf16),
            jax.ShapeDtypeStruct((ctok, HD), f32),
            jax.ShapeDtypeStruct(queries.shape, bf16),
        ],
        scratch_shapes=[
            pltpu.VMEM((2 * n * BLK, HD), bf16),
            pltpu.VMEM((4 * BLK, HD), bf16),
            pltpu.VMEM((n, 2 * BLK, HD), bf16),
            pltpu.VMEM((4 * BLK, HD), bf16),
            pltpu.VMEM((n, 2 * BLK, HD), bf16),
            pltpu.VMEM((n, 2 * BLK, HD), bf16),
            pltpu.VMEM((4 * BLK, HD), f32),
            pltpu.VMEM((2, n * ctok, HD), bf16),
            pltpu.VMEM((HD, n * ctok), bf16),
            pltpu.VMEM((HD, n * ctok), bf16),
            pltpu.VMEM(queries.shape, bf16),
            pltpu.VMEM(queries.shape, bf16),
            pltpu.VMEM((width, n * ctok), f32),
            pltpu.VMEM((width, n * ctok), f32),
            pltpu.VMEM((BLK, n * ctok), f32),
            pltpu.VMEM((4, width, HD), f32),
            pltpu.VMEM((2, HD, n * ctok), f32),
            pltpu.VMEM((2, n * ctok, HD), bf16),
            pltpu.VMEM((n * ctok, HD), bf16),
            pltpu.VMEM((n * ctok, HD), bf16),
            pltpu.VMEM((n, ctok, HD), bf16),
            pltpu.VMEM((8, 2 * BLK, HD), bf16),
            dma((6,)),
            dma((n + 2,)), dma((n + 2,)), dma((n,)), dma((n,)), dma((n,)), dma((n,)),
            dma((8,)), dma((8,)),
        ],
        compiler_params=pltpu.CompilerParams(
            collective_id=1, has_side_effects=True, vmem_limit_bytes=GRANT
        ),
        name="reduce",
    )(dkv.reshape(2, slot_rows, HD), need, ckv, queries, grad_out, gate_comp.T, dq_sel)
    half = jax.ShapeDtypeStruct((HD // 2, 4 * BLK), bf16)
    chalf = jax.ShapeDtypeStruct((ctok, HD // 2), bf16)
    grad_queries, dk, dv, dck, dcv = pl.pallas_call(
        part_kernel,
        in_specs=[vmem] * 3,
        out_specs=[vmem] * 5,
        out_shape=[jax.ShapeDtypeStruct(queries.shape, bf16), half, half, chalf, chalf],
        name="part",
    )(total, ctotal, dq)
    return grad_queries, dk.T, dv.T, dck, dcv


def solution(mesh):
    placed = (
        P("ctx", "tp"),
        P("ctx", None),
        P("ctx", None),
        P("ctx", None),
        P("ctx", None),
        P("ctx", "tp"),
        P("ctx", "tp"),
        P("ctx", "tp"),
        P("ctx", None, None),
    )
    return jax.shard_map(
        local,
        mesh=mesh,
        in_specs=placed,
        out_specs=(P("ctx", "tp"), P("ctx", "tp"), P("ctx", "tp"), P("ctx", "tp"), P("ctx", "tp")),
        check_vma=False,
    )
```

```python
import functools
import math

import jax
import jax.numpy as jnp
from jax import lax
from jax.experimental import pallas as pl
from jax.experimental.pallas import tpu as pltpu
from jax.sharding import PartitionSpec as P

HD = 128
BLK = 128
STRIDE = 16
HEADS_DEV = 8
NEG = -1e30
SCALING = 1.0 / math.sqrt(HD)
LOG2E_SCALING = math.log2(math.e) / math.sqrt(HD)
NN = (((1,), (0,)), ((), ()))
ROWS = 256
COLS = 512
GRANT = 60 * 1024 * 1024
f32 = jnp.float32
bf16 = jnp.bfloat16


def tiles(x, op):
    total = x[:, :HD]
    for t in range(1, x.shape[1] // HD):
        total = op(total, x[:, t * HD : (t + 1) * HD])
    return total


def column_chunks(width):
    return [slice(k0, k0 + COLS) for k0 in range(0, width, COLS)]


def weights(q, go, kt, vt, masked, s_ref, dp_ref):
    chunks = column_chunks(kt.shape[1])
    high = None
    for t, cols in enumerate(chunks):
        s = masked(t, lax.dot_general(q, kt[:, cols], NN, preferred_element_type=f32))
        s_ref[:, cols] = s
        top = tiles(s, jnp.maximum)
        high = top if high is None else jnp.maximum(high, top)
    high = jnp.max(high, axis=1, keepdims=True)
    total = inner = 0.0
    for cols in chunks:
        dp = lax.dot_general(go, vt[:, cols], NN, preferred_element_type=f32)
        w = jnp.exp2((s_ref[:, cols] - high) * LOG2E_SCALING)
        s_ref[:, cols] = w
        dp_ref[:, cols] = dp
        total = total + tiles(w, jnp.add)
        inner = inner + tiles(w * dp, jnp.add)
    inverse = 1.0 / jnp.sum(total, axis=1, keepdims=True)
    return inverse, jnp.sum(inner, axis=1, keepdims=True) * inverse


def branch(q, go, qt, got, kt, vt, keys, masked, s_ref, dp_ref, dk_ref, dv_ref):
    inverse, delta = weights(q, go, kt, vt, masked, s_ref, dp_ref)
    dq = 0.0
    for cols in column_chunks(kt.shape[1]):
        probs = s_ref[:, cols] * inverse
        dscore = (probs * (dp_ref[:, cols] - delta)).astype(bf16)
        dq = dq + lax.dot_general(dscore, keys[cols, :], NN, preferred_element_type=f32)
        dk_ref[:, cols] += lax.dot_general(qt, dscore, NN, preferred_element_type=f32)
        dv_ref[:, cols] += lax.dot_general(got, probs.astype(bf16), NN, preferred_element_type=f32)
    return dq


def attend_kernel(
    n, nsel, sel, q_ref, go_ref, gs_ref, kv_ref, dv_out, ds_out, where, source,
    acc, kt, vt, bias, s_ref, dp_ref, qs, gs, gt, masks,
):
    block = pl.program_id(0)
    group = lax.axis_index("tp") // 2
    own = 2 * n + block

    @pl.when(block == 0)
    def _():
        acc[...] = jnp.zeros_like(acc)
        words = [jnp.int32(0)] * (4 * n // 32)
        for r in range(4):
            for j in range(nsel):
                name = sel[r, group, j]
                bit = jnp.left_shift(jnp.int32(1), name & 31)
                for w in range(len(words)):
                    words[w] = words[w] | jnp.where((name >> 5) == w, bit, 0)
        for w, word in enumerate(words):
            masks[w] = word

    places, alive = [own], [None]
    where[block, 0] = own
    for i in range(2 * n):
        source[block, i] = nsel + 1
    for j in range(nsel):
        name = sel[block, group, j]
        live = name >= 0
        safe = jnp.maximum(name, 0)
        before = jnp.right_shift(masks[safe >> 5], safe & 28) & (
            jnp.left_shift(jnp.int32(1), safe & 3) - 1
        )
        at = 2 * (safe >> 2) + jnp.where(before != 0, 1, 0)
        places.append(jnp.where(live, at, own))
        alive.append(live)
        where[block, j + 1] = places[-1]
        source[block, jnp.where(live, at, 2 * n)] = j + 1
    for j, at in enumerate(places):
        cols = slice(j * BLK, (j + 1) * BLK)
        kt[:, cols] = kv_ref[0, at].T
        vt[:, cols] = kv_ref[1, at].T
        counts = jnp.float32(0.0)
        if j > 0:
            counts = jnp.where(alive[j], 0.0, NEG).astype(f32)
        bias[:, cols] = jnp.full((8, BLK), counts, f32)
    gate = gs_ref[...].T
    for h in range(HEADS_DEV):
        cols = slice(h * HD, (h + 1) * HD)
        rows = slice(h * BLK, (h + 1) * BLK)
        qs[rows, :] = q_ref[:, cols]
        gated = (go_ref[:, cols].astype(f32) * gate[:, h : h + 1]).astype(bf16)
        gs[rows, :] = gated
        gt[:, rows] = gated.T

    def masked(t, s):
        if t > 0:
            return s + bias[:1, t * COLS : (t + 1) * COLS]
        row = lax.broadcasted_iota(jnp.int32, (s.shape[0], BLK), 0) & (BLK - 1)
        key = lax.broadcasted_iota(jnp.int32, (s.shape[0], BLK), 1)
        own_part = jnp.where(key <= row, s[:, :BLK], NEG)
        return jnp.concatenate([own_part, s[:, BLK:] + bias[:1, BLK:COLS]], axis=1)

    inverse, delta = weights(qs[...], gs[...], kt, vt, masked, s_ref, dp_ref)
    for t, cols in enumerate(column_chunks(kt.shape[1])):
        probs = s_ref[:, cols] * inverse
        ds_out[0, :, cols] = (probs * (dp_ref[:, cols] - delta)).astype(bf16)
        dv = lax.dot_general(gt[...], probs.astype(bf16), NN, preferred_element_type=f32)
        for b in range(COLS // BLK):
            at = places[t * (COLS // BLK) + b]
            acc[at] += dv[:, b * BLK : (b + 1) * BLK]

    @pl.when(block == pl.num_programs(0) - 1)
    def _():
        half = HD // 2

        def finish(i, carry):
            for side in range(2):
                dv_out[side, i] = acc[i, side * half : (side + 1) * half, :].astype(bf16)
            return carry

        lax.fori_loop(0, acc.shape[0], finish, 0)


def attend(selections, queries, grad_out, gates_s, kv):
    n = lax.axis_size("ctx")
    blocks, _, nsel = selections.shape
    keys = (nsel + 1) * BLK
    width = HEADS_DEV * BLK
    whole = lambda shape: pl.BlockSpec(shape, lambda i: (0,) * len(shape))
    scalars = pl.BlockSpec(memory_space=pltpu.SMEM)
    rows = pl.BlockSpec((BLK, width), lambda i: (i, 0))
    half = (2, kv.shape[1], HD // 2, BLK)
    return pl.pallas_call(
        functools.partial(attend_kernel, n, nsel),
        grid=(blocks,),
        in_specs=[
            scalars, rows, rows, pl.BlockSpec((HEADS_DEV, BLK), lambda i: (0, i)), whole(kv.shape),
        ],
        out_specs=[
            whole(half), pl.BlockSpec((1, width, keys), lambda i: (i, 0, 0)), scalars, scalars,
        ],
        out_shape=[
            jax.ShapeDtypeStruct(half, bf16),
            jax.ShapeDtypeStruct((blocks, width, keys), bf16),
            jax.ShapeDtypeStruct((blocks, nsel + 1), jnp.int32),
            jax.ShapeDtypeStruct((blocks, 2 * n + 1), jnp.int32),
        ],
        scratch_shapes=[
            pltpu.VMEM((kv.shape[1], HD, BLK), f32),
            pltpu.VMEM((HD, keys), bf16),
            pltpu.VMEM((HD, keys), bf16),
            pltpu.VMEM((8, keys), f32),
            pltpu.VMEM((width, keys), f32),
            pltpu.VMEM((width, keys), f32),
            pltpu.VMEM((width, HD), bf16),
            pltpu.VMEM((width, HD), bf16),
            pltpu.VMEM((HD, width), bf16),
            pltpu.SMEM((4 * n // 32,), jnp.int32),
        ],
        compiler_params=pltpu.CompilerParams(
            vmem_limit_bytes=GRANT, dimension_semantics=("arbitrary",)
        ),
        name="attend",
    )(selections, queries, grad_out, gates_s, kv)


MESH = pl.DeviceIdType.MESH


def spots():
    me = lax.axis_index("ctx")
    tp = lax.axis_index("tp")
    return me, tp, lax.rem(tp, 2)


def enter(n, me, tp, core):
    barrier = pltpu.get_barrier_semaphore()
    for d in range(1, n):
        pl.semaphore_signal(
            barrier, inc=1, device_id=(lax.rem(me + d, n), tp), device_id_type=MESH
        )
    pl.semaphore_signal(barrier, inc=1, device_id=(me, tp + 1 - 2 * core), device_id_type=MESH)
    pl.semaphore_wait(barrier, n)


def remote(src, dst, send, recv, ctx, tp):
    return pltpu.make_async_remote_copy(
        src_ref=src, dst_ref=dst, send_sem=send, recv_sem=recv, device_id=(ctx, tp), device_id_type=MESH
    )


def toward(me, sign, fn):
    def step(k, carry):
        x = me // 4 + sign * lax.rem(k, 4)
        ctx = 4 * x + lax.rem(lax.rem(me, 4) + k // 4, 4)

        @pl.when((x >= 0) & (x < 4) & (sign * (ctx - me) > 0))
        def _():
            fn(ctx)

        return carry

    lax.fori_loop(1, 16, step, 0)


def arrived(me, sign, fn):
    def step(k, carry):
        x = me // 4 - sign * lax.rem(k, 4)
        ctx = 4 * x + lax.rem(lax.rem(me, 4) + 4 - k // 4, 4)

        @pl.when((x >= 0) & (x < 4) & (sign * (me - ctx) > 0))
        def _():
            fn(ctx)

        return carry

    lax.fori_loop(1, 16, step, 0)


def gather_kernel(
    n, sel, keys, values, ckeys, cvalues, queries, grads, gc_ref, kv, need_out, dqc, dckv,
    own, owned, ownf, want, need_in, pack, ckv, q_all, go_all, ckt, cvt, s_ref, dp_ref, dqc_all, cacc,
    in_sem, keep_sem, dq_sem, ns, nr, cs, cr, ks, kr, fs, fr,
):
    me, tp, core = spots()
    group = tp // 2
    partner = tp + 1 - 2 * core
    cols = pl.ds(pl.multiple_of(group * HD, HD), HD)
    loads = [
        pltpu.make_async_copy(ckeys.at[:, cols], owned.at[0], in_sem.at[0]),
        pltpu.make_async_copy(cvalues.at[:, cols], owned.at[1], in_sem.at[1]),
        pltpu.make_async_copy(keys.at[:, cols], own.at[0], in_sem.at[2]),
        pltpu.make_async_copy(values.at[:, cols], own.at[1], in_sem.at[3]),
    ]
    late = [
        pltpu.make_async_copy(queries, q_all, in_sem.at[4]),
        pltpu.make_async_copy(grads, go_all, in_sem.at[5]),
    ]
    for load in loads + late:
        load.start()
    row = lax.broadcasted_iota(jnp.int32, (8 * n, HD), 0)
    quarter = lax.rem(row, 4)
    ident = 4 * (row // 8) + quarter
    used = jnp.zeros((8 * n, HD), f32)
    for r in range(4):
        for j in range(sel.shape[2]):
            used = jnp.where(ident == sel[r, group, j], 1.0, used)
    ahead = jnp.zeros_like(used)
    for k in range(1, 4):
        ahead = ahead + jnp.where(quarter >= k, pltpu.roll(used, k, 0), 0.0)
    place = lax.rem(row // 4, 2).astype(f32)
    want[...] = jnp.where(ahead == place, used, 0.0)
    for load in loads:
        load.wait()
    enter(n, me, tp, core)
    ctok = ckeys.shape[0]
    crows = pl.ds(pl.multiple_of(me * ctok, ctok), ctok)
    my_slots = pl.ds(pl.multiple_of(me * 2 * BLK, 2 * BLK), 2 * BLK)

    def slots(i):
        return pl.ds(pl.multiple_of(i * 2 * BLK, 2 * BLK), 2 * BLK)

    def send_need(i):
        rows = pl.ds(pl.multiple_of(i * 8, 8), 8)
        return remote(want.at[rows, :], need_in.at[me], ns.at[i], nr.at[me], i, tp)

    def send_comp(j):
        return remote(owned, ckv.at[:, crows, :], cs.at[j], cr.at[me], j, tp)

    def send_kv(j):
        return remote(pack.at[j], kv.at[core, my_slots, :], ks.at[j], kr.at[me], j, tp)

    def forward(i):
        return remote(
            kv.at[core, slots(i), :], kv.at[core, slots(i), :], fs.at[i], fr.at[i], me, partner
        )

    def need_from(j):
        return remote(want.at[pl.ds(0, 8), :], need_in.at[j], ns.at[j], nr.at[j], j, tp)

    def comp_from(j):
        rows = pl.ds(pl.multiple_of(j * ctok, ctok), ctok)
        return remote(owned, ckv.at[:, rows, :], cs.at[j], cr.at[j], j, tp)

    def kv_from(i):
        return remote(pack.at[i], kv.at[core, slots(i), :], ks.at[i], kr.at[i], i, tp)

    def forwarded(i):
        return remote(
            kv.at[core, slots(i), :], kv.at[1 - core, slots(i), :], fs.at[i], fr.at[i], me, partner
        )

    def down(fn):
        def step(k, carry):
            fn(me - 1 - k)
            return carry

        lax.fori_loop(0, me, step, 0)

    def up(fn):
        def step(j, carry):
            fn(j)
            return carry

        lax.fori_loop(me + 1, n, step, 0)

    down(lambda i: send_need(i).start())
    keep = [
        pltpu.make_async_copy(own, kv.at[:, pl.ds(2 * n * BLK, 4 * BLK), :], keep_sem.at[0]),
        pltpu.make_async_copy(owned, ckv.at[:, crows, :], keep_sem.at[1]),
    ]
    for copy in keep:
        copy.start()

    def others(fn):
        def step(d, carry):
            fn(lax.rem(me + d, n))
            return carry

        lax.fori_loop(1, n, step, 0)

    others(lambda j: send_comp(j).start())
    ownf[...] = own[core].astype(f32)

    def pack_and_send(j):
        need_from(j).wait_recv()
        mask = need_in[j]
        for s in range(2):
            total = mask[4 * s : 4 * s + 1] * ownf[:BLK, :]
            for b in range(1, 4):
                total = total + mask[4 * s + b : 4 * s + b + 1] * ownf[b * BLK : (b + 1) * BLK, :]
            pack[j, s * BLK : (s + 1) * BLK, :] = total.astype(bf16)
        need_out[j] = mask
        send_kv(j).start()

    toward(me, 1, pack_and_send)

    cacc[...] = jnp.zeros_like(cacc)
    for load in late:
        load.wait()
    others(lambda j: comp_from(j).wait_recv())
    keep[1].wait()
    ckt[...] = ckv[0].T
    cvt[...] = ckv[1].T
    gate = gc_ref[...].T

    def compressed(block):
        tokens = slice(block * BLK, (block + 1) * BLK)
        start = (me * 4 + block) * BLK

        def before(t, s):
            row = lax.broadcasted_iota(jnp.int32, s.shape, 0) & (BLK - 1)
            key = lax.broadcasted_iota(jnp.int32, s.shape, 1) * STRIDE + t * (COLS * STRIDE)
            return jnp.where(key - row <= start, s, NEG)

        for r in range(HEADS_DEV * BLK // ROWS):
            parts = range(r * ROWS // BLK, (r + 1) * ROWS // BLK)
            q = jnp.concatenate([q_all[tokens, h * HD : (h + 1) * HD] for h in parts], axis=0)
            go = jnp.concatenate(
                [
                    (go_all[tokens, h * HD : (h + 1) * HD].astype(f32) * gate[tokens, h : h + 1]).astype(bf16)
                    for h in parts
                ],
                axis=0,
            )
            dqc_all[block, r * ROWS : (r + 1) * ROWS, :] = branch(
                q, go, q.T, go.T, ckt, cvt, ckv.at[0], before,
                s_ref, dp_ref, cacc.at[0], cacc.at[1],
            )

    def save(block):
        return pltpu.make_async_copy(dqc_all.at[block], dqc.at[block], dq_sem.at[block])

    def pass_on(i):
        kv_from(i).wait_recv()
        forward(i).start()

    for block in range(3):
        compressed(block)
        save(block).start()
    arrived(me, 1, pass_on)
    compressed(3)
    save(3).start()
    half = HD // 2
    for side in range(2):
        rows = slice(side * half, (side + 1) * half)
        joined = jnp.concatenate([cacc[0, rows, :] * SCALING, cacc[1, rows, :]], axis=0)
        dckv[side] = joined.T.astype(bf16)
    down(lambda i: forwarded(i).wait_recv())
    down(lambda i: send_need(i).wait_send())
    up(lambda j: send_kv(j).wait_send())
    down(lambda i: forward(i).wait_send())
    others(lambda j: send_comp(j).wait_send())
    keep[0].wait()
    for block in range(4):
        save(block).wait()


def reduce_kernel(
    n, dv, ds, dckv, need, queries, kv, dqc, where, source, total_out, ctotal_out, dq_out,
    ds_all, dks, mine, mcomp, xin, xown, xcomp, pack, recv, kmine, kgive, kin, kown_give, kown_in,
    kpack, krecv, acc, q_all, qt, kbuf, ksel, dqc_all,
    in_sem, ds_sem, xs, xr, ss, sr, ks, kr, ts, tr,
):
    me, tp, core = spots()
    partner = tp + 1 - 2 * core
    ctok = dckv.shape[1] // n
    half = HD // 2
    blocks, nkeys = ds.shape[0], ds.shape[2]
    per = nkeys // BLK
    own = pl.ds(2 * n, 4)

    def slots(i):
        return pl.ds(i * 2, 2)

    def comp_rows(i):
        return pl.ds(pl.multiple_of(i * ctok, ctok), ctok)

    loads = [
        pltpu.make_async_copy(queries, q_all, in_sem.at[0]),
        pltpu.make_async_copy(dckv.at[core], mcomp, in_sem.at[1]),
        pltpu.make_async_copy(dv.at[core], mine, in_sem.at[2]),
        pltpu.make_async_copy(kv.at[0], kbuf, in_sem.at[3]),
        pltpu.make_async_copy(dqc, dqc_all, in_sem.at[4]),
    ]
    ds_loads = [
        pltpu.make_async_copy(ds.at[b], ds_all.at[b], ds_sem.at[b]) for b in range(blocks)
    ]
    loads[0].start()
    ds_loads[0].start()
    for load in loads[1:] + ds_loads[1:]:
        load.start()
    enter(n, me, tp, core)

    def below(fn):
        def step(i, carry):
            fn(i)
            return carry

        lax.fori_loop(0, me, step, 0)

    swap_comp = remote(dckv.at[1 - core], xcomp, xs.at[n], xr.at[n], me, partner)
    swap_own = remote(dv.at[1 - core, own], xown, xs.at[n + 1], xr.at[n + 1], me, partner)
    swap_kown = remote(kown_give, kown_in, ts.at[n], tr.at[n], me, partner)

    def swap(i):
        return remote(dv.at[1 - core, slots(i)], xin.at[i], xs.at[i], xr.at[i], me, partner)

    def send(i):
        return remote(pack.at[i], recv.at[me], ss.at[i], sr.at[me], i, tp)

    def came(j):
        return remote(pack.at[j], recv.at[j], ss.at[j], sr.at[j], j, tp)

    def kswap(i):
        return remote(kgive.at[i], kin.at[i], ts.at[i], tr.at[i], me, partner)

    def ksend(i):
        return remote(kpack.at[i], krecv.at[me], ks.at[i], kr.at[me], i, tp)

    def kcame(j):
        return remote(kpack.at[j], krecv.at[j], ks.at[j], kr.at[j], j, tp)

    swap_comp.start()
    toward(me, -1, lambda i: swap(i).start())
    swap_own.start()
    for load in loads:
        load.wait()

    def add_and_send(i):
        swap(i).wait_recv()
        for s in range(2):
            pack[i, s * half : (s + 1) * half, :] = (
                mine[2 * i + s].astype(f32) + xin[i, s].astype(f32)
            ).astype(bf16)
        rows = comp_rows(i)
        pack[i, HD:, :] = (mcomp[rows, :].astype(f32) + xcomp[rows, :].astype(f32)).astype(bf16)
        send(i).start()

    for b in range(blocks):
        for h in range(HEADS_DEV):
            cols = slice(h * HD, (h + 1) * HD)
            qt[:, cols] = q_all[b * BLK : (b + 1) * BLK, cols].T
        ds_loads[b].wait()
        for t, cols in enumerate(column_chunks(nkeys)):
            dk = SCALING * lax.dot_general(qt[...], ds_all[b, :, cols], NN, preferred_element_type=f32)
            for c in range(COLS // BLK):
                dks[b * (per + 1) + t * (COLS // BLK) + c] = dk[:, c * BLK : (c + 1) * BLK]
        dks[b * (per + 1) + per] = jnp.zeros((HD, BLK), f32)
        if b == 0:
            swap_comp.wait_recv()
            toward(me, -1, add_and_send)
    first = core == 0

    def ours(x):
        return jnp.where(first, x[:half], x[half:])

    def theirs(x):
        return jnp.where(first, x[half:], x[:half])

    def slot_sum(i):
        for s in range(2):
            total = dks[source[0, 2 * i + s]]
            for b in range(1, blocks):
                total = total + dks[b * (per + 1) + source[b, 2 * i + s]]
            kmine[i, s * half : (s + 1) * half, :] = ours(total)
            kgive[i, s * half : (s + 1) * half, :] = theirs(total).astype(bf16)
        kswap(i).start()

    toward(me, -1, slot_sum)
    for b in range(blocks):
        kown_give[b] = theirs(dks[b * (per + 1)]).astype(bf16)
    swap_kown.start()

    def kadd_and_send(i):
        kswap(i).wait_recv()
        kpack[i] = (kmine[i] + kin[i].astype(f32)).astype(bf16)
        ksend(i).start()

    toward(me, -1, kadd_and_send)
    for b in range(blocks):
        for j in range(per):
            ksel[j * BLK : (j + 1) * BLK, :] = kbuf[where[b, j]]
        dq = dqc_all[b]
        for cols in column_chunks(nkeys):
            dq = dq + lax.dot_general(
                ds_all[b, :, cols], ksel[cols, :], NN, preferred_element_type=f32
            )
        for h in range(HEADS_DEV):
            dq_out[b * BLK : (b + 1) * BLK, h * HD : (h + 1) * HD] = (
                dq[h * BLK : (h + 1) * BLK] * SCALING
            ).astype(bf16)
    swap_own.wait_recv()
    swap_kown.wait_recv()
    for b in range(blocks):
        acc[b, half:, :] = mine[2 * n + b].astype(f32) + xown[b].astype(f32)
        acc[b, :half, :] = ours(dks[b * (per + 1)]) + kown_in[b].astype(f32)
    rows = comp_rows(me)

    ctotal_out[...] = mcomp[rows, :].astype(f32) + xcomp[rows, :].astype(f32)

    def take(j):
        came(j).wait_recv()
        mask = need[j]
        part = recv[j].astype(f32)
        for b in range(4):
            acc[b, half:, :] += mask[b : b + 1] * part[:half] + mask[4 + b : 5 + b] * part[half:HD]
        ctotal_out[...] += part[HD:]

    arrived(me, -1, take)

    def ktake(j):
        kcame(j).wait_recv()
        mask = need[j]
        part = krecv[j].astype(f32)
        for b in range(4):
            acc[b, :half, :] += mask[b : b + 1] * part[:half] + mask[4 + b : 5 + b] * part[half:]

    arrived(me, -1, ktake)
    for b in range(4):
        total_out[:, b * BLK : (b + 1) * BLK] = acc[b].astype(bf16)
    below(lambda i: swap(i).wait_send())
    swap_comp.wait_send()
    swap_own.wait_send()
    swap_kown.wait_send()
    below(lambda i: send(i).wait_send())
    below(lambda i: kswap(i).wait_send())
    below(lambda i: ksend(i).wait_send())


def part_kernel(total, ctotal, dq, dq_out, dk_out, dv_out, dck_out, dcv_out):
    half = HD // 2
    dq_out[...] = dq[...]
    dk_out[...] = total[:half, :]
    dv_out[...] = total[half:, :]
    both = ctotal[...]
    dck_out[...] = both[:, :half].astype(bf16)
    dcv_out[...] = both[:, half:].astype(bf16)


def local(queries, keys, values, comp_keys, comp_values, gate_comp, gate_sel, grad_out, selections):
    n = lax.axis_size("ctx")
    ctok = comp_keys.shape[0]
    anywhere = pl.BlockSpec(memory_space=pl.ANY)
    scalars = pl.BlockSpec(memory_space=pltpu.SMEM)
    vmem = pl.BlockSpec(memory_space=pltpu.VMEM)
    dma = pltpu.SemaphoreType.DMA
    slot_rows = (2 * n + 4) * BLK
    width = HEADS_DEV * BLK
    kv, need, dqc, dckv = pl.pallas_call(
        functools.partial(gather_kernel, n),
        in_specs=[scalars] + [anywhere] * 6 + [vmem],
        out_specs=[anywhere, vmem, anywhere, vmem],
        out_shape=[
            jax.ShapeDtypeStruct((2, slot_rows, HD), bf16),
            jax.ShapeDtypeStruct((n, 8, HD), f32),
            jax.ShapeDtypeStruct((4, width, HD), f32),
            jax.ShapeDtypeStruct((2, n * ctok, HD), bf16),
        ],
        scratch_shapes=[
            pltpu.VMEM((2, 4 * BLK, HD), bf16),
            pltpu.VMEM((2, ctok, HD), bf16),
            pltpu.VMEM((4 * BLK, HD), f32),
            pltpu.VMEM((8 * n, HD), f32),
            pltpu.VMEM((n, 8, HD), f32),
            pltpu.VMEM((n, 2 * BLK, HD), bf16),
            pltpu.VMEM((2, n * ctok, HD), bf16),
            pltpu.VMEM(queries.shape, bf16),
            pltpu.VMEM(queries.shape, bf16),
            pltpu.VMEM((HD, n * ctok), bf16),
            pltpu.VMEM((HD, n * ctok), bf16),
            pltpu.VMEM((ROWS, n * ctok), f32),
            pltpu.VMEM((ROWS, n * ctok), f32),
            pltpu.VMEM((4, width, HD), f32),
            pltpu.VMEM((2, HD, n * ctok), f32),
            dma((6,)), dma((2,)), dma((4,)),
            dma((n,)), dma((n,)), dma((n,)), dma((n,)),
            dma((n,)), dma((n,)), dma((n,)), dma((n,)),
        ],
        compiler_params=pltpu.CompilerParams(
            collective_id=0, has_side_effects=True, vmem_limit_bytes=GRANT
        ),
        name="gather",
    )(
        selections, keys, values, comp_keys, comp_values, queries, grad_out,
        gate_comp.T,
    )
    kv = kv.reshape(2, 2 * n + 4, BLK, HD)
    dv_half, ds, where, source = attend(selections, queries, grad_out, gate_sel.T, kv)
    blocks, _, nkeys = ds.shape
    half = HD // 2
    total, ctotal, dq = pl.pallas_call(
        functools.partial(reduce_kernel, n),
        in_specs=[anywhere, anywhere, anywhere, vmem, anywhere, anywhere, anywhere, scalars, scalars],
        out_specs=[vmem] * 3,
        out_shape=[
            jax.ShapeDtypeStruct((HD, 4 * BLK), bf16),
            jax.ShapeDtypeStruct((ctok, HD), f32),
            jax.ShapeDtypeStruct(queries.shape, bf16),
        ],
        scratch_shapes=[
            pltpu.VMEM(ds.shape, bf16),
            pltpu.VMEM((blocks * (nkeys // BLK + 1), HD, BLK), f32),
            pltpu.VMEM((2 * n + 4, half, BLK), bf16),
            pltpu.VMEM((n * ctok, HD), bf16),
            pltpu.VMEM((n, 2, half, BLK), bf16),
            pltpu.VMEM((4, half, BLK), bf16),
            pltpu.VMEM((n * ctok, HD), bf16),
            pltpu.VMEM((n, HD + ctok, BLK), bf16),
            pltpu.VMEM((n, HD + ctok, BLK), bf16),
            pltpu.VMEM((n, HD, BLK), f32),
            pltpu.VMEM((n, HD, BLK), bf16),
            pltpu.VMEM((n, HD, BLK), bf16),
            pltpu.VMEM((4, half, BLK), bf16),
            pltpu.VMEM((4, half, BLK), bf16),
            pltpu.VMEM((n, HD, BLK), bf16),
            pltpu.VMEM((n, HD, BLK), bf16),
            pltpu.VMEM((4, HD, BLK), f32),
            pltpu.VMEM(queries.shape, bf16),
            pltpu.VMEM((HD, width), bf16),
            pltpu.VMEM((2 * n + 4, BLK, HD), bf16),
            pltpu.VMEM((nkeys, HD), bf16),
            pltpu.VMEM(dqc.shape, f32),
            dma((5,)), dma((blocks,)),
            dma((n + 2,)), dma((n + 2,)), dma((n,)), dma((n,)),
            dma((n,)), dma((n,)), dma((n + 1,)), dma((n + 1,)),
        ],
        compiler_params=pltpu.CompilerParams(
            collective_id=1, has_side_effects=True, vmem_limit_bytes=GRANT
        ),
        name="reduce",
    )(dv_half, ds, dckv, need, queries, kv, dqc, where, source)
    half = jax.ShapeDtypeStruct((HD // 2, 4 * BLK), bf16)
    chalf = jax.ShapeDtypeStruct((ctok, HD // 2), bf16)
    grad_queries, dk, dv, dck, dcv = pl.pallas_call(
        part_kernel,
        in_specs=[vmem] * 3,
        out_specs=[vmem] * 5,
        out_shape=[jax.ShapeDtypeStruct(queries.shape, bf16), half, half, chalf, chalf],
        name="part",
    )(total, ctotal, dq)
    return grad_queries, dk.T, dv.T, dck, dcv


def solution(mesh):
    placed = (
        P("ctx", "tp"),
        P("ctx", None),
        P("ctx", None),
        P("ctx", None),
        P("ctx", None),
        P("ctx", "tp"),
        P("ctx", "tp"),
        P("ctx", "tp"),
        P("ctx", None, None),
    )
    return jax.shard_map(
        local,
        mesh=mesh,
        in_specs=placed,
        out_specs=(P("ctx", "tp"), P("ctx", "tp"), P("ctx", "tp"), P("ctx", "tp"), P("ctx", "tp")),
        check_vma=False,
    )
```

```python
import functools
import math

import jax
import jax.numpy as jnp
from jax import lax
from jax.experimental import pallas as pl
from jax.experimental.pallas import tpu as pltpu
from jax.sharding import PartitionSpec as P

HD = 128
BLK = 128
STRIDE = 16
HEADS_DEV = 8
NEG = -1e30
SCALING = 1.0 / math.sqrt(HD)
LOG2E_SCALING = math.log2(math.e) / math.sqrt(HD)
NN = (((1,), (0,)), ((), ()))
ROWS = 256
COLS = 512
GRANT = 60 * 1024 * 1024
f32 = jnp.float32
bf16 = jnp.bfloat16


def tiles(x, op):
    total = x[:, :HD]
    for t in range(1, x.shape[1] // HD):
        total = op(total, x[:, t * HD : (t + 1) * HD])
    return total


def column_chunks(width):
    return [slice(k0, k0 + COLS) for k0 in range(0, width, COLS)]


def weights(q, go, kt, vt, masked, s_ref, dp_ref):
    chunks = column_chunks(kt.shape[1])
    high = None
    for t, cols in enumerate(chunks):
        s = masked(t, lax.dot_general(q, kt[:, cols], NN, preferred_element_type=f32))
        s_ref[:, cols] = s
        top = tiles(s, jnp.maximum)
        high = top if high is None else jnp.maximum(high, top)
    high = jnp.max(high, axis=1, keepdims=True)
    total = inner = 0.0
    for cols in chunks:
        dp = lax.dot_general(go, vt[:, cols], NN, preferred_element_type=f32)
        w = jnp.exp2((s_ref[:, cols] - high) * LOG2E_SCALING)
        s_ref[:, cols] = w
        dp_ref[:, cols] = dp
        total = total + tiles(w, jnp.add)
        inner = inner + tiles(w * dp, jnp.add)
    inverse = 1.0 / jnp.sum(total, axis=1, keepdims=True)
    return inverse, jnp.sum(inner, axis=1, keepdims=True) * inverse


def branch(q, go, qt, got, kt, vt, keys, masked, s_ref, dp_ref, dk_ref, dv_ref):
    inverse, delta = weights(q, go, kt, vt, masked, s_ref, dp_ref)
    dq = 0.0
    for cols in column_chunks(kt.shape[1]):
        probs = s_ref[:, cols] * inverse
        dscore = (probs * (dp_ref[:, cols] - delta)).astype(bf16)
        dq = dq + lax.dot_general(dscore, keys[cols, :], NN, preferred_element_type=f32)
        dk_ref[:, cols] += lax.dot_general(qt, dscore, NN, preferred_element_type=f32)
        dv_ref[:, cols] += lax.dot_general(got, probs.astype(bf16), NN, preferred_element_type=f32)
    return dq


def attend_kernel(
    n, nsel, sel, q_ref, go_ref, gs_ref, kv_ref, dv_out, ds_out, where, source,
    acc, kt, vt, bias, s_ref, dp_ref, qs, gs, gt, masks,
):
    block = pl.program_id(0)
    group = lax.axis_index("tp") // 2
    own = 2 * n + block

    @pl.when(block == 0)
    def _():
        acc[...] = jnp.zeros_like(acc)
        words = [jnp.int32(0)] * (4 * n // 32)
        for r in range(4):
            for j in range(nsel):
                name = sel[r, group, j]
                bit = jnp.left_shift(jnp.int32(1), name & 31)
                for w in range(len(words)):
                    words[w] = words[w] | jnp.where((name >> 5) == w, bit, 0)
        for w, word in enumerate(words):
            masks[w] = word

    places, alive = [own], [None]
    where[block, 0] = own
    for i in range(2 * n):
        source[block, i] = nsel + 1
    for j in range(nsel):
        name = sel[block, group, j]
        live = name >= 0
        safe = jnp.maximum(name, 0)
        before = jnp.right_shift(masks[safe >> 5], safe & 28) & (
            jnp.left_shift(jnp.int32(1), safe & 3) - 1
        )
        at = 2 * (safe >> 2) + jnp.where(before != 0, 1, 0)
        places.append(jnp.where(live, at, own))
        alive.append(live)
        where[block, j + 1] = places[-1]
        source[block, jnp.where(live, at, 2 * n)] = j + 1
    for j, at in enumerate(places):
        cols = slice(j * BLK, (j + 1) * BLK)
        kt[:, cols] = kv_ref[0, at].T
        vt[:, cols] = kv_ref[1, at].T
        counts = jnp.float32(0.0)
        if j > 0:
            counts = jnp.where(alive[j], 0.0, NEG).astype(f32)
        bias[:, cols] = jnp.full((8, BLK), counts, f32)
    gate = gs_ref[...].T
    for h in range(HEADS_DEV):
        cols = slice(h * HD, (h + 1) * HD)
        rows = slice(h * BLK, (h + 1) * BLK)
        qs[rows, :] = q_ref[:, cols]
        gated = (go_ref[:, cols].astype(f32) * gate[:, h : h + 1]).astype(bf16)
        gs[rows, :] = gated
        gt[:, rows] = gated.T

    def masked(t, s):
        if t > 0:
            return s + bias[:1, t * COLS : (t + 1) * COLS]
        row = lax.broadcasted_iota(jnp.int32, (s.shape[0], BLK), 0) & (BLK - 1)
        key = lax.broadcasted_iota(jnp.int32, (s.shape[0], BLK), 1)
        own_part = jnp.where(key <= row, s[:, :BLK], NEG)
        return jnp.concatenate([own_part, s[:, BLK:] + bias[:1, BLK:COLS]], axis=1)

    inverse, delta = weights(qs[...], gs[...], kt, vt, masked, s_ref, dp_ref)
    for t, cols in enumerate(column_chunks(kt.shape[1])):
        probs = s_ref[:, cols] * inverse
        ds_out[0, :, cols] = (probs * (dp_ref[:, cols] - delta)).astype(bf16)
        dv = lax.dot_general(gt[...], probs.astype(bf16), NN, preferred_element_type=f32)
        for b in range(COLS // BLK):
            at = places[t * (COLS // BLK) + b]
            acc[at] += dv[:, b * BLK : (b + 1) * BLK]

    @pl.when(block == pl.num_programs(0) - 1)
    def _():
        half = HD // 2

        def finish(i, carry):
            for side in range(2):
                dv_out[side, i] = acc[i, side * half : (side + 1) * half, :].astype(bf16)
            return carry

        lax.fori_loop(0, acc.shape[0], finish, 0)


def attend(selections, queries, grad_out, gates_s, kv):
    n = lax.axis_size("ctx")
    blocks, _, nsel = selections.shape
    keys = (nsel + 1) * BLK
    width = HEADS_DEV * BLK
    whole = lambda shape: pl.BlockSpec(shape, lambda i: (0,) * len(shape))
    scalars = pl.BlockSpec(memory_space=pltpu.SMEM)
    rows = pl.BlockSpec((BLK, width), lambda i: (i, 0))
    half = (2, kv.shape[1], HD // 2, BLK)
    return pl.pallas_call(
        functools.partial(attend_kernel, n, nsel),
        grid=(blocks,),
        in_specs=[
            scalars, rows, rows, pl.BlockSpec((HEADS_DEV, BLK), lambda i: (0, i)), whole(kv.shape),
        ],
        out_specs=[
            whole(half), pl.BlockSpec((1, width, keys), lambda i: (i, 0, 0)), scalars, scalars,
        ],
        out_shape=[
            jax.ShapeDtypeStruct(half, bf16),
            jax.ShapeDtypeStruct((blocks, width, keys), bf16),
            jax.ShapeDtypeStruct((blocks, nsel + 1), jnp.int32),
            jax.ShapeDtypeStruct((blocks, 2 * n + 1), jnp.int32),
        ],
        scratch_shapes=[
            pltpu.VMEM((kv.shape[1], HD, BLK), f32),
            pltpu.VMEM((HD, keys), bf16),
            pltpu.VMEM((HD, keys), bf16),
            pltpu.VMEM((8, keys), f32),
            pltpu.VMEM((width, keys), f32),
            pltpu.VMEM((width, keys), f32),
            pltpu.VMEM((width, HD), bf16),
            pltpu.VMEM((width, HD), bf16),
            pltpu.VMEM((HD, width), bf16),
            pltpu.SMEM((4 * n // 32,), jnp.int32),
        ],
        compiler_params=pltpu.CompilerParams(
            vmem_limit_bytes=GRANT, dimension_semantics=("arbitrary",)
        ),
        name="attend",
    )(selections, queries, grad_out, gates_s, kv)


MESH = pl.DeviceIdType.MESH


def spots():
    me = lax.axis_index("ctx")
    tp = lax.axis_index("tp")
    return me, tp, lax.rem(tp, 2)


def greet(n, me, tp, core):
    barrier = pltpu.get_barrier_semaphore()
    for d in range(1, n):
        pl.semaphore_signal(
            barrier, inc=1, device_id=(lax.rem(me + d, n), tp), device_id_type=MESH
        )
    pl.semaphore_signal(barrier, inc=1, device_id=(me, tp + 1 - 2 * core), device_id_type=MESH)


def all_here(n):
    pl.semaphore_wait(pltpu.get_barrier_semaphore(), n)


def remote(src, dst, send, recv, ctx, tp):
    return pltpu.make_async_remote_copy(
        src_ref=src, dst_ref=dst, send_sem=send, recv_sem=recv, device_id=(ctx, tp), device_id_type=MESH
    )


def toward(me, sign, fn):
    def step(k, carry):
        x = me // 4 + sign * lax.rem(k, 4)
        ctx = 4 * x + lax.rem(lax.rem(me, 4) + k // 4, 4)

        @pl.when((x >= 0) & (x < 4) & (sign * (ctx - me) > 0))
        def _():
            fn(ctx)

        return carry

    lax.fori_loop(1, 16, step, 0)


def arrived(me, sign, fn):
    def step(k, carry):
        x = me // 4 - sign * lax.rem(k, 4)
        ctx = 4 * x + lax.rem(lax.rem(me, 4) + 4 - k // 4, 4)

        @pl.when((x >= 0) & (x < 4) & (sign * (me - ctx) > 0))
        def _():
            fn(ctx)

        return carry

    lax.fori_loop(1, 16, step, 0)


def gather_kernel(
    n, sel, keys, values, ckeys, cvalues, queries, grads, gc_ref, kv, need_out, dqc, dckv,
    own, owned, ownf, want, need_in, pack, ckv, q_all, go_all, ckt, cvt, s_ref, dp_ref, dqc_all, cacc,
    in_sem, keep_sem, dq_sem, ns, nr, cs, cr, ks, kr, fs, fr,
):
    me, tp, core = spots()
    group = tp // 2
    partner = tp + 1 - 2 * core
    cols = pl.ds(pl.multiple_of(group * HD, HD), HD)
    loads = [
        pltpu.make_async_copy(ckeys.at[:, cols], owned.at[0], in_sem.at[0]),
        pltpu.make_async_copy(cvalues.at[:, cols], owned.at[1], in_sem.at[1]),
        pltpu.make_async_copy(keys.at[:, cols], own.at[0], in_sem.at[2]),
        pltpu.make_async_copy(values.at[:, cols], own.at[1], in_sem.at[3]),
    ]
    greet(n, me, tp, core)
    late = [
        pltpu.make_async_copy(queries, q_all, in_sem.at[4]),
        pltpu.make_async_copy(grads, go_all, in_sem.at[5]),
    ]
    for load in loads + late:
        load.start()
    row = lax.broadcasted_iota(jnp.int32, (8 * n, HD), 0)
    quarter = lax.rem(row, 4)
    ident = 4 * (row // 8) + quarter
    used = jnp.zeros((8 * n, HD), f32)
    for r in range(4):
        for j in range(sel.shape[2]):
            used = jnp.where(ident == sel[r, group, j], 1.0, used)
    ahead = jnp.zeros_like(used)
    for k in range(1, 4):
        ahead = ahead + jnp.where(quarter >= k, pltpu.roll(used, k, 0), 0.0)
    place = lax.rem(row // 4, 2).astype(f32)
    want[...] = jnp.where(ahead == place, used, 0.0)
    ctok = ckeys.shape[0]
    crows = pl.ds(pl.multiple_of(me * ctok, ctok), ctok)
    my_slots = pl.ds(pl.multiple_of(me * 2 * BLK, 2 * BLK), 2 * BLK)

    def slots(i):
        return pl.ds(pl.multiple_of(i * 2 * BLK, 2 * BLK), 2 * BLK)

    def send_need(i):
        rows = pl.ds(pl.multiple_of(i * 8, 8), 8)
        return remote(want.at[rows, :], need_in.at[me], ns.at[i], nr.at[me], i, tp)

    def send_comp(j):
        return remote(owned, ckv.at[:, crows, :], cs.at[j], cr.at[me], j, tp)

    def send_kv(j):
        return remote(pack.at[j], kv.at[core, my_slots, :], ks.at[j], kr.at[me], j, tp)

    def forward(i):
        return remote(
            kv.at[core, slots(i), :], kv.at[core, slots(i), :], fs.at[i], fr.at[i], me, partner
        )

    def need_from(j):
        return remote(want.at[pl.ds(0, 8), :], need_in.at[j], ns.at[j], nr.at[j], j, tp)

    def comp_from(j):
        rows = pl.ds(pl.multiple_of(j * ctok, ctok), ctok)
        return remote(owned, ckv.at[:, rows, :], cs.at[j], cr.at[j], j, tp)

    def kv_from(i):
        return remote(pack.at[i], kv.at[core, slots(i), :], ks.at[i], kr.at[i], i, tp)

    def forwarded(i):
        return remote(
            kv.at[core, slots(i), :], kv.at[1 - core, slots(i), :], fs.at[i], fr.at[i], me, partner
        )

    def down(fn):
        def step(k, carry):
            fn(me - 1 - k)
            return carry

        lax.fori_loop(0, me, step, 0)

    def up(fn):
        def step(j, carry):
            fn(j)
            return carry

        lax.fori_loop(me + 1, n, step, 0)

    all_here(n)
    down(lambda i: send_need(i).start())
    for load in loads:
        load.wait()
    keep = [
        pltpu.make_async_copy(own, kv.at[:, pl.ds(2 * n * BLK, 4 * BLK), :], keep_sem.at[0]),
        pltpu.make_async_copy(owned, ckv.at[:, crows, :], keep_sem.at[1]),
    ]
    for copy in keep:
        copy.start()

    up(lambda j: send_comp(j).start())
    ownf[...] = own[core].astype(f32)

    def pack_and_send(j):
        need_from(j).wait_recv()
        mask = need_in[j]
        for s in range(2):
            total = mask[4 * s : 4 * s + 1] * ownf[:BLK, :]
            for b in range(1, 4):
                total = total + mask[4 * s + b : 4 * s + b + 1] * ownf[b * BLK : (b + 1) * BLK, :]
            pack[j, s * BLK : (s + 1) * BLK, :] = total.astype(bf16)
        need_out[j] = mask
        send_kv(j).start()

    toward(me, 1, pack_and_send)

    cacc[...] = jnp.zeros_like(cacc)
    for load in late:
        load.wait()

    def no_rows(j):
        rows = pl.ds(pl.multiple_of(j * ctok, ctok), ctok)
        ckv[:, rows, :] = jnp.zeros((2, ctok, HD), bf16)

    up(no_rows)
    down(lambda j: comp_from(j).wait_recv())
    keep[1].wait()
    ckt[...] = ckv[0].T
    cvt[...] = ckv[1].T
    gate = gc_ref[...].T

    def compressed(block):
        tokens = slice(block * BLK, (block + 1) * BLK)
        start = (me * 4 + block) * BLK

        def before(t, s):
            row = lax.broadcasted_iota(jnp.int32, s.shape, 0) & (BLK - 1)
            key = lax.broadcasted_iota(jnp.int32, s.shape, 1) * STRIDE + t * (COLS * STRIDE)
            return jnp.where(key - row <= start, s, NEG)

        for r in range(HEADS_DEV * BLK // ROWS):
            parts = range(r * ROWS // BLK, (r + 1) * ROWS // BLK)
            q = jnp.concatenate([q_all[tokens, h * HD : (h + 1) * HD] for h in parts], axis=0)
            go = jnp.concatenate(
                [
                    (go_all[tokens, h * HD : (h + 1) * HD].astype(f32) * gate[tokens, h : h + 1]).astype(bf16)
                    for h in parts
                ],
                axis=0,
            )
            dqc_all[block, r * ROWS : (r + 1) * ROWS, :] = branch(
                q, go, q.T, go.T, ckt, cvt, ckv.at[0], before,
                s_ref, dp_ref, cacc.at[0], cacc.at[1],
            )

    def save(block):
        return pltpu.make_async_copy(dqc_all.at[block], dqc.at[block], dq_sem.at[block])

    def pass_on(i):
        kv_from(i).wait_recv()
        forward(i).start()

    for block in range(3):
        compressed(block)
        save(block).start()
    arrived(me, 1, pass_on)
    compressed(3)
    save(3).start()
    half = HD // 2
    for side in range(2):
        rows = slice(side * half, (side + 1) * half)
        joined = jnp.concatenate([cacc[0, rows, :] * SCALING, cacc[1, rows, :]], axis=0)
        dckv[side] = joined.T.astype(bf16)
    down(lambda i: forwarded(i).wait_recv())
    down(lambda i: send_need(i).wait_send())
    up(lambda j: send_kv(j).wait_send())
    down(lambda i: forward(i).wait_send())
    up(lambda j: send_comp(j).wait_send())
    keep[0].wait()
    for block in range(4):
        save(block).wait()


def reduce_kernel(
    n, dv, ds, dckv, need, queries, kv, dqc, where, source, total_out, ctotal_out, dq_out,
    ds_all, dks, mine, mcomp, xin, xown, xcomp, pack, recv, kmine, kgive, kin, kown_give, kown_in,
    kpack, krecv, acc, q_all, qt, kbuf, ksel, dqc_all,
    in_sem, ds_sem, xs, xr, ss, sr, ks, kr, ts, tr,
):
    me, tp, core = spots()
    partner = tp + 1 - 2 * core
    ctok = dckv.shape[1] // n
    half = HD // 2
    blocks, nkeys = ds.shape[0], ds.shape[2]
    per = nkeys // BLK
    own = pl.ds(2 * n, 4)

    def slots(i):
        return pl.ds(i * 2, 2)

    def comp_rows(i):
        return pl.ds(pl.multiple_of(i * ctok, ctok), ctok)

    loads = [
        pltpu.make_async_copy(queries, q_all, in_sem.at[0]),
        pltpu.make_async_copy(dckv.at[core], mcomp, in_sem.at[1]),
        pltpu.make_async_copy(dv.at[core], mine, in_sem.at[2]),
        pltpu.make_async_copy(kv.at[0], kbuf, in_sem.at[3]),
        pltpu.make_async_copy(dqc, dqc_all, in_sem.at[4]),
    ]
    ds_loads = [
        pltpu.make_async_copy(ds.at[b], ds_all.at[b], ds_sem.at[b]) for b in range(blocks)
    ]
    greet(n, me, tp, core)
    for load in loads[:1] + ds_loads[:1] + loads[1:3] + ds_loads[1:] + loads[3:]:
        load.start()
    all_here(n)

    def below(fn):
        def step(i, carry):
            fn(i)
            return carry

        lax.fori_loop(0, me, step, 0)

    swap_comp = remote(dckv.at[1 - core], xcomp, xs.at[n], xr.at[n], me, partner)
    swap_own = remote(dv.at[1 - core, own], xown, xs.at[n + 1], xr.at[n + 1], me, partner)
    swap_kown = remote(kown_give, kown_in, ts.at[n], tr.at[n], me, partner)

    def swap(i):
        return remote(dv.at[1 - core, slots(i)], xin.at[i], xs.at[i], xr.at[i], me, partner)

    def send(i):
        return remote(pack.at[i], recv.at[me], ss.at[i], sr.at[me], i, tp)

    def came(j):
        return remote(pack.at[j], recv.at[j], ss.at[j], sr.at[j], j, tp)

    def kswap(i):
        return remote(kgive.at[i], kin.at[i], ts.at[i], tr.at[i], me, partner)

    def ksend(i):
        return remote(kpack.at[i], krecv.at[me], ks.at[i], kr.at[me], i, tp)

    def kcame(j):
        return remote(kpack.at[j], krecv.at[j], ks.at[j], kr.at[j], j, tp)

    swap_comp.start()
    toward(me, -1, lambda i: swap(i).start())
    swap_own.start()
    for load in loads[:3]:
        load.wait()

    def add_and_send(i):
        swap(i).wait_recv()
        for s in range(2):
            pack[i, s * half : (s + 1) * half, :] = (
                mine[2 * i + s].astype(f32) + xin[i, s].astype(f32)
            ).astype(bf16)
        rows = comp_rows(i)
        pack[i, HD:, :] = (mcomp[rows, :].astype(f32) + xcomp[rows, :].astype(f32)).astype(bf16)
        send(i).start()

    for b in range(blocks):
        for h in range(HEADS_DEV):
            cols = slice(h * HD, (h + 1) * HD)
            qt[:, cols] = q_all[b * BLK : (b + 1) * BLK, cols].T
        ds_loads[b].wait()
        for t, cols in enumerate(column_chunks(nkeys)):
            dk = SCALING * lax.dot_general(qt[...], ds_all[b, :, cols], NN, preferred_element_type=f32)
            for c in range(COLS // BLK):
                dks[b * (per + 1) + t * (COLS // BLK) + c] = dk[:, c * BLK : (c + 1) * BLK]
        dks[b * (per + 1) + per] = jnp.zeros((HD, BLK), f32)
        if b == 0:
            swap_comp.wait_recv()
            toward(me, -1, add_and_send)
    first = core == 0

    def ours(x):
        return jnp.where(first, x[:half], x[half:])

    def theirs(x):
        return jnp.where(first, x[half:], x[:half])

    def slot_sum(i):
        for s in range(2):
            total = dks[source[0, 2 * i + s]]
            for b in range(1, blocks):
                total = total + dks[b * (per + 1) + source[b, 2 * i + s]]
            kmine[i, s * half : (s + 1) * half, :] = ours(total)
            kgive[i, s * half : (s + 1) * half, :] = theirs(total).astype(bf16)
        kswap(i).start()

    toward(me, -1, slot_sum)
    for b in range(blocks):
        kown_give[b] = theirs(dks[b * (per + 1)]).astype(bf16)
    swap_kown.start()

    def kadd_and_send(i):
        kswap(i).wait_recv()
        kpack[i] = (kmine[i] + kin[i].astype(f32)).astype(bf16)
        ksend(i).start()

    toward(me, -1, kadd_and_send)
    for load in loads[3:]:
        load.wait()
    for b in range(blocks):
        for j in range(per):
            ksel[j * BLK : (j + 1) * BLK, :] = kbuf[where[b, j]]
        dq = dqc_all[b]
        for cols in column_chunks(nkeys):
            dq = dq + lax.dot_general(
                ds_all[b, :, cols], ksel[cols, :], NN, preferred_element_type=f32
            )
        for h in range(HEADS_DEV):
            dq_out[b * BLK : (b + 1) * BLK, h * HD : (h + 1) * HD] = (
                dq[h * BLK : (h + 1) * BLK] * SCALING
            ).astype(bf16)
    swap_own.wait_recv()
    swap_kown.wait_recv()
    for b in range(blocks):
        acc[b, half:, :] = mine[2 * n + b].astype(f32) + xown[b].astype(f32)
        acc[b, :half, :] = ours(dks[b * (per + 1)]) + kown_in[b].astype(f32)
    rows = comp_rows(me)

    ctotal_out[...] = mcomp[rows, :].astype(f32) + xcomp[rows, :].astype(f32)

    def take(j):
        came(j).wait_recv()
        mask = need[j]
        part = recv[j].astype(f32)
        for b in range(4):
            acc[b, half:, :] += mask[b : b + 1] * part[:half] + mask[4 + b : 5 + b] * part[half:HD]
        ctotal_out[...] += part[HD:]

    arrived(me, -1, take)

    def ktake(j):
        kcame(j).wait_recv()
        mask = need[j]
        part = krecv[j].astype(f32)
        for b in range(4):
            acc[b, :half, :] += mask[b : b + 1] * part[:half] + mask[4 + b : 5 + b] * part[half:]

    arrived(me, -1, ktake)
    for b in range(4):
        total_out[:, b * BLK : (b + 1) * BLK] = acc[b].astype(bf16)
    below(lambda i: swap(i).wait_send())
    swap_comp.wait_send()
    swap_own.wait_send()
    swap_kown.wait_send()
    below(lambda i: send(i).wait_send())
    below(lambda i: kswap(i).wait_send())
    below(lambda i: ksend(i).wait_send())


def part_kernel(total, ctotal, dq, dq_out, dk_out, dv_out, dck_out, dcv_out):
    half = HD // 2
    dq_out[...] = dq[...]
    dk_out[...] = total[:half, :]
    dv_out[...] = total[half:, :]
    both = ctotal[...]
    dck_out[...] = both[:, :half].astype(bf16)
    dcv_out[...] = both[:, half:].astype(bf16)


def local(queries, keys, values, comp_keys, comp_values, gate_comp, gate_sel, grad_out, selections):
    n = lax.axis_size("ctx")
    ctok = comp_keys.shape[0]
    anywhere = pl.BlockSpec(memory_space=pl.ANY)
    scalars = pl.BlockSpec(memory_space=pltpu.SMEM)
    vmem = pl.BlockSpec(memory_space=pltpu.VMEM)
    dma = pltpu.SemaphoreType.DMA
    slot_rows = (2 * n + 4) * BLK
    width = HEADS_DEV * BLK
    kv, need, dqc, dckv = pl.pallas_call(
        functools.partial(gather_kernel, n),
        in_specs=[scalars] + [anywhere] * 6 + [vmem],
        out_specs=[anywhere, vmem, anywhere, vmem],
        out_shape=[
            jax.ShapeDtypeStruct((2, slot_rows, HD), bf16),
            jax.ShapeDtypeStruct((n, 8, HD), f32),
            jax.ShapeDtypeStruct((4, width, HD), f32),
            jax.ShapeDtypeStruct((2, n * ctok, HD), bf16),
        ],
        scratch_shapes=[
            pltpu.VMEM((2, 4 * BLK, HD), bf16),
            pltpu.VMEM((2, ctok, HD), bf16),
            pltpu.VMEM((4 * BLK, HD), f32),
            pltpu.VMEM((8 * n, HD), f32),
            pltpu.VMEM((n, 8, HD), f32),
            pltpu.VMEM((n, 2 * BLK, HD), bf16),
            pltpu.VMEM((2, n * ctok, HD), bf16),
            pltpu.VMEM(queries.shape, bf16),
            pltpu.VMEM(queries.shape, bf16),
            pltpu.VMEM((HD, n * ctok), bf16),
            pltpu.VMEM((HD, n * ctok), bf16),
            pltpu.VMEM((ROWS, n * ctok), f32),
            pltpu.VMEM((ROWS, n * ctok), f32),
            pltpu.VMEM((4, width, HD), f32),
            pltpu.VMEM((2, HD, n * ctok), f32),
            dma((6,)), dma((2,)), dma((4,)),
            dma((n,)), dma((n,)), dma((n,)), dma((n,)),
            dma((n,)), dma((n,)), dma((n,)), dma((n,)),
        ],
        compiler_params=pltpu.CompilerParams(
            collective_id=0, has_side_effects=True, vmem_limit_bytes=GRANT
        ),
        name="gather",
    )(
        selections, keys, values, comp_keys, comp_values, queries, grad_out,
        gate_comp.T,
    )
    kv = kv.reshape(2, 2 * n + 4, BLK, HD)
    dv_half, ds, where, source = attend(selections, queries, grad_out, gate_sel.T, kv)
    blocks, _, nkeys = ds.shape
    half = HD // 2
    total, ctotal, dq = pl.pallas_call(
        functools.partial(reduce_kernel, n),
        in_specs=[anywhere, anywhere, anywhere, vmem, anywhere, anywhere, anywhere, scalars, scalars],
        out_specs=[vmem] * 3,
        out_shape=[
            jax.ShapeDtypeStruct((HD, 4 * BLK), bf16),
            jax.ShapeDtypeStruct((ctok, HD), f32),
            jax.ShapeDtypeStruct(queries.shape, bf16),
        ],
        scratch_shapes=[
            pltpu.VMEM(ds.shape, bf16),
            pltpu.VMEM((blocks * (nkeys // BLK + 1), HD, BLK), f32),
            pltpu.VMEM((2 * n + 4, half, BLK), bf16),
            pltpu.VMEM((n * ctok, HD), bf16),
            pltpu.VMEM((n, 2, half, BLK), bf16),
            pltpu.VMEM((4, half, BLK), bf16),
            pltpu.VMEM((n * ctok, HD), bf16),
            pltpu.VMEM((n, HD + ctok, BLK), bf16),
            pltpu.VMEM((n, HD + ctok, BLK), bf16),
            pltpu.VMEM((n, HD, BLK), f32),
            pltpu.VMEM((n, HD, BLK), bf16),
            pltpu.VMEM((n, HD, BLK), bf16),
            pltpu.VMEM((4, half, BLK), bf16),
            pltpu.VMEM((4, half, BLK), bf16),
            pltpu.VMEM((n, HD, BLK), bf16),
            pltpu.VMEM((n, HD, BLK), bf16),
            pltpu.VMEM((4, HD, BLK), f32),
            pltpu.VMEM(queries.shape, bf16),
            pltpu.VMEM((HD, width), bf16),
            pltpu.VMEM((2 * n + 4, BLK, HD), bf16),
            pltpu.VMEM((nkeys, HD), bf16),
            pltpu.VMEM(dqc.shape, f32),
            dma((5,)), dma((blocks,)),
            dma((n + 2,)), dma((n + 2,)), dma((n,)), dma((n,)),
            dma((n,)), dma((n,)), dma((n + 1,)), dma((n + 1,)),
        ],
        compiler_params=pltpu.CompilerParams(
            collective_id=1, has_side_effects=True, vmem_limit_bytes=GRANT
        ),
        name="reduce",
    )(dv_half, ds, dckv, need, queries, kv, dqc, where, source)
    half = jax.ShapeDtypeStruct((HD // 2, 4 * BLK), bf16)
    chalf = jax.ShapeDtypeStruct((ctok, HD // 2), bf16)
    grad_queries, dk, dv, dck, dcv = pl.pallas_call(
        part_kernel,
        in_specs=[vmem] * 3,
        out_specs=[vmem] * 5,
        out_shape=[jax.ShapeDtypeStruct(queries.shape, bf16), half, half, chalf, chalf],
        name="part",
    )(total, ctotal, dq)
    return grad_queries, dk.T, dv.T, dck, dcv


def solution(mesh):
    placed = (
        P("ctx", "tp"),
        P("ctx", None),
        P("ctx", None),
        P("ctx", None),
        P("ctx", None),
        P("ctx", "tp"),
        P("ctx", "tp"),
        P("ctx", "tp"),
        P("ctx", None, None),
    )
    return jax.shard_map(
        local,
        mesh=mesh,
        in_specs=placed,
        out_specs=(P("ctx", "tp"), P("ctx", "tp"), P("ctx", "tp"), P("ctx", "tp"), P("ctx", "tp")),
        check_vma=False,
    )
```

```python
import functools
import math

import jax
import jax.numpy as jnp
from jax import lax
from jax.experimental import pallas as pl
from jax.experimental.pallas import tpu as pltpu
from jax.sharding import PartitionSpec as P

HD = 128
BLK = 128
STRIDE = 16
HEADS_DEV = 8
NEG = -1e30
SCALING = 1.0 / math.sqrt(HD)
LOG2E_SCALING = math.log2(math.e) / math.sqrt(HD)
NN = (((1,), (0,)), ((), ()))
ROWS = 256
COLS = 512
GRANT = 60 * 1024 * 1024
f32 = jnp.float32
bf16 = jnp.bfloat16


def tiles(x, op):
    total = x[:, :HD]
    for t in range(1, x.shape[1] // HD):
        total = op(total, x[:, t * HD : (t + 1) * HD])
    return total


def column_chunks(width):
    return [slice(k0, k0 + COLS) for k0 in range(0, width, COLS)]


def weights(q, go, kt, vt, masked, s_ref, dp_ref):
    chunks = column_chunks(kt.shape[1])
    high = None
    for t, cols in enumerate(chunks):
        s = masked(t, lax.dot_general(q, kt[:, cols], NN, preferred_element_type=f32))
        s_ref[:, cols] = s
        top = tiles(s, jnp.maximum)
        high = top if high is None else jnp.maximum(high, top)
    high = jnp.max(high, axis=1, keepdims=True)
    total = inner = 0.0
    for cols in chunks:
        dp = lax.dot_general(go, vt[:, cols], NN, preferred_element_type=f32)
        w = jnp.exp2((s_ref[:, cols] - high) * LOG2E_SCALING)
        s_ref[:, cols] = w
        dp_ref[:, cols] = dp
        total = total + tiles(w, jnp.add)
        inner = inner + tiles(w * dp, jnp.add)
    inverse = 1.0 / jnp.sum(total, axis=1, keepdims=True)
    return inverse, jnp.sum(inner, axis=1, keepdims=True) * inverse


def branch(q, go, qt, got, kt, vt, keys, masked, s_ref, dp_ref, dk_ref, dv_ref):
    inverse, delta = weights(q, go, kt, vt, masked, s_ref, dp_ref)
    dq = 0.0
    for cols in column_chunks(kt.shape[1]):
        probs = s_ref[:, cols] * inverse
        dscore = (probs * (dp_ref[:, cols] - delta)).astype(bf16)
        dq = dq + lax.dot_general(dscore, keys[cols, :], NN, preferred_element_type=f32)
        dk_ref[:, cols] += lax.dot_general(qt, dscore, NN, preferred_element_type=f32)
        dv_ref[:, cols] += lax.dot_general(got, probs.astype(bf16), NN, preferred_element_type=f32)
    return dq


def attend_kernel(
    n, nsel, sel, q_ref, go_ref, gs_ref, kv_ref, dv_out, ds_out, where, source,
    acc, kt, vt, bias, s_ref, dp_ref, qs, gs, gt, masks,
):
    block = pl.program_id(0)
    group = lax.axis_index("tp") // 2
    own = 2 * n + block

    @pl.when(block == 0)
    def _():
        acc[...] = jnp.zeros_like(acc)
        words = [jnp.int32(0)] * (4 * n // 32)
        for r in range(4):
            for j in range(nsel):
                name = sel[r, group, j]
                bit = jnp.left_shift(jnp.int32(1), name & 31)
                for w in range(len(words)):
                    words[w] = words[w] | jnp.where((name >> 5) == w, bit, 0)
        for w, word in enumerate(words):
            masks[w] = word

    places, alive = [own], [None]
    where[block, 0] = own
    for i in range(2 * n):
        source[block, i] = nsel + 1
    for j in range(nsel):
        name = sel[block, group, j]
        live = name >= 0
        safe = jnp.maximum(name, 0)
        before = jnp.right_shift(masks[safe >> 5], safe & 28) & (
            jnp.left_shift(jnp.int32(1), safe & 3) - 1
        )
        at = 2 * (safe >> 2) + jnp.where(before != 0, 1, 0)
        places.append(jnp.where(live, at, own))
        alive.append(live)
        where[block, j + 1] = places[-1]
        source[block, jnp.where(live, at, 2 * n)] = j + 1
    for j, at in enumerate(places):
        cols = slice(j * BLK, (j + 1) * BLK)
        kt[:, cols] = kv_ref[0, at].T
        vt[:, cols] = kv_ref[1, at].T
        counts = jnp.float32(0.0)
        if j > 0:
            counts = jnp.where(alive[j], 0.0, NEG).astype(f32)
        bias[:, cols] = jnp.full((8, BLK), counts, f32)
    gate = gs_ref[...].T
    for h in range(HEADS_DEV):
        cols = slice(h * HD, (h + 1) * HD)
        rows = slice(h * BLK, (h + 1) * BLK)
        qs[rows, :] = q_ref[:, cols]
        gated = (go_ref[:, cols].astype(f32) * gate[:, h : h + 1]).astype(bf16)
        gs[rows, :] = gated
        gt[:, rows] = gated.T

    def masked(t, s):
        if t > 0:
            return s + bias[:1, t * COLS : (t + 1) * COLS]
        row = lax.broadcasted_iota(jnp.int32, (s.shape[0], BLK), 0) & (BLK - 1)
        key = lax.broadcasted_iota(jnp.int32, (s.shape[0], BLK), 1)
        own_part = jnp.where(key <= row, s[:, :BLK], NEG)
        return jnp.concatenate([own_part, s[:, BLK:] + bias[:1, BLK:COLS]], axis=1)

    inverse, delta = weights(qs[...], gs[...], kt, vt, masked, s_ref, dp_ref)
    for t, cols in enumerate(column_chunks(kt.shape[1])):
        probs = s_ref[:, cols] * inverse
        ds_out[0, :, cols] = (probs * (dp_ref[:, cols] - delta)).astype(bf16)
        dv = lax.dot_general(gt[...], probs.astype(bf16), NN, preferred_element_type=f32)
        for b in range(COLS // BLK):
            at = places[t * (COLS // BLK) + b]
            acc[at] += dv[:, b * BLK : (b + 1) * BLK]

    @pl.when(block == pl.num_programs(0) - 1)
    def _():
        half = HD // 2

        def finish(i, carry):
            for side in range(2):
                dv_out[side, i] = acc[i, side * half : (side + 1) * half, :].astype(bf16)
            return carry

        lax.fori_loop(0, acc.shape[0], finish, 0)


def attend(selections, queries, grad_out, gates_s, kv):
    n = lax.axis_size("ctx")
    blocks, _, nsel = selections.shape
    keys = (nsel + 1) * BLK
    width = HEADS_DEV * BLK
    whole = lambda shape: pl.BlockSpec(shape, lambda i: (0,) * len(shape))
    scalars = pl.BlockSpec(memory_space=pltpu.SMEM)
    rows = pl.BlockSpec((BLK, width), lambda i: (i, 0))
    half = (2, kv.shape[1], HD // 2, BLK)
    return pl.pallas_call(
        functools.partial(attend_kernel, n, nsel),
        grid=(blocks,),
        in_specs=[
            scalars, rows, rows, pl.BlockSpec((HEADS_DEV, BLK), lambda i: (0, i)), whole(kv.shape),
        ],
        out_specs=[
            whole(half), pl.BlockSpec((1, width, keys), lambda i: (i, 0, 0)), scalars, scalars,
        ],
        out_shape=[
            jax.ShapeDtypeStruct(half, bf16),
            jax.ShapeDtypeStruct((blocks, width, keys), bf16),
            jax.ShapeDtypeStruct((blocks, nsel + 1), jnp.int32),
            jax.ShapeDtypeStruct((blocks, 2 * n + 1), jnp.int32),
        ],
        scratch_shapes=[
            pltpu.VMEM((kv.shape[1], HD, BLK), f32),
            pltpu.VMEM((HD, keys), bf16),
            pltpu.VMEM((HD, keys), bf16),
            pltpu.VMEM((8, keys), f32),
            pltpu.VMEM((width, keys), f32),
            pltpu.VMEM((width, keys), f32),
            pltpu.VMEM((width, HD), bf16),
            pltpu.VMEM((width, HD), bf16),
            pltpu.VMEM((HD, width), bf16),
            pltpu.SMEM((4 * n // 32,), jnp.int32),
        ],
        compiler_params=pltpu.CompilerParams(
            vmem_limit_bytes=GRANT, dimension_semantics=("arbitrary",)
        ),
        name="attend",
    )(selections, queries, grad_out, gates_s, kv)


MESH = pl.DeviceIdType.MESH


def spots():
    me = lax.axis_index("ctx")
    tp = lax.axis_index("tp")
    return me, tp, lax.rem(tp, 2)


def greet(n, me, tp, core):
    barrier = pltpu.get_barrier_semaphore()
    for d in range(1, n):
        pl.semaphore_signal(
            barrier, inc=1, device_id=(lax.rem(me + d, n), tp), device_id_type=MESH
        )
    pl.semaphore_signal(barrier, inc=1, device_id=(me, tp + 1 - 2 * core), device_id_type=MESH)


def all_here(n):
    pl.semaphore_wait(pltpu.get_barrier_semaphore(), n)


def remote(src, dst, send, recv, ctx, tp):
    return pltpu.make_async_remote_copy(
        src_ref=src, dst_ref=dst, send_sem=send, recv_sem=recv, device_id=(ctx, tp), device_id_type=MESH
    )


def toward(me, sign, fn):
    def step(k, carry):
        x = me // 4 + sign * lax.rem(k, 4)
        ctx = 4 * x + lax.rem(lax.rem(me, 4) + k // 4, 4)

        @pl.when((x >= 0) & (x < 4) & (sign * (ctx - me) > 0))
        def _():
            fn(ctx)

        return carry

    lax.fori_loop(1, 16, step, 0)


def arrived(me, sign, fn):
    def step(k, carry):
        x = me // 4 - sign * lax.rem(k, 4)
        ctx = 4 * x + lax.rem(lax.rem(me, 4) + 4 - k // 4, 4)

        @pl.when((x >= 0) & (x < 4) & (sign * (me - ctx) > 0))
        def _():
            fn(ctx)

        return carry

    lax.fori_loop(1, 16, step, 0)


def gather_kernel(
    n, sel, keys, values, ckeys, cvalues, queries, grads, gc_ref, kv, need_out, dqc, dckv,
    own, owned, ownf, want, need_in, pack, ckv, q_all, go_all, ckt, cvt, s_ref, dp_ref, dqc_all, cacc,
    in_sem, keep_sem, dq_sem, ns, nr, cs, cr, ks, kr, fs, fr,
):
    me, tp, core = spots()
    group = tp // 2
    partner = tp + 1 - 2 * core
    cols = pl.ds(pl.multiple_of(group * HD, HD), HD)
    loads = [
        pltpu.make_async_copy(ckeys.at[:, cols], owned.at[0], in_sem.at[0]),
        pltpu.make_async_copy(cvalues.at[:, cols], owned.at[1], in_sem.at[1]),
        pltpu.make_async_copy(keys.at[:, cols], own.at[0], in_sem.at[2]),
        pltpu.make_async_copy(values.at[:, cols], own.at[1], in_sem.at[3]),
    ]
    greet(n, me, tp, core)
    late = [
        pltpu.make_async_copy(queries, q_all, in_sem.at[4]),
        pltpu.make_async_copy(grads, go_all, in_sem.at[5]),
    ]
    for load in loads + late:
        load.start()
    row = lax.broadcasted_iota(jnp.int32, (8 * n, HD), 0)
    quarter = lax.rem(row, 4)
    ident = 4 * (row // 8) + quarter
    used = jnp.zeros((8 * n, HD), f32)
    for r in range(4):
        for j in range(sel.shape[2]):
            used = jnp.where(ident == sel[r, group, j], 1.0, used)
    ahead = jnp.zeros_like(used)
    for k in range(1, 4):
        ahead = ahead + jnp.where(quarter >= k, pltpu.roll(used, k, 0), 0.0)
    place = lax.rem(row // 4, 2).astype(f32)
    want[...] = jnp.where(ahead == place, used, 0.0)
    ctok = ckeys.shape[0]
    crows = pl.ds(pl.multiple_of(me * ctok, ctok), ctok)
    my_slots = pl.ds(pl.multiple_of(me * 2 * BLK, 2 * BLK), 2 * BLK)

    def slots(i):
        return pl.ds(pl.multiple_of(i * 2 * BLK, 2 * BLK), 2 * BLK)

    def send_need(i):
        rows = pl.ds(pl.multiple_of(i * 8, 8), 8)
        return remote(want.at[rows, :], need_in.at[me], ns.at[i], nr.at[me], i, tp)

    def send_comp(j):
        return remote(owned, ckv.at[:, crows, :], cs.at[j], cr.at[me], j, tp)

    def send_kv(j):
        return remote(pack.at[j], kv.at[core, my_slots, :], ks.at[j], kr.at[me], j, tp)

    def forward(i):
        return remote(
            kv.at[core, slots(i), :], kv.at[core, slots(i), :], fs.at[i], fr.at[i], me, partner
        )

    def need_from(j):
        return remote(want.at[pl.ds(0, 8), :], need_in.at[j], ns.at[j], nr.at[j], j, tp)

    def comp_from(j):
        rows = pl.ds(pl.multiple_of(j * ctok, ctok), ctok)
        return remote(owned, ckv.at[:, rows, :], cs.at[j], cr.at[j], j, tp)

    def kv_from(i):
        return remote(pack.at[i], kv.at[core, slots(i), :], ks.at[i], kr.at[i], i, tp)

    def forwarded(i):
        return remote(
            kv.at[core, slots(i), :], kv.at[1 - core, slots(i), :], fs.at[i], fr.at[i], me, partner
        )

    def down(fn):
        def step(k, carry):
            fn(me - 1 - k)
            return carry

        lax.fori_loop(0, me, step, 0)

    def up(fn):
        def step(j, carry):
            fn(j)
            return carry

        lax.fori_loop(me + 1, n, step, 0)

    all_here(n)

    def ask(i, carry):
        send_need(i).start()
        return carry

    lax.fori_loop(0, me, ask, 0)
    for load in loads:
        load.wait()
    keep = [
        pltpu.make_async_copy(own, kv.at[:, pl.ds(2 * n * BLK, 4 * BLK), :], keep_sem.at[0]),
        pltpu.make_async_copy(owned, ckv.at[:, crows, :], keep_sem.at[1]),
    ]
    for copy in keep:
        copy.start()

    up(lambda j: send_comp(j).start())
    ownf[...] = own[core].astype(f32)

    def pack_and_send(j):
        need_from(j).wait_recv()
        mask = need_in[j]
        for s in range(2):
            total = mask[4 * s : 4 * s + 1] * ownf[:BLK, :]
            for b in range(1, 4):
                total = total + mask[4 * s + b : 4 * s + b + 1] * ownf[b * BLK : (b + 1) * BLK, :]
            pack[j, s * BLK : (s + 1) * BLK, :] = total.astype(bf16)
        need_out[j] = mask
        send_kv(j).start()

    toward(me, 1, pack_and_send)

    cacc[...] = jnp.zeros_like(cacc)
    for load in late:
        load.wait()

    def no_rows(j):
        rows = pl.ds(pl.multiple_of(j * ctok, ctok), ctok)
        ckv[:, rows, :] = jnp.zeros((2, ctok, HD), bf16)

    up(no_rows)
    down(lambda j: comp_from(j).wait_recv())
    keep[1].wait()
    ckt[...] = ckv[0].T
    cvt[...] = ckv[1].T
    gate = gc_ref[...].T

    def compressed(block):
        tokens = slice(block * BLK, (block + 1) * BLK)
        start = (me * 4 + block) * BLK

        def before(t, s):
            row = lax.broadcasted_iota(jnp.int32, s.shape, 0) & (BLK - 1)
            key = lax.broadcasted_iota(jnp.int32, s.shape, 1) * STRIDE + t * (COLS * STRIDE)
            return jnp.where(key - row <= start, s, NEG)

        for r in range(HEADS_DEV * BLK // ROWS):
            parts = range(r * ROWS // BLK, (r + 1) * ROWS // BLK)
            q = jnp.concatenate([q_all[tokens, h * HD : (h + 1) * HD] for h in parts], axis=0)
            go = jnp.concatenate(
                [
                    (go_all[tokens, h * HD : (h + 1) * HD].astype(f32) * gate[tokens, h : h + 1]).astype(bf16)
                    for h in parts
                ],
                axis=0,
            )
            dqc_all[block, r * ROWS : (r + 1) * ROWS, :] = branch(
                q, go, q.T, go.T, ckt, cvt, ckv.at[0], before,
                s_ref, dp_ref, cacc.at[0], cacc.at[1],
            )

    def save(block):
        return pltpu.make_async_copy(dqc_all.at[block], dqc.at[block], dq_sem.at[block])

    def pass_on(i):
        kv_from(i).wait_recv()
        forward(i).start()

    for block in range(3):
        compressed(block)
        save(block).start()
    arrived(me, 1, pass_on)
    compressed(3)
    save(3).start()
    half = HD // 2
    for side in range(2):
        rows = slice(side * half, (side + 1) * half)
        joined = jnp.concatenate([cacc[0, rows, :] * SCALING, cacc[1, rows, :]], axis=0)
        dckv[side] = joined.T.astype(bf16)
    down(lambda i: forwarded(i).wait_recv())
    down(lambda i: send_need(i).wait_send())
    up(lambda j: send_kv(j).wait_send())
    down(lambda i: forward(i).wait_send())
    up(lambda j: send_comp(j).wait_send())
    keep[0].wait()
    for block in range(4):
        save(block).wait()


def reduce_kernel(
    n, dv, ds, dckv, need, queries, kv, dqc, where, source, total_out, ctotal_out, dq_out,
    ds_all, dks, mine, mcomp, xin, xown, xcomp, pack, recv, kmine, kgive, kin, kown_give, kown_in,
    kpack, krecv, acc, q_all, qt, kbuf, ksel, dqc_all,
    in_sem, ds_sem, xs, xr, ss, sr, ks, kr, ts, tr,
):
    me, tp, core = spots()
    partner = tp + 1 - 2 * core
    ctok = dckv.shape[1] // n
    half = HD // 2
    blocks, nkeys = ds.shape[0], ds.shape[2]
    per = nkeys // BLK
    own = pl.ds(2 * n, 4)

    def slots(i):
        return pl.ds(i * 2, 2)

    def comp_rows(i):
        return pl.ds(pl.multiple_of(i * ctok, ctok), ctok)

    loads = [
        pltpu.make_async_copy(queries, q_all, in_sem.at[0]),
        pltpu.make_async_copy(dckv.at[core], mcomp, in_sem.at[1]),
        pltpu.make_async_copy(dv.at[core], mine, in_sem.at[2]),
        pltpu.make_async_copy(kv.at[0], kbuf, in_sem.at[3]),
        pltpu.make_async_copy(dqc, dqc_all, in_sem.at[4]),
    ]
    ds_loads = [
        pltpu.make_async_copy(ds.at[b], ds_all.at[b], ds_sem.at[b]) for b in range(blocks)
    ]
    greet(n, me, tp, core)
    for load in loads[:1] + ds_loads[:1] + loads[1:3] + ds_loads[1:] + loads[3:]:
        load.start()
    all_here(n)

    def below(fn):
        def step(i, carry):
            fn(i)
            return carry

        lax.fori_loop(0, me, step, 0)

    swap_comp = remote(dckv.at[1 - core], xcomp, xs.at[n], xr.at[n], me, partner)
    swap_own = remote(dv.at[1 - core, own], xown, xs.at[n + 1], xr.at[n + 1], me, partner)
    swap_kown = remote(kown_give, kown_in, ts.at[n], tr.at[n], me, partner)

    def swap(i):
        return remote(dv.at[1 - core, slots(i)], xin.at[i], xs.at[i], xr.at[i], me, partner)

    def send(i):
        return remote(pack.at[i], recv.at[me], ss.at[i], sr.at[me], i, tp)

    def came(j):
        return remote(pack.at[j], recv.at[j], ss.at[j], sr.at[j], j, tp)

    def kswap(i):
        return remote(kgive.at[i], kin.at[i], ts.at[i], tr.at[i], me, partner)

    def ksend(i):
        return remote(kpack.at[i], krecv.at[me], ks.at[i], kr.at[me], i, tp)

    def kcame(j):
        return remote(kpack.at[j], krecv.at[j], ks.at[j], kr.at[j], j, tp)

    swap_comp.start()
    toward(me, -1, lambda i: swap(i).start())
    swap_own.start()
    for load in loads[:3]:
        load.wait()

    def add_and_send(i):
        swap(i).wait_recv()
        for s in range(2):
            pack[i, s * half : (s + 1) * half, :] = (
                mine[2 * i + s].astype(f32) + xin[i, s].astype(f32)
            ).astype(bf16)
        rows = comp_rows(i)
        pack[i, HD:, :] = (mcomp[rows, :].astype(f32) + xcomp[rows, :].astype(f32)).astype(bf16)
        send(i).start()

    for b in range(blocks):
        for h in range(HEADS_DEV):
            cols = slice(h * HD, (h + 1) * HD)
            qt[:, cols] = q_all[b * BLK : (b + 1) * BLK, cols].T
        ds_loads[b].wait()
        for t, cols in enumerate(column_chunks(nkeys)):
            dk = SCALING * lax.dot_general(qt[...], ds_all[b, :, cols], NN, preferred_element_type=f32)
            for c in range(COLS // BLK):
                dks[b * (per + 1) + t * (COLS // BLK) + c] = dk[:, c * BLK : (c + 1) * BLK]
        dks[b * (per + 1) + per] = jnp.zeros((HD, BLK), f32)
        if b == 0:
            swap_comp.wait_recv()
            toward(me, -1, add_and_send)
    first = core == 0

    def ours(x):
        return jnp.where(first, x[:half], x[half:])

    def theirs(x):
        return jnp.where(first, x[half:], x[:half])

    def slot_sum(i):
        for s in range(2):
            total = dks[source[0, 2 * i + s]]
            for b in range(1, blocks):
                total = total + dks[b * (per + 1) + source[b, 2 * i + s]]
            kmine[i, s * half : (s + 1) * half, :] = ours(total)
            kgive[i, s * half : (s + 1) * half, :] = theirs(total).astype(bf16)
        kswap(i).start()

    toward(me, -1, slot_sum)
    for b in range(blocks):
        kown_give[b] = theirs(dks[b * (per + 1)]).astype(bf16)
    swap_kown.start()

    def kadd_and_send(i):
        kswap(i).wait_recv()
        kpack[i] = (kmine[i] + kin[i].astype(f32)).astype(bf16)
        ksend(i).start()

    toward(me, -1, kadd_and_send)
    for load in loads[3:]:
        load.wait()
    for b in range(blocks):
        for j in range(per):
            ksel[j * BLK : (j + 1) * BLK, :] = kbuf[where[b, j]]
        dq = dqc_all[b]
        for cols in column_chunks(nkeys):
            dq = dq + lax.dot_general(
                ds_all[b, :, cols], ksel[cols, :], NN, preferred_element_type=f32
            )
        for h in range(HEADS_DEV):
            dq_out[b * BLK : (b + 1) * BLK, h * HD : (h + 1) * HD] = (
                dq[h * BLK : (h + 1) * BLK] * SCALING
            ).astype(bf16)
    swap_own.wait_recv()
    swap_kown.wait_recv()
    for b in range(blocks):
        acc[b, half:, :] = mine[2 * n + b].astype(f32) + xown[b].astype(f32)
        acc[b, :half, :] = ours(dks[b * (per + 1)]) + kown_in[b].astype(f32)
    rows = comp_rows(me)

    ctotal_out[...] = mcomp[rows, :].astype(f32) + xcomp[rows, :].astype(f32)

    def take(j):
        came(j).wait_recv()
        mask = need[j]
        part = recv[j].astype(f32)
        for b in range(4):
            acc[b, half:, :] += mask[b : b + 1] * part[:half] + mask[4 + b : 5 + b] * part[half:HD]
        ctotal_out[...] += part[HD:]

    arrived(me, -1, take)

    def ktake(j):
        kcame(j).wait_recv()
        mask = need[j]
        part = krecv[j].astype(f32)
        for b in range(4):
            acc[b, :half, :] += mask[b : b + 1] * part[:half] + mask[4 + b : 5 + b] * part[half:]

    arrived(me, -1, ktake)
    for b in range(4):
        total_out[:, b * BLK : (b + 1) * BLK] = acc[b].astype(bf16)
    below(lambda i: swap(i).wait_send())
    swap_comp.wait_send()
    swap_own.wait_send()
    swap_kown.wait_send()
    below(lambda i: send(i).wait_send())
    below(lambda i: kswap(i).wait_send())
    below(lambda i: ksend(i).wait_send())


def part_kernel(total, ctotal, dq, dq_out, dk_out, dv_out, dck_out, dcv_out):
    half = HD // 2
    dq_out[...] = dq[...]
    dk_out[...] = total[:half, :]
    dv_out[...] = total[half:, :]
    both = ctotal[...]
    dck_out[...] = both[:, :half].astype(bf16)
    dcv_out[...] = both[:, half:].astype(bf16)


def local(queries, keys, values, comp_keys, comp_values, gate_comp, gate_sel, grad_out, selections):
    n = lax.axis_size("ctx")
    ctok = comp_keys.shape[0]
    anywhere = pl.BlockSpec(memory_space=pl.ANY)
    scalars = pl.BlockSpec(memory_space=pltpu.SMEM)
    vmem = pl.BlockSpec(memory_space=pltpu.VMEM)
    dma = pltpu.SemaphoreType.DMA
    slot_rows = (2 * n + 4) * BLK
    width = HEADS_DEV * BLK
    kv, need, dqc, dckv = pl.pallas_call(
        functools.partial(gather_kernel, n),
        in_specs=[scalars] + [anywhere] * 6 + [vmem],
        out_specs=[anywhere, vmem, anywhere, vmem],
        out_shape=[
            jax.ShapeDtypeStruct((2, slot_rows, HD), bf16),
            jax.ShapeDtypeStruct((n, 8, HD), f32),
            jax.ShapeDtypeStruct((4, width, HD), f32),
            jax.ShapeDtypeStruct((2, n * ctok, HD), bf16),
        ],
        scratch_shapes=[
            pltpu.VMEM((2, 4 * BLK, HD), bf16),
            pltpu.VMEM((2, ctok, HD), bf16),
            pltpu.VMEM((4 * BLK, HD), f32),
            pltpu.VMEM((8 * n, HD), f32),
            pltpu.VMEM((n, 8, HD), f32),
            pltpu.VMEM((n, 2 * BLK, HD), bf16),
            pltpu.VMEM((2, n * ctok, HD), bf16),
            pltpu.VMEM(queries.shape, bf16),
            pltpu.VMEM(queries.shape, bf16),
            pltpu.VMEM((HD, n * ctok), bf16),
            pltpu.VMEM((HD, n * ctok), bf16),
            pltpu.VMEM((ROWS, n * ctok), f32),
            pltpu.VMEM((ROWS, n * ctok), f32),
            pltpu.VMEM((4, width, HD), f32),
            pltpu.VMEM((2, HD, n * ctok), f32),
            dma((6,)), dma((2,)), dma((4,)),
            dma((n,)), dma((n,)), dma((n,)), dma((n,)),
            dma((n,)), dma((n,)), dma((n,)), dma((n,)),
        ],
        compiler_params=pltpu.CompilerParams(
            collective_id=0, has_side_effects=True, vmem_limit_bytes=GRANT
        ),
        name="gather",
    )(
        selections, keys, values, comp_keys, comp_values, queries, grad_out,
        gate_comp.T,
    )
    kv = kv.reshape(2, 2 * n + 4, BLK, HD)
    dv_half, ds, where, source = attend(selections, queries, grad_out, gate_sel.T, kv)
    blocks, _, nkeys = ds.shape
    half = HD // 2
    total, ctotal, dq = pl.pallas_call(
        functools.partial(reduce_kernel, n),
        in_specs=[anywhere, anywhere, anywhere, vmem, anywhere, anywhere, anywhere, scalars, scalars],
        out_specs=[vmem] * 3,
        out_shape=[
            jax.ShapeDtypeStruct((HD, 4 * BLK), bf16),
            jax.ShapeDtypeStruct((ctok, HD), f32),
            jax.ShapeDtypeStruct(queries.shape, bf16),
        ],
        scratch_shapes=[
            pltpu.VMEM(ds.shape, bf16),
            pltpu.VMEM((blocks * (nkeys // BLK + 1), HD, BLK), f32),
            pltpu.VMEM((2 * n + 4, half, BLK), bf16),
            pltpu.VMEM((n * ctok, HD), bf16),
            pltpu.VMEM((n, 2, half, BLK), bf16),
            pltpu.VMEM((4, half, BLK), bf16),
            pltpu.VMEM((n * ctok, HD), bf16),
            pltpu.VMEM((n, HD + ctok, BLK), bf16),
            pltpu.VMEM((n, HD + ctok, BLK), bf16),
            pltpu.VMEM((n, HD, BLK), f32),
            pltpu.VMEM((n, HD, BLK), bf16),
            pltpu.VMEM((n, HD, BLK), bf16),
            pltpu.VMEM((4, half, BLK), bf16),
            pltpu.VMEM((4, half, BLK), bf16),
            pltpu.VMEM((n, HD, BLK), bf16),
            pltpu.VMEM((n, HD, BLK), bf16),
            pltpu.VMEM((4, HD, BLK), f32),
            pltpu.VMEM(queries.shape, bf16),
            pltpu.VMEM((HD, width), bf16),
            pltpu.VMEM((2 * n + 4, BLK, HD), bf16),
            pltpu.VMEM((nkeys, HD), bf16),
            pltpu.VMEM(dqc.shape, f32),
            dma((5,)), dma((blocks,)),
            dma((n + 2,)), dma((n + 2,)), dma((n,)), dma((n,)),
            dma((n,)), dma((n,)), dma((n + 1,)), dma((n + 1,)),
        ],
        compiler_params=pltpu.CompilerParams(
            collective_id=1, has_side_effects=True, vmem_limit_bytes=GRANT
        ),
        name="reduce",
    )(dv_half, ds, dckv, need, queries, kv, dqc, where, source)
    half = jax.ShapeDtypeStruct((HD // 2, 4 * BLK), bf16)
    chalf = jax.ShapeDtypeStruct((ctok, HD // 2), bf16)
    grad_queries, dk, dv, dck, dcv = pl.pallas_call(
        part_kernel,
        in_specs=[vmem] * 3,
        out_specs=[vmem] * 5,
        out_shape=[jax.ShapeDtypeStruct(queries.shape, bf16), half, half, chalf, chalf],
        name="part",
    )(total, ctotal, dq)
    return grad_queries, dk.T, dv.T, dck, dcv


def solution(mesh):
    placed = (
        P("ctx", "tp"),
        P("ctx", None),
        P("ctx", None),
        P("ctx", None),
        P("ctx", None),
        P("ctx", "tp"),
        P("ctx", "tp"),
        P("ctx", "tp"),
        P("ctx", None, None),
    )
    return jax.shard_map(
        local,
        mesh=mesh,
        in_specs=placed,
        out_specs=(P("ctx", "tp"), P("ctx", "tp"), P("ctx", "tp"), P("ctx", "tp"), P("ctx", "tp")),
        check_vma=False,
    )
```
